32 devices in a mesh: dp: 8 (over y, x, core), mp: 4 (over z).
Axes of the slice: x: 2, y: 2, z: 4, core: 2. Of those that a mesh axis runs over, the one named last changes fastest.
Arguments:
- tokens: bfloat16 [512, 32, 1024], P('mp', 'dp'), may hold values from -6 to 6
- timesteps: int32 [32], P('dp'), may hold values from 0 to 4999
- buckets: int32 [32], P('dp'), may hold values from 0 to 31
- counts: int32 [8], replicated, may hold values from 1 to 4, as said below
- w_time: bfloat16 [1024, 1024], replicated, may hold values from -0.1875 to 0.1875
- table: float32 [32, 1024], replicated, may hold values from -3 to 3
- w_qkv: bfloat16 [3, 1024, 1024], P(None, None, 'mp'), may hold values from -0.1875 to 0.1875
- b_qv: float32 [2, 1024], P(None, 'mp'), may hold values from -0.6 to 0.6
- w_out: bfloat16 [1024, 1024], P('mp'), may hold values from -0.5 to 0.5
- b_out: float32 [1024], replicated, may hold values from -2 to 2
- gain1: float32 [1024], replicated, may hold values from 0.5 to 1.5
- shift1: float32 [1024], replicated, may hold values from -1.2 to 1.2
- w_up: bfloat16 [1024, 4096], P(None, 'mp'), may hold values from -0.1875 to 0.1875
- b_up: float32 [4096], P('mp'), may hold values from -3 to 3
- w_down: bfloat16 [4096, 1024], P('mp'), may hold values from -0.09375 to 0.09375
- b_down: float32 [1024], replicated, may hold values from -2 to 2
- gain2: float32 [1024], replicated, may hold values from 0.5 to 1.5
- shift2: float32 [1024], replicated, may hold values from -1.2 to 1.2
- cotangent: bfloat16 [512, 32, 1024], P('mp', 'dp'), may hold values from -6 to 6
Outputs:
- output: bfloat16 [512, 32, 1024], P('mp', 'dp')
- grad_tokens: float32 [512, 32, 1024], P('mp', 'dp')
- grad_w_time: float32 [1024, 1024], P(None, ('dp', 'mp'))
- grad_table: float32 [32, 1024], P(None, ('dp', 'mp'))
- grad_w_qkv: float32 [3, 1024, 1024], P(None, 'dp', 'mp')
- grad_b_qv: float32 [2, 1024], P(None, ('dp', 'mp'))
- grad_w_out: float32 [1024, 1024], P('mp', 'dp')
- grad_b_out: float32 [1024], P(('dp', 'mp'))
- grad_gain1: float32 [1024], P(('dp', 'mp'))
- grad_shift1: float32 [1024], P(('dp', 'mp'))
- grad_w_up: float32 [1024, 4096], P('dp', 'mp')
- grad_b_up: float32 [4096], P(('dp', 'mp'))
- grad_w_down: float32 [4096, 1024], P('mp', 'dp')
- grad_b_down: float32 [1024], P(('dp', 'mp'))
- grad_gain2: float32 [1024], P(('dp', 'mp'))
- grad_shift2: float32 [1024], P(('dp', 'mp'))
The draws below stay inside these ranges and needn't reach their ends.
Inputs may be any that keep to these rules, and one draw needn't show every extreme that they name: Slot s of group g holds a live item iff s < counts[g]; in every draw some group has all 4 slots live.
All inputs are finite; a program needn't handle non-finite values.
Results may differ from the reference program's by a relative error of at most 0.025.
Values may be sent and summed in bfloat16 or wider, within the bound.
No kernel may reach another device: no remote copies, remote signals or barrier semaphores. Data moves between devices by JAX's collectives and lax.ppermute only.
A program may use at most 192 MiB of HBM per device.

```python
import math
import jax
import jax.numpy as jnp
from jax import lax

D = 1024
HEADS = 16
HD = 64
FF = 4096
LEN = 512
NB = 32
TSTEPS = 5000
SLOTS = 4
ITEMS = 32
N_DP = 8
N_MP = 4


def draw_counts(key, part):
    first_key, second_key = jax.random.split(jax.random.fold_in(key, 17))
    drawn = jax.random.randint(first_key, (N_DP,), 1, SLOTS + 1)
    full_group = jax.random.randint(second_key, (), 0, N_DP)
    return jnp.where(jnp.arange(N_DP) == full_group, SLOTS, drawn).astype(jnp.int32)


def plant(array, key, least, high):
    extent = array.shape
    spot = [jax.random.randint(jax.random.fold_in(key, axis), (), 0, extent[axis]) for axis in range(len(extent))]
    array = array.at[tuple(spot)].set(least)
    longest = extent.index(max(extent))
    spot[longest] = (spot[longest] + 1) % extent[longest]
    return array.at[tuple(spot)].set(high)


def shard_levels(key, dims, pieces, least, largest):
    level = 1.0
    for axis_at, shards_of in pieces:
        draws = jax.random.uniform(jax.random.fold_in(jax.random.fold_in(key, 6), axis_at), (shards_of,), jnp.float32, least / len(pieces), largest / len(pieces))
        level = level * jnp.repeat(jnp.exp(draws), dims[axis_at] // shards_of).reshape((-1,) + (1,) * (len(dims) - 1 - axis_at))
    return level


def bell_draw(own_key, shape, width, bound, shards=(), kind=jnp.bfloat16):
    values = width * jax.random.normal(own_key, shape, jnp.float32)
    if shards:
        values = values * shard_levels(own_key, shape, shards, -0.22, 0.18)
    return jnp.clip(values, -bound, bound).astype(kind)


def setup_inputs(seed: int = 0) -> dict:
    key_of = jax.random.split(jax.random.key(seed), 20)
    return {
        "tokens": bell_draw(key_of[0], (LEN, ITEMS, D), 1.0, 6.0, ((0, 4), (1, 8))),
        "timesteps": plant(jax.random.randint(key_of[1], (ITEMS,), 0, TSTEPS), jax.random.fold_in(key_of[1], 1), 0, TSTEPS - 1).astype(jnp.int32),
        "buckets": plant(jax.random.randint(key_of[2], (ITEMS,), 0, NB), jax.random.fold_in(key_of[2], 1), 0, NB - 1).astype(jnp.int32),
        "counts": draw_counts(jax.random.fold_in(key_of[19], 71), 0),
        "w_time": bell_draw(key_of[4], (D, D), D ** -0.5, 0.1875),
        "table": bell_draw(key_of[5], (NB, D), 0.5, 3.0, (), jnp.float32),
        "w_qkv": bell_draw(key_of[6], (3, D, D), D ** -0.5, 0.1875, ((2, 4),)),
        "b_qv": bell_draw(key_of[7], (2, D), 0.1, 0.6, ((1, 4),), jnp.float32),
        "w_out": bell_draw(key_of[8], (D, D), (D // 8) ** -0.5, 0.5, ((0, 4),)),
        "b_out": bell_draw(key_of[9], (D,), 0.3, 2.0, (), jnp.float32),
        "gain1": jnp.clip(1.0 + 0.1 * jax.random.normal(key_of[10], (D,), jnp.float32), 0.5, 1.5),
        "shift1": bell_draw(key_of[11], (D,), 0.2, 1.2, (), jnp.float32),
        "w_up": bell_draw(key_of[12], (D, FF), D ** -0.5, 0.1875, ((1, 4),)),
        "b_up": bell_draw(key_of[13], (FF,), 0.5, 3.0, ((0, 4),), jnp.float32),
        "w_down": bell_draw(key_of[14], (FF, D), FF ** -0.5, 0.09375, ((0, 4),)),
        "b_down": bell_draw(key_of[15], (D,), 0.3, 2.0, (), jnp.float32),
        "gain2": jnp.clip(1.0 + 0.1 * jax.random.normal(key_of[16], (D,), jnp.float32), 0.5, 1.5),
        "shift2": bell_draw(key_of[17], (D,), 0.2, 1.2, (), jnp.float32),
        "cotangent": bell_draw(key_of[18], (LEN, ITEMS, D), 1.0, 6.0, ((0, 4), (1, 8))),
    }


@jax.custom_vjp
def low(v):
    return lax.optimization_barrier(v.astype(jnp.bfloat16)).astype(jnp.float32)

@jax.custom_vjp
def low_back(v):
    return v

def low_keep(v):
    return (low(v), None)

def low_pass(kept, grad):
    return (grad,)

def back_keep(v):
    return (v, None)

def back_low(kept, grad):
    return (low(grad),)
low.defvjp(low_keep, low_pass)
low_back.defvjp(back_keep, back_low)

def product(form, left, right):
    return jnp.einsum(form, left, right, precision=lax.Precision.HIGHEST)

def layer_norm(values, gain, shift):
    center = values - lax.optimization_barrier(jnp.mean(values, axis=-1, keepdims=True))
    spread = lax.optimization_barrier(jnp.mean(center * center, axis=-1, keepdims=True))
    return center * lax.rsqrt(spread + 1e-05) * gain + shift

def exact_gelu(values):
    return jax.nn.gelu(values, approximate=False)

def sinusoid(steps, model_width):
    half_width = model_width // 2
    freqs = jnp.exp(-math.log(10000.0) * jnp.arange(half_width, dtype=jnp.float32) / half_width)
    angles = steps.astype(jnp.float32)[:, None] * freqs[None, :]
    return jnp.concatenate([jnp.sin(angles), jnp.cos(angles)], axis=-1)

def layer_pass(params, token_rows, sinus_rows, bucket_rows):
    w_time, table, w_qkv, b_qv, w_out, b_out, gain1, shift1, w_up, b_up, w_down, b_down, gain2, shift2 = params
    head_cols = D // N_MP
    unit_cols = FF // N_MP
    time_embed = product('nd,de->ne', low(sinus_rows), w_time) + jnp.take(table, bucket_rows, axis=0)
    start_rows = token_rows + time_embed[None]
    hidden = low(start_rows)
    projected = jnp.concatenate([product('lnd,cde->clne', low_back(hidden), w_qkv[:, :, block * head_cols:(block + 1) * head_cols]) for block in range(N_MP)], axis=-1)
    zero_bias = jnp.zeros_like(b_qv[0])
    projected = projected + jnp.stack([b_qv[0], zero_bias, b_qv[1]])[:, None, None, :]
    projected = low(low_back(projected))
    length = token_rows.shape[0]
    item_count = token_rows.shape[1]
    split_heads = projected.reshape(3, length, item_count, HEADS, HD)
    scores = low_back(product('qnhe,knhe->nhqk', split_heads[0], split_heads[1]) * 0.125)
    attend = jax.nn.softmax(scores, axis=-1)
    context = product('nhqk,knhe->qnhe', low(attend), split_heads[2]).reshape(length, item_count, D)
    context = low(low_back(context))
    mixing = jnp.zeros_like(start_rows) + b_out
    for block in range(N_MP):
        mixing = mixing + low(product('lnh,hd->lnd', context[:, :, block * head_cols:(block + 1) * head_cols], w_out[block * head_cols:(block + 1) * head_cols]))
    mixing = low_back(mixing)
    normed = layer_norm(start_rows + mixing, gain1, shift1)
    normed_low = low(normed)
    upward = jnp.concatenate([product('lnd,df->lnf', low_back(normed_low), w_up[:, block * unit_cols:(block + 1) * unit_cols]) for block in range(N_MP)], axis=-1) + b_up
    upward = low_back(upward)
    active = low(exact_gelu(upward))
    branch = jnp.zeros_like(start_rows) + b_down
    for block in range(N_MP):
        branch = branch + low(product('lnf,fd->lnd', active[:, :, block * unit_cols:(block + 1) * unit_cols], w_down[block * unit_cols:(block + 1) * unit_cols]))
    branch = low_back(branch)
    return layer_norm(normed + branch, gain2, shift2)

def reference(tokens, timesteps, buckets, counts, w_time, table, w_qkv, b_qv, w_out, b_out, gain1, shift1, w_up, b_up, w_down, b_down, gain2, shift2, cotangent):
    params = tuple((weight.astype(jnp.float32) for weight in (w_time, table, w_qkv, b_qv, w_out, b_out, gain1, shift1, w_up, b_up, w_down, b_down, gain2, shift2)))
    live_mask = (jnp.arange(SLOTS)[None, :] < counts[:, None]).astype(jnp.float32)
    token_groups = tokens.astype(jnp.float32).reshape(LEN, N_DP, SLOTS, D).transpose(1, 0, 2, 3)
    grad_groups = cotangent.astype(jnp.float32).reshape(LEN, N_DP, SLOTS, D).transpose(1, 0, 2, 3)
    grad_groups = grad_groups * live_mask[:, None, :, None]
    sinus_groups = sinusoid(timesteps, D).reshape(N_DP, SLOTS, D)
    bucket_groups = buckets.reshape(N_DP, SLOTS)

    def group_step(totals, inputs):
        token_rows, sinus_rows, bucket_rows, grad_rows = inputs

        def forward_only(weights, rows):
            return layer_pass(weights, rows, sinus_rows, bucket_rows)
        result, pull = jax.vjp(forward_only, params, token_rows)
        weight_grads, row_grads = pull(grad_rows)
        return (jax.tree.map(jnp.add, totals, weight_grads), (result, row_grads))
    start_totals = jax.tree.map(jnp.zeros_like, params)
    totals, (results, row_grads) = lax.scan(group_step, start_totals, (token_groups, sinus_groups, bucket_groups, grad_groups))
    total_live = jnp.sum(counts).astype(jnp.float32)
    weight_grads = tuple((grad / total_live for grad in totals))
    output = results.transpose(1, 0, 2, 3).reshape(LEN, ITEMS, D).astype(jnp.bfloat16)
    grad_tokens = row_grads.transpose(1, 0, 2, 3).reshape(LEN, ITEMS, D)
    return (output, grad_tokens, weight_grads[0], weight_grads[1], weight_grads[2], weight_grads[3], weight_grads[4], weight_grads[5], weight_grads[6], weight_grads[7], weight_grads[8], weight_grads[9], weight_grads[10], weight_grads[11], weight_grads[12], weight_grads[13])
```

```python
import functools
import math

import jax
import jax.numpy as jnp
from jax import lax
from jax.experimental import pallas as pl
from jax.experimental.pallas import tpu as pltpu
from jax.sharding import PartitionSpec as P

HD = 64
f32 = jnp.float32
bf16 = jnp.bfloat16
VMEM_LIMIT = 56 * 2**20
PATHS = ((2, 4), (4, 2))


def params(**more):
    return pltpu.CompilerParams(vmem_limit_bytes=VMEM_LIMIT, **more)


def dot(a, b, dims):
    return lax.dot_general(a, b, (dims, ((), ())), preferred_element_type=f32)


def sinusoid(steps, model_width):
    half_width = model_width // 2
    freqs = jnp.exp(-math.log(10000.0) * jnp.arange(half_width, dtype=f32) / half_width)
    angles = steps[:, None] * freqs[None, :]
    return jnp.concatenate([jnp.sin(angles), jnp.cos(angles)], axis=-1).astype(bf16)


def assemble_body(plan, n_out, place_ref, *refs):
    pieces = refs[: len(plan)]
    outs = refs[len(plan) : len(plan) + n_out]
    sems = refs[-1]
    here = place_ref[0]
    copies = []
    for piece, (path, masks, spans) in zip(pieces, plan):
        for i, mask in enumerate(masks):
            for out, (axes, start, size) in zip(outs, spans):
                lead = (slice(None),) * axes
                src = piece.at[i].at[lead + (pl.ds(start, size),)]
                dst = out.at[lead + (here ^ mask, path)]
                copies.append(pltpu.make_async_copy(src, dst, sems.at[len(copies)]))
    for copy in copies:
        copy.start()
    for copy in copies:
        copy.wait()


def assemble(place, pieces, plan, shapes):
    n_copies = sum(len(masks) * len(spans) for _, masks, spans in plan)
    hbm = pl.BlockSpec(memory_space=pl.ANY)
    return pl.pallas_call(
        functools.partial(assemble_body, plan, len(shapes)),
        out_shape=[jax.ShapeDtypeStruct(s, bf16) for s in shapes],
        in_specs=[pl.BlockSpec(memory_space=pltpu.SMEM)] + [hbm] * len(pieces),
        out_specs=[hbm] * len(shapes),
        scratch_shapes=[pltpu.SemaphoreType.DMA((n_copies,))],
        compiler_params=params(),
        name="assemble",
    )(place, *pieces)


def attend_body(q_ref, k_ref, v_ref, p_ref, c_ref):
    q, k, v = q_ref[...], k_ref[...], v_ref[...]
    lane = lax.broadcasted_iota(jnp.int32, q.shape, 1)
    joined = None
    for hh in range(2):
        mine = (lane // HD) == hh
        kh = jnp.where(mine, k, jnp.zeros_like(k))
        st = dot(kh, q, ((1,), (1,))) * 0.125
        top = jnp.max(st, axis=0, keepdims=True)
        e = jnp.exp(st - top)
        p = (e * (1.0 / jnp.sum(e, axis=0, keepdims=True))).astype(bf16)
        p_ref[hh] = p
        c = dot(p, v, ((0,), (0,)))
        joined = c if joined is None else jnp.where(mine, c, joined)
    c_ref[...] = joined.astype(bf16)


def attend(q, k, v):
    length, cols = q.shape
    pairs = cols // (2 * HD)
    block = pl.BlockSpec((length, 2 * HD), lambda i: (0, i))
    return pl.pallas_call(
        attend_body,
        grid=(pairs,),
        out_shape=[
            jax.ShapeDtypeStruct((2 * pairs, length, length), bf16),
            jax.ShapeDtypeStruct((length, cols), bf16),
        ],
        in_specs=[block] * 3,
        out_specs=[pl.BlockSpec((2, length, length), lambda i: (i, 0, 0)), block],
        compiler_params=params(),
        name="attend",
    )(q, k, v)


def attend_back_body(q_ref, k_ref, v_ref, p_ref, g_ref, dq_ref, dk_ref, dv_ref):
    q, k, v, g = q_ref[...], k_ref[...], v_ref[...], g_ref[...]
    lane = lax.broadcasted_iota(jnp.int32, q.shape, 1)
    dq = dk = dv = None
    for hh in range(2):
        mine = (lane // HD) == hh
        zero = jnp.zeros_like(q)
        gh = jnp.where(mine, g, zero)
        kh = jnp.where(mine, k, zero)
        qh = jnp.where(mine, q, zero)
        p = p_ref[hh]
        dpt = dot(v, gh, ((1,), (1,)))
        pf = p.astype(f32)
        row = jnp.sum(pf * dpt, axis=0, keepdims=True)
        ds = (pf * (dpt - row)).astype(bf16)
        a = dot(p, gh, ((1,), (0,)))
        b = dot(ds, qh, ((1,), (0,)))
        c = dot(ds, kh, ((0,), (0,)))
        dv = a if dv is None else dv + a
        dk = b if dk is None else dk + b
        dq = c if dq is None else dq + c
    dq_ref[...] = (dq * 0.125).astype(bf16)
    dk_ref[...] = (dk * 0.125).astype(bf16)
    dv_ref[...] = dv.astype(bf16)


def attend_back(q, k, v, p, g):
    length, cols = q.shape
    pairs = cols // (2 * HD)
    block = pl.BlockSpec((length, 2 * HD), lambda i: (0, i))
    return pl.pallas_call(
        attend_back_body,
        grid=(pairs,),
        out_shape=[jax.ShapeDtypeStruct((length, cols), bf16)] * 3,
        in_specs=[block] * 3 + [pl.BlockSpec((2, length, length), lambda i: (i, 0, 0)), block],
        out_specs=[block] * 3,
        compiler_params=params(),
        name="attend_back",
    )(q, k, v, p, g)


def weight_grad_body(on_rows, order, width, a_ref, a2_ref, b_ref, b2_ref, keep_ref, send_ref):
    g = dot(a_ref[...], b_ref[...], ((0,), (0,))) + dot(a2_ref[...], b2_ref[...], ((0,), (0,)))
    g = g.astype(bf16)
    for out, picks in ((keep_ref, order[:2]), (send_ref, order[2:])):
        for i, j in enumerate(picks):
            span = slice(j * width, (j + 1) * width)
            out[i] = g[span] if on_rows else g[:, span]


def weight_grad(on_rows, path, width, a, a2, b, b2):
    order = (0, 2, 1, 3) if path == 0 else (0, 1, 2, 3)
    rows, cols = a.shape[1], b.shape[1]
    tile = (width, cols) if on_rows else (rows, width)
    full = pl.BlockSpec(memory_space=pltpu.VMEM)
    out = jax.ShapeDtypeStruct((2,) + tile, bf16)
    return pl.pallas_call(
        functools.partial(weight_grad_body, on_rows, order, width),
        out_shape=[out, out],
        in_specs=[full] * 4,
        out_specs=[full] * 2,
        compiler_params=params(),
        name="weight_grad",
    )(a, a2, b, b2)


def norm_stats(values):
    center = values - jnp.mean(values, axis=-1, keepdims=True)
    inv = lax.rsqrt(jnp.mean(center * center, axis=-1, keepdims=True) + 1e-05)
    return center * inv, inv


def norm_back(grad, n, inv, gain):
    gn = grad * gain
    return (gn - jnp.mean(gn, -1, keepdims=True) - n * jnp.mean(gn * n, -1, keepdims=True)) * inv


def on_device(
    tokens,
    timesteps,
    buckets,
    counts,
    w_time,
    table,
    w_qkv,
    b_qv,
    w_out,
    b_out,
    gain1,
    shift1,
    w_up,
    b_up,
    w_down,
    b_down,
    gain2,
    shift2,
    cotangent,
):
    mpn = lax.axis_size("mp")
    dpn = lax.axis_size("dp")
    extra = dpn.bit_length() - 4
    me = lax.axis_index("dp")
    z = lax.axis_index("mp")
    q8 = me >> extra
    width = w_time.shape[0]
    positions, slots = tokens.shape[:2]
    length = positions * mpn
    head_cols = w_qkv.shape[2]
    units = w_up.shape[1]
    chunk = width // 8

    def flip(x, mask):
        step = mask << extra
        return lax.ppermute(x, "dp", [(i, i ^ step) for i in range(dpn)])

    def shift(x, s):
        return lax.ppermute(x, "mp", [(i, (i + s) % mpn) for i in range(mpn)])

    def to_items(x):
        x = lax.all_to_all(jnp.moveaxis(x, 1, 0), "mp", 0, 0, tiled=False)
        return x.reshape(length, width)

    def to_positions(x):
        x = lax.all_to_all(x.reshape(mpn, positions, width), "mp", 0, 0, tiled=False)
        return jnp.moveaxis(x, 0, 1)

    def spread(part):
        arrived = [shift(part, s) for s in range(1, mpn)]
        pieces, plan = [], []
        for path, (first, second) in enumerate(PATHS):
            mine = jnp.stack([a[path] for a in arrived])
            held = jnp.stack([mine, flip(mine, first)])
            far = flip(held, second)
            near = (0, first)
            beyond = (second, first | second)
            pieces += [held, far, flip(held, 1), flip(far, 1)]
            plan += [(path, m) for m in (near, beyond)]
            plan += [(path, tuple(v ^ 1 for v in m)) for m in (near, beyond)]
        return pieces, plan

    def eighth(shard, axis):
        dims = shard.shape
        rows = dims[axis] // 16
        shaped = shard.reshape(dims[:axis] + (8, 2, rows) + dims[axis + 1 :])
        return jnp.moveaxis(lax.dynamic_index_in_dim(shaped, q8, axis, False), axis, 0)

    place = q8.astype(jnp.int32)[None]
    n_far = mpn - 1

    pieces, plan = spread(eighth(w_qkv, 1))
    rows = chunk // 2
    (far_qkv,) = assemble(
        place,
        pieces,
        [(p, m, ((2, 0, rows),)) for p, m in plan],
        [(n_far, 3, 8, 2, rows, head_cols)],
    )
    far_qkv = far_qkv.reshape(n_far, 3, width, head_cols)
    wq = [w_qkv] + [far_qkv[s] for s in range(n_far)]

    out_rows, up_rows, down_rows = head_cols // 16, width // 16, units // 16
    pieces, plan = spread(jnp.concatenate([eighth(w_out, 0), eighth(w_up, 0)], axis=1))
    far_out, far_up = assemble(
        place,
        pieces,
        [(p, m, ((1, 0, out_rows), (1, out_rows, up_rows))) for p, m in plan],
        [(n_far, 8, 2, out_rows, width), (n_far, 8, 2, up_rows, units)],
    )
    far_out = far_out.reshape(n_far, head_cols, width)
    far_up = far_up.reshape(n_far, width, units)
    wo = [w_out] + [far_out[s] for s in range(n_far)]
    wu = [w_up] + [far_up[s] for s in range(n_far)]

    pieces, plan = spread(eighth(w_down, 0))
    (far_down,) = assemble(
        place,
        pieces,
        [(p, m, ((1, 0, down_rows),)) for p, m in plan],
        [(n_far, 8, 2, down_rows, width)],
    )
    far_down = far_down.reshape(n_far, units, width)
    wd = [w_down] + [far_down[s] for s in range(n_far)]

    biases = jnp.concatenate([b_up, b_qv[0], b_qv[1]])
    biases = [biases] + [shift(biases, s) for s in range(1, mpn)]

    total_live = jnp.sum(counts).astype(f32)
    weighting = 1.0 / total_live
    live = (z < lax.dynamic_index_in_dim(counts, me, 0, False)).astype(f32)
    my_step = lax.dynamic_index_in_dim(timesteps, z, 0, True)
    my_bucket = lax.dynamic_index_in_dim(buckets, z, 0, False)
    time_embed = jnp.dot(
        sinusoid(my_step.astype(f32), width), w_time, preferred_element_type=f32
    ) + lax.dynamic_index_in_dim(table, my_bucket, 0, True)

    start = to_items(tokens).astype(f32) + time_embed
    hidden = start.astype(bf16)

    qkv, probs, ctx = [], [], []
    for s in range(mpn):
        pq = dot(hidden, wq[s][0], ((1,), (0,))) + biases[s][units : units + head_cols]
        pk = dot(hidden, wq[s][1], ((1,), (0,)))
        pv = dot(hidden, wq[s][2], ((1,), (0,))) + biases[s][units + head_cols :]
        qkv.append((pq.astype(bf16), pk.astype(bf16), pv.astype(bf16)))
        p, c = attend(*qkv[s])
        probs.append(p)
        ctx.append(c)
    mixing = b_out + sum(dot(ctx[s], wo[s], ((1,), (0,))) for s in range(mpn))
    n1, inv1 = norm_stats(start + mixing)
    normed = n1 * gain1 + shift1
    normed_low = normed.astype(bf16)
    active, slope = [], []
    for s in range(mpn):
        u = dot(normed_low, wu[s], ((1,), (0,))) + biases[s][:units]
        phi = 0.5 + 0.5 * lax.erf(u * (2.0**-0.5))
        active.append((u * phi).astype(bf16))
        slope.append((phi + u * jnp.exp(-0.5 * u * u) * (2.0 * math.pi) ** -0.5).astype(bf16))
    branch = b_down + sum(dot(active[s], wd[s], ((1,), (0,))) for s in range(mpn))
    n2, inv2 = norm_stats(normed + branch)
    output = to_positions((n2 * gain2 + shift2).astype(bf16))

    grad_result = to_items(cotangent).astype(f32) * live
    grad_gain2 = jnp.sum(grad_result * n2, axis=0)
    grad_shift2 = jnp.sum(grad_result, axis=0)
    grad_second = norm_back(grad_result, n2, inv2, gain2)
    branch_grad = grad_second.astype(bf16)
    grad_b_down = jnp.sum(branch_grad.astype(f32), axis=0)

    def pick(x, flipped):
        spans = [
            lax.dynamic_slice_in_dim(x, (q8 ^ (j * 2) ^ flipped) * chunk, chunk, 1)
            for j in range(4)
        ]
        return jnp.concatenate(spans, axis=1)

    def pair_pick(x):
        return pick(x, 0), flip(pick(x, 1), 1)

    def reduced(on_rows, mine, theirs, picked, picked2):
        total = None
        for path, (first, second) in enumerate(PATHS):
            for s in range(path * mpn // 2, (path + 1) * mpn // 2):
                if on_rows:
                    pair = weight_grad(True, path, chunk, picked, picked2, mine[s], theirs[s])
                else:
                    pair = weight_grad(False, path, chunk, mine[s], theirs[s], picked, picked2)
                keep, sent = pair
                came = flip(sent, first)
                second_part = (keep[1].astype(f32) + came[1].astype(f32)).astype(bf16)
                part = keep[0].astype(f32) + came[0].astype(f32) + flip(second_part, second).astype(f32)
                if s:
                    part = shift(part.astype(bf16), -s).astype(f32)
                total = part if total is None else total + part
        axis = 0 if on_rows else 1
        for t in reversed(range(extra)):
            half = total.shape[axis] // 2
            bit = (me >> t) & 1
            keep = lax.dynamic_slice_in_dim(total, bit * half, half, axis)
            sent = lax.dynamic_slice_in_dim(total, (1 - bit) * half, half, axis)
            total = keep + lax.ppermute(sent, "dp", [(i, i ^ (1 << t)) for i in range(dpn)])
        return total * weighting

    active2 = [flip(a, 1) for a in active]
    grad_w_down = reduced(False, active, active2, *pair_pick(branch_grad))

    up_grad = [
        (dot(branch_grad, wd[s], ((1,), (1,))) * slope[s].astype(f32)).astype(bf16)
        for s in range(mpn)
    ]
    grad_b_up = [jnp.sum(g.astype(f32), axis=0) for g in up_grad]
    up_grad2 = [flip(g, 1) for g in up_grad]
    grad_w_up = reduced(True, up_grad, up_grad2, *pair_pick(normed_low))
    grad_normed = grad_second + sum(dot(up_grad[s], wu[s], ((1,), (1,))) for s in range(mpn))
    grad_gain1 = jnp.sum(grad_normed * n1, axis=0)
    grad_shift1 = jnp.sum(grad_normed, axis=0)
    grad_first = norm_back(grad_normed, n1, inv1, gain1)
    mixing_grad = grad_first.astype(bf16)
    grad_b_out = jnp.sum(mixing_grad.astype(f32), axis=0)
    ctx2 = [flip(c, 1) for c in ctx]
    grad_w_out = reduced(False, ctx, ctx2, *pair_pick(mixing_grad))
    proj_grad, grad_b_q, grad_b_v = [], [], []
    grad_tokens = grad_first
    for s in range(mpn):
        cg = dot(mixing_grad, wo[s], ((1,), (1,))).astype(bf16)
        dq, dk, dv = attend_back(*qkv[s], probs[s], cg)
        grad_b_q.append(jnp.sum(dq.astype(f32), axis=0))
        grad_b_v.append(jnp.sum(dv.astype(f32), axis=0))
        proj_grad.append(jnp.concatenate([dq, dk, dv], axis=1))
        for c, g in enumerate((dq, dk, dv)):
            grad_tokens = grad_tokens + dot(g, wq[s][c], ((1,), (1,)))
    proj_grad2 = [flip(g, 1) for g in proj_grad]
    grad_w_qkv = reduced(True, proj_grad, proj_grad2, *pair_pick(hidden))
    grad_w_qkv = jnp.moveaxis(grad_w_qkv.reshape(grad_w_qkv.shape[0], 3, head_cols), 1, 0)
    time_grad = jnp.sum(grad_tokens, axis=0)
    grad_tokens = to_positions(grad_tokens.astype(bf16)).astype(f32)

    devices = dpn * mpn

    def in_order(parts):
        turned = jnp.stack([parts[-i % mpn] for i in range(mpn)] * 2)
        return lax.dynamic_slice_in_dim(turned, (mpn - z) % mpn, mpn, 0).reshape(-1)

    vectors = [
        in_order(grad_b_q),
        in_order(grad_b_v),
        grad_b_out,
        grad_gain1,
        grad_shift1,
        grad_b_down,
        grad_gain2,
        grad_shift2,
        in_order(grad_b_up),
    ]
    spread_out = jnp.concatenate([v.reshape(devices, -1) for v in vectors], axis=1)
    facts = jnp.stack([my_step[0].astype(f32), my_bucket.astype(f32)])
    facts = jnp.broadcast_to(facts[None], (devices, 2))
    both = ("dp", "mp")
    gathered = lax.all_to_all(jnp.concatenate([spread_out, facts], axis=1), both, 0, 0, tiled=True)
    summed = jnp.sum(gathered[:, :-2], axis=0) * weighting
    steps, rows_of = gathered[:, -2], gathered[:, -1]
    per = width // devices
    small = [summed[i * per : (i + 1) * per] for i in range(8)]
    grad_b_up = summed[8 * per :]
    grads = lax.all_to_all(time_grad.reshape(devices, per), both, 0, 0, tiled=True)
    high = lax.Precision.HIGHEST
    grad_w_time = (
        jnp.einsum("nd,ne->de", sinusoid(steps, width).astype(f32), grads, precision=high)
        * weighting
    )
    onehot = (rows_of[:, None] == jnp.arange(table.shape[0], dtype=f32)[None, :]).astype(f32)
    grad_table = jnp.einsum("nb,nd->bd", onehot, grads, precision=high) * weighting
    return (
        output,
        grad_tokens,
        grad_w_time,
        grad_table,
        grad_w_qkv,
        jnp.stack(small[:2]),
        grad_w_out,
        small[2],
        small[3],
        small[4],
        grad_w_up,
        grad_b_up,
        grad_w_down,
        small[5],
        small[6],
        small[7],
    )


def solution(mesh):
    return jax.shard_map(
        on_device,
        mesh=mesh,
        in_specs=(
            P("mp", "dp", None),
            P("dp"),
            P("dp"),
            P(),
            P(),
            P(),
            P(None, None, "mp"),
            P(None, "mp"),
            P("mp", None),
            P(),
            P(),
            P(),
            P(None, "mp"),
            P("mp"),
            P("mp", None),
            P(),
            P(),
            P(),
            P("mp", "dp", None),
        ),
        out_specs=(
            P("mp", "dp", None),
            P("mp", "dp", None),
            P(None, ("dp", "mp")),
            P(None, ("dp", "mp")),
            P(None, "dp", "mp"),
            P(None, ("dp", "mp")),
            P("mp", "dp"),
            P(("dp", "mp")),
            P(("dp", "mp")),
            P(("dp", "mp")),
            P("dp", "mp"),
            P(("dp", "mp")),
            P("mp", "dp"),
            P(("dp", "mp")),
            P(("dp", "mp")),
            P(("dp", "mp")),
        ),
        check_vma=False,
    )
```

```python
import functools
import math

import jax
import jax.numpy as jnp
from jax import lax
from jax.experimental import pallas as pl
from jax.experimental.pallas import tpu as pltpu
from jax.sharding import PartitionSpec as P

HD = 64
f32 = jnp.float32
bf16 = jnp.bfloat16
VMEM_LIMIT = 56 * 2**20
PATHS = ((2, 4), (4, 2))


def params(**more):
    return pltpu.CompilerParams(vmem_limit_bytes=VMEM_LIMIT, **more)


def dot(a, b, dims):
    return lax.dot_general(a, b, (dims, ((), ())), preferred_element_type=f32)


def sinusoid(steps, model_width):
    half_width = model_width // 2
    freqs = jnp.exp(-math.log(10000.0) * jnp.arange(half_width, dtype=f32) / half_width)
    angles = steps[:, None] * freqs[None, :]
    return jnp.concatenate([jnp.sin(angles), jnp.cos(angles)], axis=-1).astype(bf16)


class Gathered:
    def __init__(self, own, pieces, plan, lead, start):
        self.arrays = [own] + pieces
        self.plan = plan
        self.lead = len(lead)
        self.start = start
        self.dims = own.shape
        self.copies = 1 + sum(len(masks) for _, masks in plan)

    def scratch(self, shards):
        return [
            pltpu.VMEM((shards,) + self.dims, bf16),
            pltpu.SemaphoreType.DMA((shards, self.copies)),
        ]

    def _copies(self, refs, place, into, sems, shard):
        lead = (slice(None),) * self.lead
        made = []
        for ref, (path, masks) in zip(refs[1:], self.plan):
            for i, mask in enumerate(masks):
                at = lead + (pl.ds(self.start, self.dims[-2]),)
                made.append(
                    pltpu.make_async_copy(
                        ref.at[i, shard - 1].at[at],
                        into.at[(shard,) + lead + (place ^ mask, path)],
                        sems.at[shard, len(made)],
                    )
                )
        return made

    def start_all(self, refs, place, into, sems, shards):
        pltpu.make_async_copy(refs[0], into.at[0], sems.at[0, 0]).start()
        for shard in range(1, shards):
            for copy in self._copies(refs, place, into, sems, shard):
                copy.start()

    def wait(self, refs, place, into, sems, shard):
        @pl.when(shard == 0)
        def _():
            pltpu.make_async_copy(refs[0], into.at[0], sems.at[0, 0]).wait()

        @pl.when(shard > 0)
        def _():
            for copy in self._copies(refs, place, into, sems, shard):
                copy.wait()


HBM = pl.BlockSpec(memory_space=pl.ANY)
SMEM = pl.BlockSpec(memory_space=pltpu.SMEM)


def whole(shape):
    return pl.BlockSpec(shape, lambda *_: (0,) * len(shape))


def cost(flops, transcendentals, moved):
    return pl.CostEstimate(flops=flops, transcendentals=transcendentals, bytes_accessed=moved)


def attend_body(
    first, shards, gathered, place_ref, x_ref, bias_ref, *refs
):
    n = len(gathered.arrays)
    w_refs, (qkv_ref, p_ref, c_ref, w, sems) = refs[:n], refs[n:]
    s, pair = pl.program_id(0), pl.program_id(1)
    place = place_ref[0]
    cols = w.shape[-1]

    @pl.when((s == 0) & (pair == 0))
    def _():
        if first == 0:
            gathered.start_all(w_refs, place, w, sems, shards)
        else:
            for shard in range(1, shards + 1):
                for copy in gathered._copies(w_refs, place, w, sems, shard):
                    copy.start()

    @pl.when(pair == 0)
    def _():
        shard = s + first
        gathered.wait(w_refs, place, w, sems, shard)
        for c in range(3):
            wide = w[shard, c].reshape(x_ref.shape[1], cols)
            out = dot(x_ref[...], wide, ((1,), (0,))) + bias_ref[0, c]
            qkv_ref[0, :, c * cols : (c + 1) * cols] = out.astype(bf16)

    at = pl.multiple_of(pair * 2 * HD, 2 * HD)
    q = qkv_ref[0, :, pl.ds(at, 2 * HD)]
    k = qkv_ref[0, :, pl.ds(cols + at, 2 * HD)]
    v = qkv_ref[0, :, pl.ds(2 * cols + at, 2 * HD)]
    lane = lax.broadcasted_iota(jnp.int32, q.shape, 1)
    joined = None
    for hh in range(2):
        mine = (lane // HD) == hh
        kh = jnp.where(mine, k, jnp.zeros_like(k))
        st = dot(kh, q, ((1,), (1,))) * 0.125
        top = jnp.max(st, axis=0, keepdims=True)
        e = jnp.exp(st - top)
        p = (e * (1.0 / jnp.sum(e, axis=0, keepdims=True))).astype(bf16)
        p_ref[0, hh] = p
        c = dot(p, v, ((0,), (0,)))
        joined = c if joined is None else jnp.where(mine, c, joined)
    c_ref[0] = joined.astype(bf16)


def attend(first, shards, gathered, place, x, bias):
    length, width = x.shape
    cols = gathered.dims[-1]
    pairs = cols // (2 * HD)
    n_w = len(gathered.arrays)
    return pl.pallas_call(
        functools.partial(attend_body, first, shards, gathered),
        grid=(shards, pairs),
        out_shape=[
            jax.ShapeDtypeStruct((shards, length, 3 * cols), bf16),
            jax.ShapeDtypeStruct((shards, 2 * pairs, length, length), bf16),
            jax.ShapeDtypeStruct((shards, length, cols), bf16),
        ],
        in_specs=[SMEM, whole(x.shape), pl.BlockSpec((1, 3, 1, cols), lambda s, i: (s, 0, 0, 0))]
        + [HBM] * n_w,
        out_specs=[
            pl.BlockSpec((1, length, 3 * cols), lambda s, i: (s, 0, 0)),
            pl.BlockSpec((1, 2, length, length), lambda s, i: (s, i, 0, 0)),
            pl.BlockSpec((1, length, 2 * HD), lambda s, i: (s, 0, i)),
        ],
        scratch_shapes=gathered.scratch(shards + (1 if first else 0)),
        compiler_params=params(),
        cost_estimate=cost(
            shards * (6 * length * width * cols + 8 * pairs * length * length * HD),
            shards * 2 * pairs * length * length,
            shards * (6 * width * cols + 4 * pairs * length * length),
        ),
        name="attend",
    )(place, x, bias, *gathered.arrays)


def norm_stats(values):
    center = values - jnp.mean(values, axis=-1, keepdims=True)
    inv = lax.rsqrt(jnp.mean(center * center, axis=-1, keepdims=True) + 1e-05)
    return center * inv, inv


def norm_back(grad, n, inv, gain):
    gn = grad * gain
    return (gn - jnp.mean(gn, -1, keepdims=True) - n * jnp.mean(gn * n, -1, keepdims=True)) * inv


def up_body(shards, g_out, g_up, place_ref, near_ref, far_ref, x_ref, te_ref, vec_ref, bias_ref, *refs):
    n_out, n_up = len(g_out.arrays), len(g_up.arrays)
    shared = [refs[0]] + list(refs[1:n_out])
    up_refs = [refs[n_out]] + list(refs[1:n_out])
    n1_ref, inv_ref, low_ref, act_ref, slope_ref, wo, o_sems, wu, u_sems, acc = refs[n_out + 1 :]
    s = pl.program_id(0)
    place = place_ref[0]
    length, width = acc.shape

    @pl.when(s == 0)
    def _():
        g_out.start_all(shared, place, wo, o_sems, shards)
        g_up.start_all(up_refs, place, wu, u_sems, shards)
        g_out.wait(shared, place, wo, o_sems, 0)
        acc[...] = dot(near_ref[0], wo[0].reshape(-1, width), ((1,), (0,)))
        for shard in range(1, shards):
            for copy in g_out._copies(shared, place, wo, o_sems, shard):
                copy.wait()
            acc[...] += dot(far_ref[shard - 1], wo[shard].reshape(-1, width), ((1,), (0,)))

        def rows(i, _):
            at = pl.ds(pl.multiple_of(i * 64, 64), 64)
            start = x_ref[at, :].astype(f32) + te_ref[...]
            n1, inv = norm_stats(start + (acc[at, :] + vec_ref[0:1, :]))
            n1_ref[at, :] = n1
            inv_ref[at, :] = jnp.broadcast_to(inv, (64, inv_ref.shape[1]))
            low_ref[at, :] = (n1 * vec_ref[1:2, :] + vec_ref[2:3, :]).astype(bf16)
            return 0

        lax.fori_loop(0, length // 64, rows, 0)

    g_up.wait(up_refs, place, wu, u_sems, s)
    units = wu.shape[-1]
    for n in range(units // 256):
        span = slice(n * 256, (n + 1) * 256)
        u = dot(low_ref[...], wu[s, :, :, :, span].reshape(width, 256), ((1,), (0,)))
        u = u + bias_ref[0, :, span]
        phi = 0.5 + 0.5 * lax.erf(u * (2.0**-0.5))
        act_ref[0, :, span] = (u * phi).astype(bf16)
        slope_ref[0, :, span] = (
            phi + u * jnp.exp(-0.5 * u * u) * (2.0 * math.pi) ** -0.5
        ).astype(bf16)


def up_project(g_out, g_up, place, near, far, x, time_embed, vec, bias):
    length, width = x.shape
    shards = far.shape[0] + 1
    units = g_up.dims[-1]
    block = pl.BlockSpec((1, length, units), lambda s: (s, 0, 0))
    return pl.pallas_call(
        functools.partial(up_body, shards, g_out, g_up),
        grid=(shards,),
        out_shape=[
            jax.ShapeDtypeStruct((length, width), f32),
            jax.ShapeDtypeStruct((length, 128), f32),
            jax.ShapeDtypeStruct((length, width), bf16),
            jax.ShapeDtypeStruct((shards, length, units), bf16),
            jax.ShapeDtypeStruct((shards, length, units), bf16),
        ],
        in_specs=[
            SMEM,
            whole(near.shape),
            whole(far.shape),
            whole(x.shape),
            whole(time_embed.shape),
            whole(vec.shape),
            pl.BlockSpec((1, 1, units), lambda s: (s, 0, 0)),
        ]
        + [HBM] * (len(g_out.arrays) + 1),
        out_specs=[
            whole((length, width)),
            whole((length, 128)),
            whole((length, width)),
            block,
            block,
        ],
        scratch_shapes=g_out.scratch(shards) + g_up.scratch(shards) + [pltpu.VMEM((length, width), f32)],
        compiler_params=params(),
        cost_estimate=cost(
            2 * length * width * (width + shards * units),
            2 * shards * length * units,
            2 * width * (width + shards * units) + 4 * shards * length * units,
        ),
        name="up_project",
    )(place, near, far, x, time_embed, vec, bias, *g_out.arrays, g_up.arrays[0])


def down_body(shards, gathered, place_ref, live_ref, act_ref, n1_ref, cot_ref, vec_ref, *refs):
    n = len(gathered.arrays)
    w_refs, (out_ref, gs_ref, bg_ref, sums_ref, w, sems, acc) = refs[:n], refs[n:]
    s = pl.program_id(0)
    place = place_ref[0]
    length, width = acc.shape

    @pl.when(s == 0)
    def _():
        gathered.start_all(w_refs, place, w, sems, shards)

    gathered.wait(w_refs, place, w, sems, s)
    part = dot(act_ref[0], w[s].reshape(-1, width), ((1,), (0,)))

    @pl.when(s == 0)
    def _():
        acc[...] = part

    @pl.when(s > 0)
    def _():
        acc[...] += part

    @pl.when(s == shards - 1)
    def _():
        live = live_ref[0]

        def rows(i, sums):
            at = pl.ds(pl.multiple_of(i * 64, 64), 64)
            normed = n1_ref[at, :] * vec_ref[1:2, :] + vec_ref[2:3, :]
            n2, inv = norm_stats(normed + (acc[at, :] + vec_ref[0:1, :]))
            out_ref[at, :] = (n2 * vec_ref[3:4, :] + vec_ref[4:5, :]).astype(bf16)
            grad = cot_ref[at, :].astype(f32) * live
            second = norm_back(grad, n2, inv, vec_ref[3:4, :])
            gs_ref[at, :] = second
            low = second.astype(bf16)
            bg_ref[at, :] = low
            add = (low.astype(f32), grad * n2, grad)
            return tuple(a + jnp.sum(b, axis=0, keepdims=True) for a, b in zip(sums, add))

        zero = jnp.zeros((1, width), f32)
        sums = lax.fori_loop(0, length // 64, rows, (zero, zero, zero))
        for i, v in enumerate(sums):
            sums_ref[i : i + 1, :] = v


def down_project(gathered, place, live, act, n1, cot, vec):
    shards, length, units = act.shape
    width = n1.shape[1]
    return pl.pallas_call(
        functools.partial(down_body, shards, gathered),
        grid=(shards,),
        out_shape=[
            jax.ShapeDtypeStruct((length, width), bf16),
            jax.ShapeDtypeStruct((length, width), f32),
            jax.ShapeDtypeStruct((length, width), bf16),
            jax.ShapeDtypeStruct((3, width), f32),
        ],
        in_specs=[
            SMEM,
            SMEM,
            pl.BlockSpec((1, length, units), lambda s: (s, 0, 0)),
            whole(n1.shape),
            whole(cot.shape),
            whole(vec.shape),
        ]
        + [HBM] * len(gathered.arrays),
        out_specs=[whole((length, width))] * 3 + [whole((3, width))],
        scratch_shapes=gathered.scratch(shards) + [pltpu.VMEM((length, width), f32)],
        compiler_params=params(),
        cost_estimate=cost(
            2 * length * width * shards * units,
            0,
            2 * shards * units * (width + length) + 12 * length * width,
        ),
        name="down_project",
    )(place, live, act, n1, cot, vec, *gathered.arrays)


def up_back_body(shards, g_down, g_up, place_ref, bg_ref, slope_ref, gs_ref, n1_ref, inv_ref, vec_ref, *refs):
    n_d, n_u = len(g_down.arrays), len(g_up.arrays)
    d_refs, u_refs = refs[:n_d], refs[n_d : n_d + n_u]
    ug_ref, bias_ref, gf_ref, mg_ref, sums_ref, wd, d_sems, wu, u_sems, acc = refs[n_d + n_u :]
    s = pl.program_id(0)
    place = place_ref[0]
    length, width = acc.shape

    @pl.when(s == 0)
    def _():
        g_down.start_all(d_refs, place, wd, d_sems, shards)
        g_up.start_all(u_refs, place, wu, u_sems, shards)
        acc[...] = gs_ref[...]

    g_down.wait(d_refs, place, wd, d_sems, s)
    units = ug_ref.shape[2]
    for n in range(units // 256):
        span = slice(n * 256, (n + 1) * 256)
        rows = wd[s, 2 * n : 2 * n + 2].reshape(256, width)
        grad = dot(bg_ref[...], rows, ((1,), (1,)))
        low = (grad * slope_ref[0, :, span].astype(f32)).astype(bf16)
        ug_ref[0, :, span] = low
        bias_ref[0, :, span] = jnp.sum(low.astype(f32), axis=0, keepdims=True)
    g_up.wait(u_refs, place, wu, u_sems, s)
    acc[...] += dot(ug_ref[0], wu[s].reshape(width, units), ((1,), (1,)))

    @pl.when(s == shards - 1)
    def _():
        def rows(i, sums):
            at = pl.ds(pl.multiple_of(i * 64, 64), 64)
            n1, grad = n1_ref[at, :], acc[at, :]
            first = norm_back(grad, n1, inv_ref[at, 0:1], vec_ref[1:2, :])
            gf_ref[at, :] = first
            low = first.astype(bf16)
            mg_ref[at, :] = low
            add = (low.astype(f32), grad * n1, grad)
            return tuple(a + jnp.sum(b, axis=0, keepdims=True) for a, b in zip(sums, add))

        zero = jnp.zeros((1, width), f32)
        sums = lax.fori_loop(0, length // 64, rows, (zero, zero, zero))
        for i, v in enumerate(sums):
            sums_ref[i : i + 1, :] = v


def up_back(g_down, g_up, place, bg, slope, gs, n1, inv, vec):
    shards, length, units = slope.shape
    width = n1.shape[1]
    block = pl.BlockSpec((1, length, units), lambda s: (s, 0, 0))
    return pl.pallas_call(
        functools.partial(up_back_body, shards, g_down, g_up),
        grid=(shards,),
        out_shape=[
            jax.ShapeDtypeStruct((shards, length, units), bf16),
            jax.ShapeDtypeStruct((shards, 1, units), f32),
            jax.ShapeDtypeStruct((length, width), f32),
            jax.ShapeDtypeStruct((length, width), bf16),
            jax.ShapeDtypeStruct((3, width), f32),
        ],
        in_specs=[
            SMEM,
            whole(bg.shape),
            block,
            whole(gs.shape),
            whole(n1.shape),
            whole(inv.shape),
            whole(vec.shape),
        ]
        + [HBM] * (len(g_down.arrays) + len(g_up.arrays)),
        out_specs=[
            block,
            pl.BlockSpec((1, 1, units), lambda s: (s, 0, 0)),
            whole((length, width)),
            whole((length, width)),
            whole((3, width)),
        ],
        scratch_shapes=g_down.scratch(shards)
        + g_up.scratch(shards)
        + [pltpu.VMEM((length, width), f32)],
        compiler_params=params(),
        cost_estimate=cost(
            4 * length * width * shards * units,
            0,
            4 * shards * units * (width + length) + 16 * length * width,
        ),
        name="up_back",
    )(place, bg, slope, gs, n1, inv, vec, *g_down.arrays, *g_up.arrays)


def attend_back_body(shards, g_out, g_qkv, place_ref, mg_ref, near_ref, far_ref, pn_ref, pf_ref, gf_ref, *refs):
    n_o, n_q = len(g_out.arrays), len(g_qkv.arrays)
    o_refs, q_refs = refs[:n_o], refs[n_o : n_o + n_q]
    pg_ref, gt_ref, bias_ref, tg_ref, wo, o_sems, wq, q_sems, acc, cg = refs[n_o + n_q :]
    s, pair = pl.program_id(0), pl.program_id(1)
    place = place_ref[0]
    length, width = acc.shape
    cols = wq.shape[-1]

    @pl.when((s == 0) & (pair == 0))
    def _():
        g_out.start_all(o_refs, place, wo, o_sems, shards)
        g_qkv.start_all(q_refs, place, wq, q_sems, shards)
        acc[...] = gf_ref[...]

    @pl.when(pair == 0)
    def _():
        g_out.wait(o_refs, place, wo, o_sems, s)
        cg[...] = dot(mg_ref[...], wo[s].reshape(cols, width), ((1,), (1,))).astype(bf16)

    at = pl.multiple_of(pair * 2 * HD, 2 * HD)

    def one(qkv, p_of):
        q = qkv[0, :, pl.ds(at, 2 * HD)]
        k = qkv[0, :, pl.ds(cols + at, 2 * HD)]
        v = qkv[0, :, pl.ds(2 * cols + at, 2 * HD)]
        g = cg[:, pl.ds(at, 2 * HD)]
        lane = lax.broadcasted_iota(jnp.int32, q.shape, 1)
        dq = dk = dv = None
        for hh in range(2):
            mine = (lane // HD) == hh
            zero = jnp.zeros_like(q)
            gh = jnp.where(mine, g, zero)
            kh = jnp.where(mine, k, zero)
            qh = jnp.where(mine, q, zero)
            p = p_of[0, hh]
            dpt = dot(v, gh, ((1,), (1,)))
            pf = p.astype(f32)
            row = jnp.sum(pf * dpt, axis=0, keepdims=True)
            ds = (pf * (dpt - row)).astype(bf16)
            a = dot(p, gh, ((1,), (0,)))
            b = dot(ds, qh, ((1,), (0,)))
            c = dot(ds, kh, ((0,), (0,)))
            dv = a if dv is None else dv + a
            dk = b if dk is None else dk + b
            dq = c if dq is None else dq + c
        for c, g in enumerate((dq * 0.125, dk * 0.125, dv)):
            low = g.astype(bf16)
            pg_ref[0, :, pl.ds(c * cols + at, 2 * HD)] = low
            bias_ref[0, :, pl.ds(c * cols + at, 2 * HD)] = jnp.sum(
                low.astype(f32), axis=0, keepdims=True
            )

    @pl.when(s == 0)
    def _():
        one(near_ref, pn_ref)

    @pl.when(s > 0)
    def _():
        one(far_ref, pf_ref)

    @pl.when(pair == pl.num_programs(1) - 1)
    def _():
        g_qkv.wait(q_refs, place, wq, q_sems, s)
        for c in range(3):
            acc[...] += dot(
                pg_ref[0, :, c * cols : (c + 1) * cols],
                wq[s, c].reshape(width, cols),
                ((1,), (1,)),
            )

    @pl.when((pair == pl.num_programs(1) - 1) & (s == shards - 1))
    def _():
        def rows(i, total):
            rows_at = pl.ds(pl.multiple_of(i * 64, 64), 64)
            grad = acc[rows_at, :]
            gt_ref[rows_at, :] = grad.astype(bf16)
            return total + jnp.sum(grad, axis=0, keepdims=True)

        tg_ref[...] = lax.fori_loop(0, length // 64, rows, jnp.zeros((1, width), f32))


def attend_back(g_out, g_qkv, place, mg, near, far, p_near, p_far, gf):
    length, width = mg.shape
    shards = far.shape[0] + 1
    cols = g_qkv.dims[-1]
    pairs = cols // (2 * HD)
    last = pairs - 1

    def before(s, i):
        return (0, jnp.where(s == 0, i, last), 0, 0)

    def after(s, i):
        return (jnp.maximum(s - 1, 0), jnp.where(s == 0, 0, i), 0, 0)

    return pl.pallas_call(
        functools.partial(attend_back_body, shards, g_out, g_qkv),
        grid=(shards, pairs),
        out_shape=[
            jax.ShapeDtypeStruct((shards, length, 3 * cols), bf16),
            jax.ShapeDtypeStruct((length, width), bf16),
            jax.ShapeDtypeStruct((shards, 1, 3 * cols), f32),
            jax.ShapeDtypeStruct((1, width), f32),
        ],
        in_specs=[
            SMEM,
            whole(mg.shape),
            whole(near.shape),
            pl.BlockSpec((1, length, 3 * cols), lambda s, i: (jnp.maximum(s - 1, 0), 0, 0)),
            pl.BlockSpec((1, 2, length, length), before),
            pl.BlockSpec((1, 2, length, length), after),
            whole(gf.shape),
        ]
        + [HBM] * (len(g_out.arrays) + len(g_qkv.arrays)),
        out_specs=[
            pl.BlockSpec((1, length, 3 * cols), lambda s, i: (s, 0, 0)),
            whole((length, width)),
            pl.BlockSpec((1, 1, 3 * cols), lambda s, i: (s, 0, 0)),
            whole((1, width)),
        ],
        scratch_shapes=g_out.scratch(shards)
        + g_qkv.scratch(shards)
        + [pltpu.VMEM((length, width), f32), pltpu.VMEM((length, cols), bf16)],
        compiler_params=params(),
        cost_estimate=cost(
            shards * (8 * length * width * cols + 20 * pairs * length * length * HD),
            0,
            shards * (8 * width * cols + 4 * pairs * length * length) + 8 * length * width,
        ),
        name="attend_back",
    )(place, mg, near, far, p_near, p_far, gf, *g_out.arrays, *g_qkv.arrays)


def weight_grad_body(order, n_pairs, place_ref, *refs):
    ins = refs[: 4 * n_pairs]
    keep_ref, send_ref = refs[4 * n_pairs : 4 * n_pairs + 2]
    turned = refs[4 * n_pairs + 2 :]
    place = place_ref[0]
    rows = keep_ref.shape[2]

    @pl.when(pl.program_id(0) == 0)
    def _():
        for p in range(n_pairs):
            for half in range(2):
                feature_ref = ins[4 * p + half]
                length = feature_ref.shape[0]
                for j in range(4):
                    at = pl.multiple_of((place ^ (2 * j)) * rows, rows)
                    block = feature_ref[:, pl.ds(at, rows)]
                    turned[p][j * rows : (j + 1) * rows, half * length : (half + 1) * length] = block.T

    at = 0
    for p in range(n_pairs):
        b_ref, b2_ref = ins[4 * p + 2 : 4 * p + 4]
        length, cols = b_ref.shape[1:]
        for n in range(cols // 256):
            span = slice(n * 256, (n + 1) * 256)
            g = dot(turned[p][:, :length], b_ref[0, :, span], ((1,), (0,)))
            g += dot(turned[p][:, length:], b2_ref[0, :, span], ((1,), (0,)))
            g = g.astype(bf16)
            for out, picks in ((keep_ref, order[:2]), (send_ref, order[2:])):
                for i, j in enumerate(picks):
                    out[0, i, :, at : at + 256] = g[j * rows : (j + 1) * rows]
            at += 256


def weight_grad(path, place, groups):
    order = (0, 2, 1, 3) if path == 0 else (0, 1, 2, 3)
    shards, length, _ = groups[0][2].shape
    half = shards // 2
    rows = groups[0][0].shape[1] // 8
    cols = sum(g[2].shape[2] for g in groups)
    base = path * half
    specs, args, scratch = [], [], []
    for feature, feature2, b, b2 in groups:
        block = pl.BlockSpec((1,) + b.shape[1:], lambda s: (s + base, 0, 0))
        specs += [whole(feature.shape)] * 2 + [block] * 2
        args += [feature, feature2, b, b2]
        scratch.append(pltpu.VMEM((4 * rows, 2 * length), bf16))
    out = jax.ShapeDtypeStruct((half, 2, rows, cols), bf16)
    return pl.pallas_call(
        functools.partial(weight_grad_body, order, len(groups)),
        grid=(half,),
        out_shape=[out, out],
        in_specs=[SMEM] + specs,
        out_specs=[pl.BlockSpec((1, 2, rows, cols), lambda s: (s, 0, 0, 0))] * 2,
        scratch_shapes=scratch,
        compiler_params=params(),
        cost_estimate=cost(
            half * 16 * rows * length * cols,
            0,
            half * (4 * length * cols + 8 * rows * cols) + 4 * length * 8 * rows,
        ),
        name="weight_grad",
    )(place, *args)


def on_device(
    tokens,
    timesteps,
    buckets,
    counts,
    w_time,
    table,
    w_qkv,
    b_qv,
    w_out,
    b_out,
    gain1,
    shift1,
    w_up,
    b_up,
    w_down,
    b_down,
    gain2,
    shift2,
    cotangent,
):
    mpn = lax.axis_size("mp")
    dpn = lax.axis_size("dp")
    extra = dpn.bit_length() - 4
    me = lax.axis_index("dp")
    z = lax.axis_index("mp")
    q8 = me >> extra
    width = w_time.shape[0]
    positions, slots = tokens.shape[:2]
    length = positions * mpn
    head_cols = w_qkv.shape[2]
    units = w_up.shape[1]

    def flip(x, mask):
        step = mask << extra
        return lax.ppermute(x, "dp", [(i, i ^ step) for i in range(dpn)])

    def shift(x, s):
        return lax.ppermute(x, "mp", [(i, (i + s) % mpn) for i in range(mpn)])

    def to_items(x):
        x = lax.all_to_all(jnp.moveaxis(x, 1, 0), "mp", 0, 0, tiled=False)
        return x.reshape(length, width)

    def to_positions(x):
        x = lax.all_to_all(x.reshape(mpn, positions, width), "mp", 0, 0, tiled=False)
        return jnp.moveaxis(x, 0, 1)

    def spread(arrived):
        pieces, plan = [], []
        for path, (first, second) in enumerate(PATHS):
            mine = jnp.stack([a[path] for a in arrived])
            held = jnp.stack([mine, flip(mine, first)])
            far = flip(held, second)
            near = (0, first)
            beyond = (second, first | second)
            pieces += [held, far, flip(held, 1), flip(far, 1)]
            plan += [(path, m) for m in (near, beyond)]
            plan += [(path, tuple(v ^ 1 for v in m)) for m in (near, beyond)]
        return pieces, plan

    def split(shard, axis):
        dims = shard.shape
        return shard.reshape(dims[:axis] + (8, 2, dims[axis] // 16) + dims[axis + 1 :])

    def eighth(shaped, axis):
        return jnp.moveaxis(lax.dynamic_index_in_dim(shaped, q8, axis, False), axis, 0)

    def along_z(part):
        return [shift(part, s) for s in range(1, mpn)]

    place = q8.astype(jnp.int32)[None]
    own_qkv, own_out, own_up, own_down = split(w_qkv, 1), split(w_out, 0), split(w_up, 0), split(w_down, 0)

    z_qkv = along_z(eighth(own_qkv, 1))
    pieces, plan = spread(z_qkv)
    g_qkv = Gathered(own_qkv, pieces, plan, (3,), 0)

    part = jnp.concatenate([eighth(own_out, 0), eighth(own_up, 0)], axis=1)
    part, _ = lax.optimization_barrier((part, z_qkv))
    z_up = along_z(part)
    pieces, plan = spread(z_up)
    g_out = Gathered(own_out, pieces, plan, (), 0)
    g_up = Gathered(own_up, pieces, plan, (), own_out.shape[2])

    part, _ = lax.optimization_barrier((eighth(own_down, 0), z_up))
    z_down = along_z(part)
    pieces, plan = spread(z_down)
    g_down = Gathered(own_down, pieces, plan, (), 0)

    biases = jnp.concatenate([b_up, b_qv[0], b_qv[1]])
    biases = jnp.stack([biases] + [shift(biases, s) for s in range(1, mpn)])
    up_bias = biases[:, None, :units]
    qkv_bias = biases[:, units:].reshape(mpn, 2, 1, head_cols)
    qkv_bias = jnp.stack([qkv_bias[:, 0], jnp.zeros_like(qkv_bias[:, 0]), qkv_bias[:, 1]], axis=1)

    total_live = jnp.sum(counts).astype(f32)
    weighting = 1.0 / total_live
    live = (z < lax.dynamic_index_in_dim(counts, me, 0, True)).astype(f32)
    my_step = lax.dynamic_index_in_dim(timesteps, z, 0, True)
    my_bucket = lax.dynamic_index_in_dim(buckets, z, 0, False)
    time_embed = jnp.dot(
        sinusoid(my_step.astype(f32), width), w_time, preferred_element_type=f32
    ) + lax.dynamic_index_in_dim(table, my_bucket, 0, True)

    x = to_items(tokens)
    hidden = (x.astype(f32) + time_embed).astype(bf16)

    g_near = Gathered(own_qkv, [], [], (3,), 0)
    qkv_near, p_near, ctx_near = attend(0, 1, g_near, place, hidden, qkv_bias[:1])
    qkv_far, p_far, ctx_far = attend(1, mpn - 1, g_qkv, place, hidden, qkv_bias[1:])
    n1, inv1, normed_low, active, slope = up_project(
        g_out, g_up, place, ctx_near, ctx_far, x, time_embed, jnp.stack([b_out, gain1, shift1]), up_bias
    )
    late_cot, _ = lax.optimization_barrier((cotangent, z_down))
    cot = to_items(late_cot)
    output, grad_second, branch_grad, sums2 = down_project(
        g_down, place, live, active, n1, cot, jnp.stack([b_down, gain1, shift1, gain2, shift2])
    )
    output = to_positions(output)

    def reduced(groups):
        total = None
        for path, (first, second) in enumerate(PATHS):
            keep, sent = weight_grad(path, place, groups)
            came = flip(sent, first)
            passed = (keep[:, 1].astype(f32) + came[:, 1].astype(f32)).astype(bf16)
            part = keep[:, 0].astype(f32) + came[:, 0].astype(f32) + flip(passed, second).astype(f32)
            for i in range(mpn // 2):
                s = path * mpn // 2 + i
                piece = part[i] if s == 0 else shift(part[i].astype(bf16), -s).astype(f32)
                total = piece if total is None else total + piece
        for t in reversed(range(extra)):
            half = total.shape[0] // 2
            bit = (me >> t) & 1
            keep = lax.dynamic_slice_in_dim(total, bit * half, half, 0)
            sent = lax.dynamic_slice_in_dim(total, (1 - bit) * half, half, 0)
            total = keep + lax.ppermute(sent, "dp", [(i, i ^ (1 << t)) for i in range(dpn)])
        return total * weighting

    active2 = flip(active, 1)
    low2 = flip(normed_low, 1)
    ctx = jnp.concatenate([ctx_near, ctx_far])
    ctx2 = flip(ctx, 1)
    hidden2 = flip(hidden, 1)
    branch_grad2 = flip(branch_grad, 1)
    grad_w_down = reduced([(branch_grad, branch_grad2, active, active2)]).T
    up_grad, bias_up, grad_first, mixing_grad, sums1 = up_back(
        g_down, g_up, place, branch_grad, slope, grad_second, n1, inv1, jnp.stack([b_out, gain1, shift1])
    )
    grad_w_up = reduced([(normed_low, low2, up_grad, flip(up_grad, 1))])
    proj_grad, grad_tokens, bias_proj, time_grad = attend_back(
        g_out, g_qkv, place, mixing_grad, qkv_near, qkv_far, p_near, p_far, grad_first
    )
    both_grads = reduced(
        [
            (hidden, hidden2, proj_grad, flip(proj_grad, 1)),
            (mixing_grad, flip(mixing_grad, 1), ctx, ctx2),
        ]
    )
    grad_w_qkv = both_grads[:, : 3 * head_cols].reshape(-1, 3, head_cols)
    grad_w_qkv = jnp.moveaxis(grad_w_qkv, 1, 0)
    grad_w_out = both_grads[:, 3 * head_cols :].T
    grad_tokens = to_positions(grad_tokens).astype(f32)

    devices = dpn * mpn

    def in_order(parts):
        turned = jnp.stack([parts[-i % mpn] for i in range(mpn)] * 2)
        return lax.dynamic_slice_in_dim(turned, (mpn - z) % mpn, mpn, 0).reshape(-1)

    vectors = [
        in_order(bias_proj[:, 0, :head_cols]),
        in_order(bias_proj[:, 0, 2 * head_cols :]),
        sums1[0],
        sums1[1],
        sums1[2],
        sums2[0],
        sums2[1],
        sums2[2],
        in_order(bias_up[:, 0]),
    ]
    spread_out = jnp.concatenate([v.reshape(devices, -1) for v in vectors], axis=1)
    facts = jnp.stack([my_step[0].astype(f32), my_bucket.astype(f32)])
    facts = jnp.broadcast_to(facts[None], (devices, 2))
    both = ("dp", "mp")
    gathered = lax.all_to_all(jnp.concatenate([spread_out, facts], axis=1), both, 0, 0, tiled=True)
    summed = jnp.sum(gathered[:, :-2], axis=0) * weighting
    steps, rows_of = gathered[:, -2], gathered[:, -1]
    per = width // devices
    small = [summed[i * per : (i + 1) * per] for i in range(8)]
    grad_b_up = summed[8 * per :]
    grads = lax.all_to_all(time_grad.reshape(devices, per), both, 0, 0, tiled=True)
    high = lax.Precision.HIGHEST
    grad_w_time = (
        jnp.einsum("nd,ne->de", sinusoid(steps, width).astype(f32), grads, precision=high)
        * weighting
    )
    onehot = (rows_of[:, None] == jnp.arange(table.shape[0], dtype=f32)[None, :]).astype(f32)
    grad_table = jnp.einsum("nb,nd->bd", onehot, grads, precision=high) * weighting
    return (
        output,
        grad_tokens,
        grad_w_time,
        grad_table,
        grad_w_qkv,
        jnp.stack(small[:2]),
        grad_w_out,
        small[2],
        small[3],
        small[4],
        grad_w_up,
        grad_b_up,
        grad_w_down,
        small[5],
        small[6],
        small[7],
    )


def solution(mesh):
    return jax.shard_map(
        on_device,
        mesh=mesh,
        in_specs=(
            P("mp", "dp", None),
            P("dp"),
            P("dp"),
            P(),
            P(),
            P(),
            P(None, None, "mp"),
            P(None, "mp"),
            P("mp", None),
            P(),
            P(),
            P(),
            P(None, "mp"),
            P("mp"),
            P("mp", None),
            P(),
            P(),
            P(),
            P("mp", "dp", None),
        ),
        out_specs=(
            P("mp", "dp", None),
            P("mp", "dp", None),
            P(None, ("dp", "mp")),
            P(None, ("dp", "mp")),
            P(None, "dp", "mp"),
            P(None, ("dp", "mp")),
            P("mp", "dp"),
            P(("dp", "mp")),
            P(("dp", "mp")),
            P(("dp", "mp")),
            P("dp", "mp"),
            P(("dp", "mp")),
            P("mp", "dp"),
            P(("dp", "mp")),
            P(("dp", "mp")),
            P(("dp", "mp")),
        ),
        check_vma=False,
    )
```

```python
import functools
import math

import jax
import jax.numpy as jnp
from jax import lax
from jax.experimental import pallas as pl
from jax.experimental.pallas import tpu as pltpu
from jax.sharding import PartitionSpec as P

HD = 64
f32 = jnp.float32
bf16 = jnp.bfloat16
VMEM_LIMIT = 56 * 2**20


def params(**more):
    return pltpu.CompilerParams(vmem_limit_bytes=VMEM_LIMIT, **more)


def dot(a, b, dims):
    return lax.dot_general(a, b, (dims, ((), ())), preferred_element_type=f32)


def sinusoid(steps, model_width):
    half_width = model_width // 2
    freqs = jnp.exp(-math.log(10000.0) * jnp.arange(half_width, dtype=f32) / half_width)
    angles = steps[:, None] * freqs[None, :]
    return jnp.concatenate([jnp.sin(angles), jnp.cos(angles)], axis=-1).astype(bf16)


def masks(place):
    first = 2 + 2 * (place & 1)
    return first, 6 - first


class Gathered:
    def __init__(self, own, pieces, lead, start):
        self.arrays = [own] + pieces
        self.lead = lead
        self.start = start
        self.dims = own.shape

    def scratch(self, shards):
        return [pltpu.VMEM((shards,) + self.dims, bf16), pltpu.SemaphoreType.DMA((shards, 8))]

    def copies_of(self, refs, place, into, sems, shard, slot):
        if isinstance(shard, int) and shard == 0:
            return [pltpu.make_async_copy(refs[0], into.at[slot], sems.at[slot, 0])]
        lead = (slice(None),) * self.lead
        first, second = masks(place)
        held = (place, place ^ first)
        far = (place ^ second, place ^ 6)
        held2 = (place ^ 1, place ^ 1 ^ second)
        far2 = (place ^ 1 ^ first, place ^ 7)
        made = []
        for ref, chunks in zip(refs[1:], (held, far, held2, far2)):
            for i, chunk in enumerate(chunks):
                at = lead + (pl.ds(self.start, self.dims[-2]),)
                made.append(
                    pltpu.make_async_copy(
                        ref.at[i, shard - 1].at[at],
                        into.at[(slot,) + lead + (chunk,)],
                        sems.at[slot, len(made)],
                    )
                )
        return made

    def start_all(self, refs, place, into, sems, shards):
        for shard in range(shards):
            for copy in self.copies_of(refs, place, into, sems, shard, shard):
                copy.start()

    def wait(self, refs, place, into, sems, shard):
        @pl.when(shard == 0)
        def _():
            for copy in self.copies_of(refs, place, into, sems, 0, 0):
                copy.wait()

        @pl.when(shard > 0)
        def _():
            for copy in self.copies_of(refs, place, into, sems, shard, shard):
                copy.wait()


HBM = pl.BlockSpec(memory_space=pl.ANY)
SMEM = pl.BlockSpec(memory_space=pltpu.SMEM)


def whole(shape):
    return pl.BlockSpec(shape, lambda *_: (0,) * len(shape))


def cost(micros):
    return pl.CostEstimate(flops=int(micros * 1.15e9), transcendentals=0, bytes_accessed=0)


def over_rows(length, step, body, init):
    def one(i, carry):
        return body(pl.ds(pl.multiple_of(i * step, step), step), carry)

    return lax.fori_loop(0, length // step, one, init)


def row_sum(v):
    return jnp.sum(v, axis=0, keepdims=True)


def pack_body(rows, n, *refs):
    out_ref = refs[n]
    for i, ref in enumerate(refs[:n]):
        out_ref[i] = ref[..., :rows, :]
        if len(refs) > n + 1:
            total = ref[..., rows : rows + 1, :].astype(f32)
            for part in range(1, 3):
                total += ref[..., rows + part : rows + part + 1, :].astype(f32)
            refs[n + 1][i] = total


def pack(covers, parts, rows=None):
    dims = parts[0].shape
    n = len(parts)
    out = [(n,) + dims[:-2] + (rows or dims[-2], dims[-1])]
    if rows:
        out.append((n,) + dims[:-2] + (1, dims[-1]))
    made = pl.pallas_call(
        functools.partial(pack_body, rows or dims[-2], n),
        out_shape=[jax.ShapeDtypeStruct(o, t) for o, t in zip(out, (bf16, f32))],
        compiler_params=params(),
        cost_estimate=cost(covers),
        name="pack",
    )(*parts)
    return made if rows else made[0]


def in_three(v):
    parts = []
    for _ in range(3):
        parts.append(lax.reduce_precision(v, 8, 7))
        v = v - parts[-1]
    return jnp.concatenate(parts + [jnp.zeros_like(v)] * 5, axis=-2).astype(bf16)


def embed_body(sinus_ref, w_ref, row_ref, out_ref):
    out_ref[...] = dot(sinus_ref[...], w_ref[...], ((1,), (0,)))[:1] + row_ref[...]


def embed(covers, sinus, w, row):
    return pl.pallas_call(
        embed_body,
        out_shape=jax.ShapeDtypeStruct(row.shape, f32),
        compiler_params=params(),
        cost_estimate=cost(covers),
        name="embed",
    )(jnp.broadcast_to(sinus, (16,) + sinus.shape[1:]), w, row)


def attend_body(shard, gathered, place_ref, x_ref, bias_ref, *refs):
    n = len(gathered.arrays)
    w_refs = refs[:n]
    qkv_ref, p_ref, c_ref, w, sems = refs[-5:]
    pair = pl.program_id(0)
    place = place_ref[0]
    cols = w.shape[-1]

    @pl.when(pair == 0)
    def _():
        copies = gathered.copies_of(w_refs, place, w, sems, shard, 0)
        for copy in copies:
            copy.start()
        for copy in copies:
            copy.wait()
        for c in range(3):
            wide = w[0, c].reshape(x_ref.shape[1], cols)
            out = dot(x_ref[...], wide, ((1,), (0,))) + bias_ref[0, c]
            qkv_ref[0, :, c * cols : (c + 1) * cols] = out.astype(bf16)

    at = pl.multiple_of(pair * 2 * HD, 2 * HD)
    q = qkv_ref[0, :, pl.ds(at, 2 * HD)]
    k = qkv_ref[0, :, pl.ds(cols + at, 2 * HD)]
    v = qkv_ref[0, :, pl.ds(2 * cols + at, 2 * HD)]
    lane = lax.broadcasted_iota(jnp.int32, q.shape, 1)
    joined = None
    for hh in range(2):
        mine = (lane // HD) == hh
        kh = jnp.where(mine, k, jnp.zeros_like(k))
        st = dot(kh, q, ((1,), (1,))) * 0.125
        top = jnp.max(st, axis=0, keepdims=True)
        e = jnp.exp(st - top)
        p = (e * (1.0 / jnp.sum(e, axis=0, keepdims=True))).astype(bf16)
        p_ref[0, hh] = p
        c = dot(p, v, ((0,), (0,)))
        joined = c if joined is None else jnp.where(mine, c, joined)
    c_ref[0] = joined.astype(bf16)


def attend(covers, shard, shards, gathered, place, x, bias, old):
    length, width = x.shape
    cols = gathered.dims[-1]
    pairs = cols // (2 * HD)
    n_w = len(gathered.arrays)
    return pl.pallas_call(
        functools.partial(attend_body, shard, gathered),
        grid=(pairs,),
        out_shape=[
            jax.ShapeDtypeStruct((shards, length, 3 * cols), bf16),
            jax.ShapeDtypeStruct((shards, 2 * pairs, length, length), bf16),
            jax.ShapeDtypeStruct((shards, length, cols), bf16),
        ],
        in_specs=[SMEM, whole(x.shape), pl.BlockSpec((1, 3, 1, cols), lambda i: (max(shard - 1, 0), 0, 0, 0))]
        + [HBM] * (n_w + len(old)),
        out_specs=[
            pl.BlockSpec((1, length, 3 * cols), lambda i: (shard, 0, 0)),
            pl.BlockSpec((1, 2, length, length), lambda i: (shard, i, 0, 0)),
            pl.BlockSpec((1, length, 2 * HD), lambda i: (shard, 0, i)),
        ],
        input_output_aliases={3 + n_w + i: i for i in range(len(old))},
        scratch_shapes=gathered.scratch(1),
        compiler_params=params(),
        cost_estimate=cost(covers),
        name="attend",
    )(place, x, bias, *gathered.arrays, *old)


def norm_stats(values):
    center = values - jnp.mean(values, axis=-1, keepdims=True)
    inv = lax.rsqrt(jnp.mean(center * center, axis=-1, keepdims=True) + 1e-05)
    return center * inv, inv


def norm_back(grad, n, inv, gain):
    gn = grad * gain
    return (gn - jnp.mean(gn, -1, keepdims=True) - n * jnp.mean(gn * n, -1, keepdims=True)) * inv


def up_body(
    shards, g_out, g_up, place_ref, ctx_ref, x_ref, te_ref, b_ref, gain_ref, shift_ref, bias_ref, *refs
):
    n_out = len(g_out.arrays)
    out_refs = list(refs[:n_out])
    up_refs = [refs[n_out]] + list(refs[1:n_out])
    n1_ref, inv_ref, low_ref, act_ref, slope_ref, wo_full, wu_full = refs[n_out + 1 : n_out + 8]
    wo, o_sems, wu, u_sems, acc, keep_o, keep_u = refs[n_out + 8 :]
    s = pl.program_id(0)
    place = place_ref[0]
    length, width = acc.shape

    def keep_out(shard):
        return pltpu.make_async_copy(wo.at[shard], wo_full.at[shard], keep_o.at[shard])

    def keep_up(shard):
        return pltpu.make_async_copy(wu.at[shard], wu_full.at[shard], keep_u.at[shard])

    @pl.when(s == 0)
    def _():
        g_out.start_all(out_refs, place, wo, o_sems, shards)
        g_up.start_all(up_refs, place, wu, u_sems, shards)
        for shard in range(shards):
            g_out.wait(out_refs, place, wo, o_sems, shard)
            keep_out(shard).start()
            part = dot(ctx_ref[shard], wo[shard].reshape(-1, width), ((1,), (0,)))
            if shard == 0:
                acc[...] = part
            else:
                acc[...] += part

        def rows(at, _):
            start = x_ref[at, :].astype(f32) + te_ref[...]
            n1, inv = norm_stats(start + (acc[at, :] + b_ref[...]))
            n1_ref[at, :] = n1
            inv_ref[at, :] = jnp.broadcast_to(inv, (64, inv_ref.shape[1]))
            low_ref[at, :] = (n1 * gain_ref[...] + shift_ref[...]).astype(bf16)
            return 0

        over_rows(length, 64, rows, 0)

    g_up.wait(up_refs, place, wu, u_sems, s)
    keep_up(s).start()
    units = wu.shape[-1]
    for n in range(units // 256):
        span = slice(n * 256, (n + 1) * 256)
        u = dot(low_ref[...], wu[s, :, :, span].reshape(width, 256), ((1,), (0,)))
        u = u + bias_ref[0, :, span]
        phi = 0.5 + 0.5 * lax.erf(u * (2.0**-0.5))
        act_ref[0, :, span] = (u * phi).astype(bf16)
        slope_ref[0, :, span] = (
            phi + u * jnp.exp(-0.5 * u * u) * (2.0 * math.pi) ** -0.5
        ).astype(bf16)

    @pl.when(s == shards - 1)
    def _():
        for shard in range(shards):
            keep_out(shard).wait()
            keep_up(shard).wait()


def up_project(g_out, g_up, place, ctx, x, time_embed, b_out, gain, shift, bias):
    length, width = x.shape
    shards = ctx.shape[0]
    units = g_up.dims[-1]
    block = pl.BlockSpec((1, length, units), lambda s: (s, 0, 0))
    row = whole((1, width))
    return pl.pallas_call(
        functools.partial(up_body, shards, g_out, g_up),
        grid=(shards,),
        out_shape=[
            jax.ShapeDtypeStruct((length, width), f32),
            jax.ShapeDtypeStruct((length, 128), f32),
            jax.ShapeDtypeStruct((length, width), bf16),
            jax.ShapeDtypeStruct((shards, length, units), bf16),
            jax.ShapeDtypeStruct((shards, length, units), bf16),
            jax.ShapeDtypeStruct((shards,) + g_out.dims, bf16),
            jax.ShapeDtypeStruct((shards,) + g_up.dims, bf16),
        ],
        in_specs=[
            SMEM,
            whole(ctx.shape),
            whole(x.shape),
            row,
            row,
            row,
            row,
            pl.BlockSpec((1, 1, units), lambda s: (s, 0, 0)),
        ]
        + [HBM] * (len(g_out.arrays) + 1),
        out_specs=[
            whole((length, width)),
            whole((length, 128)),
            whole((length, width)),
            block,
            block,
            HBM,
            HBM,
        ],
        scratch_shapes=g_out.scratch(shards)
        + g_up.scratch(shards)
        + [pltpu.VMEM((length, width), f32)]
        + [pltpu.SemaphoreType.DMA((shards,))] * 2,
        compiler_params=params(),
        cost_estimate=cost(40),
        name="up_project",
    )(place, ctx, x, time_embed, b_out, gain, shift, bias, *g_out.arrays, g_up.arrays[0])


def down_body(
    shards, gathered, place_ref, live_ref, act_ref, b_ref, gain1_ref, shift1_ref, gain2_ref, shift2_ref,
    n1_hbm, cot_hbm, *refs
):
    n = len(gathered.arrays)
    w_refs, (out_ref, gs_ref, bg_ref, sums_ref, w_full) = refs[:n], refs[n : n + 5]
    w, sems, acc, n1_ref, cot_ref, late, keep_sems = refs[n + 5 :]
    s = pl.program_id(0)
    place = place_ref[0]
    length, width = acc.shape

    def fetch(i):
        return pltpu.make_async_copy((n1_hbm, cot_hbm)[i], (n1_ref, cot_ref)[i], late.at[i])

    def keep(shard):
        return pltpu.make_async_copy(w.at[shard], w_full.at[shard], keep_sems.at[shard])

    @pl.when(s == 0)
    def _():
        gathered.start_all(w_refs, place, w, sems, shards)
        fetch(0).start()
        fetch(1).start()

    gathered.wait(w_refs, place, w, sems, s)
    keep(s).start()
    part = dot(act_ref[0], w[s].reshape(-1, width), ((1,), (0,)))

    @pl.when(s == 0)
    def _():
        acc[...] = part

    @pl.when(s > 0)
    def _():
        acc[...] += part

    @pl.when(s == shards - 1)
    def _():
        live = live_ref[0]
        fetch(0).wait()
        fetch(1).wait()

        def rows(at, sums):
            normed = n1_ref[at, :] * gain1_ref[...] + shift1_ref[...]
            n2, inv = norm_stats(normed + (acc[at, :] + b_ref[...]))
            out_ref[at, :] = (n2 * gain2_ref[...] + shift2_ref[...]).astype(bf16)
            grad = cot_ref[at, :].astype(f32) * live
            second = norm_back(grad, n2, inv, gain2_ref[...])
            gs_ref[at, :] = second
            low = second.astype(bf16)
            bg_ref[at, :] = low
            add = (low.astype(f32), grad * n2, grad)
            return tuple(a + row_sum(b) for a, b in zip(sums, add))

        zero = jnp.zeros((1, width), f32)
        sums = over_rows(length, 64, rows, (zero, zero, zero))
        for i, v in enumerate(sums):
            sums_ref[i : i + 1, :] = v
        for shard in range(shards):
            keep(shard).wait()


def down_project(gathered, place, live, act, n1, cot, b_down, gain1, shift1, gain2, shift2):
    shards, length, units = act.shape
    width = n1.shape[1]
    row = whole((1, width))
    return pl.pallas_call(
        functools.partial(down_body, shards, gathered),
        grid=(shards,),
        out_shape=[
            jax.ShapeDtypeStruct((length, width), bf16),
            jax.ShapeDtypeStruct((length, width), f32),
            jax.ShapeDtypeStruct((length, width), bf16),
            jax.ShapeDtypeStruct((3, width), f32),
            jax.ShapeDtypeStruct((shards,) + gathered.dims, bf16),
        ],
        in_specs=[SMEM, SMEM, pl.BlockSpec((1, length, units), lambda s: (s, 0, 0))]
        + [row] * 5
        + [HBM] * (2 + len(gathered.arrays)),
        out_specs=[whole((length, width))] * 3 + [whole((3, width)), HBM],
        scratch_shapes=gathered.scratch(shards)
        + [
            pltpu.VMEM((length, width), f32),
            pltpu.VMEM((length, width), f32),
            pltpu.VMEM((length, width), bf16),
            pltpu.SemaphoreType.DMA((2,)),
            pltpu.SemaphoreType.DMA((shards,)),
        ],
        compiler_params=params(),
        cost_estimate=cost(40),
        name="down_project",
    )(place, live, act, b_down, gain1, shift1, gain2, shift2, n1, cot, *gathered.arrays)


def up_back_body(
    shards, bg_ref, slope_ref, wd_ref, wu_ref, inv_ref, gain_ref, gs_hbm, n1_hbm,
    ug_ref, bias_ref, gf_ref, mg_ref, sums_ref, acc, gs_ref, n1_ref, late
):
    s = pl.program_id(0)
    length, width = acc.shape

    def fetch(i):
        return pltpu.make_async_copy((gs_hbm, n1_hbm)[i], (gs_ref, n1_ref)[i], late.at[i])

    @pl.when(s == 0)
    def _():
        fetch(0).start()
        fetch(1).start()

    units = ug_ref.shape[2]
    for n in range(units // 256):
        span = slice(n * 256, (n + 1) * 256)
        grad = dot(bg_ref[...], wd_ref[0, span, :], ((1,), (1,)))
        low = (grad * slope_ref[0, :, span].astype(f32)).astype(bf16)
        ug_ref[0, :, span] = low
        bias_ref[0, :, span] = row_sum(low.astype(f32))
    part = dot(ug_ref[0], wu_ref[0], ((1,), (1,)))

    @pl.when(s == 0)
    def _():
        acc[...] = part

    @pl.when(s > 0)
    def _():
        acc[...] += part

    @pl.when(s == shards - 1)
    def _():
        fetch(0).wait()
        fetch(1).wait()

        def rows(at, sums):
            n1, grad = n1_ref[at, :], acc[at, :] + gs_ref[at, :]
            first = norm_back(grad, n1, inv_ref[at, 0:1], gain_ref[...])
            gf_ref[at, :] = first
            low = first.astype(bf16)
            mg_ref[at, :] = low
            add = (low.astype(f32), grad * n1, grad)
            return tuple(a + row_sum(b) for a, b in zip(sums, add))

        zero = jnp.zeros((1, width), f32)
        sums = over_rows(length, 64, rows, (zero, zero, zero))
        for i, v in enumerate(sums):
            sums_ref[i : i + 1, :] = v


def up_back(w_down, w_up, bg, slope, gs, n1, inv, gain):
    shards, length, units = slope.shape
    width = n1.shape[1]
    block = pl.BlockSpec((1, length, units), lambda s: (s, 0, 0))
    return pl.pallas_call(
        functools.partial(up_back_body, shards),
        grid=(shards,),
        out_shape=[
            jax.ShapeDtypeStruct((shards, length, units), bf16),
            jax.ShapeDtypeStruct((shards, 1, units), f32),
            jax.ShapeDtypeStruct((length, width), f32),
            jax.ShapeDtypeStruct((length, width), bf16),
            jax.ShapeDtypeStruct((3, width), f32),
        ],
        in_specs=[
            whole(bg.shape),
            block,
            pl.BlockSpec((1, units, width), lambda s: (s, 0, 0)),
            pl.BlockSpec((1, width, units), lambda s: (s, 0, 0)),
            whole(inv.shape),
            whole((1, width)),
            HBM,
            HBM,
        ],
        out_specs=[
            block,
            pl.BlockSpec((1, 1, units), lambda s: (s, 0, 0)),
            whole((length, width)),
            whole((length, width)),
            whole((3, width)),
        ],
        scratch_shapes=[pltpu.VMEM((length, width), f32)] * 3 + [pltpu.SemaphoreType.DMA((2,))],
        compiler_params=params(),
        cost_estimate=cost(40),
        name="up_back",
    )(bg, slope, w_down, w_up, inv, gain, gs, n1)


def attend_back_body(mg_ref, wo_ref, qkv, p_of, *refs):
    pg_ref, bias_ref, cg = refs[-3:]
    pair = pl.program_id(1)
    cols = cg.shape[1]

    @pl.when(pair == 0)
    def _():
        cg[...] = dot(mg_ref[...], wo_ref[0], ((1,), (1,))).astype(bf16)

    at = pl.multiple_of(pair * 2 * HD, 2 * HD)
    q = qkv[0, :, pl.ds(at, 2 * HD)]
    k = qkv[0, :, pl.ds(cols + at, 2 * HD)]
    v = qkv[0, :, pl.ds(2 * cols + at, 2 * HD)]
    g = cg[:, pl.ds(at, 2 * HD)]
    lane = lax.broadcasted_iota(jnp.int32, q.shape, 1)
    dq = dk = dv = None
    for hh in range(2):
        mine = (lane // HD) == hh
        zero = jnp.zeros_like(q)
        gh = jnp.where(mine, g, zero)
        kh = jnp.where(mine, k, zero)
        qh = jnp.where(mine, q, zero)
        p = p_of[0, hh]
        dpt = dot(v, gh, ((1,), (1,)))
        pf = p.astype(f32)
        row = row_sum(pf * dpt)
        ds = (pf * (dpt - row)).astype(bf16)
        a = dot(p, gh, ((1,), (0,)))
        b = dot(ds, qh, ((1,), (0,)))
        c = dot(ds, kh, ((0,), (0,)))
        dv = a if dv is None else dv + a
        dk = b if dk is None else dk + b
        dq = c if dq is None else dq + c
    for c, g in enumerate((dq * 0.125, dk * 0.125, dv)):
        low = g.astype(bf16)
        pg_ref[0, :, pl.ds(c * cols + at, 2 * HD)] = low
        bias_ref[0, :, pl.ds(c * cols + at, 2 * HD)] = row_sum(low.astype(f32))


def attend_back(covers, base, count, w_out, mg, qkv, p, pg):
    length, width = mg.shape
    shards, cols = w_out.shape[:2]
    pairs = cols // (2 * HD)
    old = [] if pg is None else [pg]
    return pl.pallas_call(
        attend_back_body,
        grid=(count, pairs),
        out_shape=[
            jax.ShapeDtypeStruct((shards, length, 3 * cols), bf16),
            jax.ShapeDtypeStruct((count, 1, 3 * cols), f32),
        ],
        in_specs=[
            whole(mg.shape),
            pl.BlockSpec((1, cols, width), lambda s, i: (s + base, 0, 0)),
            pl.BlockSpec((1, length, 3 * cols), lambda s, i: (s + base, 0, 0)),
            pl.BlockSpec((1, 2, length, length), lambda s, i: (s + base, i, 0, 0)),
        ]
        + [HBM] * len(old),
        out_specs=[
            pl.BlockSpec((1, length, 3 * cols), lambda s, i: (s + base, 0, 0)),
            pl.BlockSpec((1, 1, 3 * cols), lambda s, i: (s, 0, 0)),
        ],
        input_output_aliases={4: 0} if old else {},
        scratch_shapes=[pltpu.VMEM((length, cols), bf16)],
        compiler_params=params(),
        cost_estimate=cost(covers),
        name="attend_back",
    )(mg, w_out, qkv, p, *old)


def input_back_body(shards, gathered, place_ref, pg_ref, gf_hbm, *refs):
    n = len(gathered.arrays)
    w_refs, (gt_ref, tg_ref, w, sems, acc, gf_ref, late) = refs[:n], refs[n:]
    s = pl.program_id(0)
    place = place_ref[0]
    cols = w.shape[-1]
    length, width = acc.shape
    fetch = pltpu.make_async_copy(gf_hbm, gf_ref, late.at[0])

    @pl.when(s == 0)
    def _():
        gathered.start_all(w_refs, place, w, sems, shards)
        fetch.start()
        acc[...] = jnp.zeros_like(acc)

    gathered.wait(w_refs, place, w, sems, s)
    part = None
    for c in range(3):
        new = dot(pg_ref[0, :, c * cols : (c + 1) * cols], w[s, c].reshape(width, cols), ((1,), (1,)))
        part = new if part is None else part + new
    acc[...] += part

    @pl.when(s == shards - 1)
    def _():
        fetch.wait()

        def rows(at, total):
            grad = acc[at, :] + gf_ref[at, :]
            gt_ref[at, :] = grad.astype(bf16)
            return total + row_sum(grad)

        tg_ref[...] = over_rows(length, 64, rows, jnp.zeros((1, width), f32))


def input_back(gathered, place, pg, gf):
    shards, length, cols3 = pg.shape
    width = gf.shape[1]
    return pl.pallas_call(
        functools.partial(input_back_body, shards, gathered),
        grid=(shards,),
        out_shape=[
            jax.ShapeDtypeStruct((length, width), bf16),
            jax.ShapeDtypeStruct((1, width), f32),
        ],
        in_specs=[SMEM, pl.BlockSpec((1, length, cols3), lambda s: (s, 0, 0)), HBM]
        + [HBM] * len(gathered.arrays),
        out_specs=[whole((length, width)), whole((1, width))],
        scratch_shapes=gathered.scratch(shards)
        + [pltpu.VMEM((length, width), f32)] * 2
        + [pltpu.SemaphoreType.DMA((1,))],
        compiler_params=params(),
        cost_estimate=cost(5),
        name="input_back",
    )(place, pg, gf, *gathered.arrays)


def weight_grad_body(n_pairs, place_ref, *refs):
    ins = refs[: 4 * n_pairs]
    keep_ref, send_ref = refs[4 * n_pairs : 4 * n_pairs + 2]
    turned = refs[4 * n_pairs + 2 :]
    place = place_ref[0]
    rows = keep_ref.shape[2]
    first, second = masks(place)

    @pl.when(pl.program_id(0) == 0)
    def _():
        for p in range(n_pairs):
            for core in range(2):
                feature_ref = ins[4 * p + core]
                length = feature_ref.shape[0]
                for j, mask in enumerate((0, second, first, 6)):
                    at = pl.multiple_of((place ^ mask) * rows, rows)
                    block = feature_ref[:, pl.ds(at, rows)]
                    turned[p][j * rows : (j + 1) * rows, core * length : (core + 1) * length] = block.T

    at = 0
    for p in range(n_pairs):
        b_ref, b2_ref = ins[4 * p + 2 : 4 * p + 4]
        length, cols = b_ref.shape[1:]
        for n in range(cols // 256):
            span = slice(n * 256, (n + 1) * 256)
            g = dot(turned[p][:, :length], b_ref[0, :, span], ((1,), (0,)))
            g += dot(turned[p][:, length:], b2_ref[0, :, span], ((1,), (0,)))
            g = g.astype(bf16)
            for i in range(2):
                keep_ref[i, 0, :, at : at + 256] = g[i * rows : (i + 1) * rows]
                send_ref[i, 0, :, at : at + 256] = g[(i + 2) * rows : (i + 3) * rows]
            at += 256


def weight_grad(covers, place, groups):
    shards, length, _ = groups[0][2].shape
    rows = groups[0][0].shape[1] // 8
    cols = sum(g[2].shape[2] for g in groups)
    specs, args, scratch = [], [], []
    for feature, feature2, b, b2 in groups:
        block = pl.BlockSpec((1,) + b.shape[1:], lambda s: (s, 0, 0))
        specs += [whole(feature.shape)] * 2 + [block] * 2
        args += [feature, feature2, b, b2]
        scratch.append(pltpu.VMEM((4 * rows, 2 * length), bf16))
    out = jax.ShapeDtypeStruct((2, shards, rows, cols), bf16)
    return pl.pallas_call(
        functools.partial(weight_grad_body, len(groups)),
        grid=(shards,),
        out_shape=[out] * 2,
        in_specs=[SMEM] + specs,
        out_specs=[pl.BlockSpec((2, 1, rows, cols), lambda s: (0, s, 0, 0))] * 2,
        scratch_shapes=scratch,
        compiler_params=params(),
        cost_estimate=cost(covers),
        name="weight_grad",
    )(place, *args)


def after(x, *deps):
    return lax.optimization_barrier((x, deps))[0]


def on_device(
    tokens,
    timesteps,
    buckets,
    counts,
    w_time,
    table,
    w_qkv,
    b_qv,
    w_out,
    b_out,
    gain1,
    shift1,
    w_up,
    b_up,
    w_down,
    b_down,
    gain2,
    shift2,
    cotangent,
):
    mpn = lax.axis_size("mp")
    dpn = lax.axis_size("dp")
    extra = dpn.bit_length() - 4
    me = lax.axis_index("dp")
    z = lax.axis_index("mp")
    q8 = me >> extra
    width = w_time.shape[0]
    positions, slots = tokens.shape[:2]
    length = positions * mpn
    head_cols = w_qkv.shape[2]
    units = w_up.shape[1]

    def exchange(x, partner):
        low = (1 << extra) - 1
        pairs = [(i, (partner(i >> extra) << extra) | (i & low)) for i in range(dpn)]
        return lax.ppermute(x, "dp", pairs)

    def cores(x):
        return exchange(x, lambda p: p ^ 1)

    def first_link(x):
        return exchange(x, lambda p: p ^ masks(p)[0])

    def second_link(x):
        return exchange(x, lambda p: p ^ masks(p)[1])

    def shift(x, s):
        return lax.ppermute(x, "mp", [(i, (i + s) % mpn) for i in range(mpn)])

    def at_item(x, s):
        return lax.dynamic_index_in_dim(x, lax.rem(z + s, mpn), 1, False)

    def to_items(x):
        return [at_item(x, 0)] + [shift(at_item(x, s), s) for s in range(1, mpn)]

    def to_positions(x):
        blocks = x.reshape(mpn, positions, width)
        return [blocks[0]] + [shift(blocks[s], -s) for s in range(1, mpn)]

    def in_item_order(parts):
        turned = jnp.concatenate([p[:, None] for p in parts] * 2, axis=1)
        return lax.dynamic_slice_in_dim(turned, lax.rem(mpn - z, mpn), mpn, 1)

    def split(shard, axis):
        dims = shard.shape
        return shard.reshape(dims[:axis] + (8, dims[axis] // 8) + dims[axis + 1 :])

    def eighth(shaped, axis):
        return lax.dynamic_index_in_dim(shaped, q8, axis, False)

    def along_z(part):
        return [shift(part, s) for s in range(1, mpn)]

    place = q8.astype(jnp.int32)[None]
    own_qkv, own_out, own_up, own_down = split(w_qkv, 1), split(w_out, 0), split(w_up, 0), split(w_down, 0)
    b_out, gain1, shift1, b_down, gain2, shift2 = [
        v[None] for v in (b_out, gain1, shift1, b_down, gain2, shift2)
    ]

    own_bias = jnp.stack([b_qv[0], jnp.zeros_like(b_qv[0]), b_qv[1]])[:, None]
    z_qkv = along_z(jnp.concatenate([eighth(own_qkv, 1), in_three(own_bias)], axis=1))
    part_up = jnp.concatenate([eighth(own_out, 0), eighth(own_up, 0), in_three(b_up[None])])
    part_down = eighth(own_down, 0)
    mine_qkv, far_bias = pack(1, after(z_qkv, part_up, part_down), own_qkv.shape[2])
    came_qkv = first_link(mine_qkv)
    z_up = along_z(after(part_up, mine_qkv))

    timesteps, buckets, counts = after((timesteps, buckets, counts), mine_qkv)
    total_live = jnp.sum(counts).astype(f32)
    weighting = 1.0 / total_live
    live = (z < lax.dynamic_index_in_dim(counts, me, 0, True)).astype(f32)
    my_step = lax.dynamic_index_in_dim(timesteps, z, 0, True)
    my_bucket = lax.dynamic_index_in_dim(buckets, z, 0, False)
    time_embed = embed(
        40,
        sinusoid(my_step.astype(f32), width), w_time, lax.dynamic_index_in_dim(table, my_bucket, 0, True)
    )
    held_qkv = pack(1, [mine_qkv, after(came_qkv, time_embed)])
    far_qkv = second_link(held_qkv)
    mine_up, far_up_bias = pack(1, after(z_up, held_qkv), own_out.shape[1] + own_up.shape[1])
    came_up = first_link(mine_up)
    x = to_items(after(tokens, mine_up))
    held2_qkv, far2_qkv = cores(held_qkv), cores(after(far_qkv, mine_up))
    g_qkv = Gathered(own_qkv, [held_qkv, far_qkv, held2_qkv, far2_qkv], 1, 0)
    held_up = pack(1, [mine_up, after(came_up, held2_qkv, far2_qkv)])
    far_up = second_link(held_up)
    x = jnp.concatenate(after(x, held_up))
    hidden = (x.astype(f32) + time_embed).astype(bf16)
    z_down = along_z(after(part_down, hidden))

    done = attend(10, 0, mpn, Gathered(own_qkv, [], 1, 0), place, hidden, own_bias[None], [])
    done = attend(10, 1, mpn, g_qkv, place, hidden, far_bias, done)
    held2_up, far2_up = cores(held_up), cores(after(far_up, done))
    done = attend(10, 2, mpn, g_qkv, place, after(hidden, held2_up, far2_up), far_bias, done)
    mine_down = pack(1, after(z_down, done))
    came_down = first_link(mine_down)
    cot = to_items(after(cotangent, mine_down))
    qkv, probs, ctx = attend(20, 3, mpn, g_qkv, place, after(hidden, mine_down), far_bias, done)
    held_down = pack(1, [mine_down, after(came_down, ctx)])
    far_down = second_link(held_down)
    ctx2, hidden2 = cores(after(ctx, held_down)), cores(after(hidden, held_down))
    up_pieces = [held_up, far_up, held2_up, far2_up]
    g_out = Gathered(own_out, up_pieces, 0, 0)
    g_up = Gathered(own_up, up_pieces, 0, own_out.shape[1])
    n1, inv1, normed_low, active, slope, full_out, full_up = up_project(
        g_out,
        g_up,
        place,
        after(ctx, held_down, ctx2, hidden2),
        x,
        time_embed,
        b_out,
        gain1,
        shift1,
        jnp.concatenate([b_up[None, None], far_up_bias]),
    )
    full_out = full_out.reshape(mpn, head_cols, width)
    full_up = full_up.reshape(mpn, width, units)
    held2_down, far2_down = cores(held_down), cores(after(far_down, normed_low))
    g_down = Gathered(own_down, [held_down, far_down, held2_down, far2_down], 0, 0)
    cot = jnp.concatenate(after(cot, normed_low))
    active2, low2 = cores(active), cores(normed_low)
    output, grad_second, branch_grad, sums2, full_down = down_project(
        g_down, place, live, active, n1, cot, b_down, gain1, shift1, gain2, shift2
    )
    full_down = full_down.reshape(mpn, units, width)

    def pass_on(keep, came):
        return (keep[1].astype(f32) + came[1].astype(f32)).astype(bf16)

    def send_home(keep, came, last):
        part = keep[0].astype(f32) + came[0].astype(f32) + last.astype(f32)
        sent = [part[s].astype(bf16) for s in range(1, mpn)]
        return [part[0]] + [shift(v, -s - 1) for s, v in enumerate(sent)], sent

    def finish(arrived):
        total = sum(a.astype(f32) for a in arrived)
        for t in reversed(range(extra)):
            half = total.shape[0] // 2
            bit = (me >> t) & 1
            keep = lax.dynamic_slice_in_dim(total, bit * half, half, 0)
            sent = lax.dynamic_slice_in_dim(total, (1 - bit) * half, half, 0)
            total = keep + lax.ppermute(sent, "dp", [(i, i ^ (1 << t)) for i in range(dpn)])
        return total * weighting

    devices = dpn * mpn
    both = ("dp", "mp")

    def in_order(parts):
        turned = jnp.stack([parts[-i % mpn] for i in range(mpn)] * 2)
        return lax.dynamic_slice_in_dim(turned, (mpn - z) % mpn, mpn, 0).reshape(-1)

    keep_d, send_d = weight_grad(20, place, [(branch_grad, cores(branch_grad), active, active2)])
    came_d = first_link(send_d)
    out_items = to_positions(after(output, keep_d))
    up_grad, bias_up, grad_first, mixing_grad, sums1 = up_back(
        full_down, full_up, after(branch_grad, keep_d, low2), slope, grad_second, n1, inv1, gain1
    )
    up_grad2, mixing_grad2 = cores(up_grad), cores(mixing_grad)
    pass_d = pass_on(keep_d, after(came_d, mixing_grad))
    last_d = second_link(pass_d)
    output = in_item_order(after(out_items, pass_d))
    pg, bias_near = attend_back(
        80, 0, mpn // 2, full_out, after(mixing_grad, pass_d, output), qkv, probs, None
    )
    keep_u, send_u = weight_grad(
        30, place, after([(normed_low, low2, up_grad, up_grad2), (mixing_grad, mixing_grad2, ctx, ctx2)], pg)
    )
    came_u = first_link(send_u)
    home_d, sent_d = send_home(keep_d, came_d, after(last_d, keep_u))
    pg, bias_far = attend_back(
        30, mpn // 2, mpn - mpn // 2, full_out, after(mixing_grad, sent_d), qkv, probs, pg
    )
    pg2 = cores(pg)
    grad_tokens, time_grad = input_back(g_qkv, place, pg, grad_first)
    grad_w_down = finish(after(home_d, grad_tokens)).T
    pass_u = pass_on(keep_u, after(came_u, grad_w_down))
    last_u = second_link(pass_u)
    back_items = to_positions(grad_tokens)
    bias_proj = jnp.concatenate([bias_near, bias_far])
    vectors = [
        in_order(bias_proj[:, 0, :head_cols]),
        in_order(bias_proj[:, 0, 2 * head_cols :]),
        sums1[0],
        sums1[1],
        sums1[2],
        sums2[0],
        sums2[1],
        sums2[2],
        in_order(bias_up[:, 0]),
        time_grad,
    ]
    facts = jnp.stack([my_step[0].astype(f32), my_bucket.astype(f32)])
    facts = jnp.broadcast_to(facts[None], (devices, 2))
    vectors = jnp.concatenate([facts] + [v.reshape(devices, -1) for v in vectors], axis=1)
    keep_q, send_q = weight_grad(20, place, after([(hidden, hidden2, pg, pg2)], pass_u))
    came_q = first_link(send_q)
    home_u, sent_u = send_home(keep_u, came_u, after(last_u, keep_q))
    gathered = lax.all_to_all(after(vectors, sent_u), both, 0, 0, tiled=True)
    per = width // devices
    grad_tokens = in_item_order(after(back_items, sent_u)).astype(f32)
    pass_q = pass_on(keep_q, after(came_q, grad_tokens))
    last_q = second_link(pass_q)
    up_and_out = finish(after(home_u, pass_q))
    grad_w_up = up_and_out[:, :units]
    grad_w_out = up_and_out[:, units:].T
    home_q, sent_q = send_home(keep_q, came_q, after(last_q, up_and_out))
    grad_w_qkv = finish(home_q).reshape(-1, 3, head_cols)
    grad_w_qkv = jnp.moveaxis(grad_w_qkv, 1, 0)

    gathered = after(gathered, pass_q)
    grads = gathered[:, -per:]
    summed = jnp.sum(gathered[:, 2:-per], axis=0) * weighting
    steps, rows_of = gathered[:, 0], gathered[:, 1]
    small = [summed[i * per : (i + 1) * per] for i in range(8)]
    grad_b_up = summed[8 * per :]
    high = lax.Precision.HIGHEST
    grad_w_time = (
        jnp.einsum("nd,ne->de", sinusoid(steps, width).astype(f32), grads, precision=high)
        * weighting
    )
    onehot = (rows_of[:, None] == jnp.arange(table.shape[0], dtype=f32)[None, :]).astype(f32)
    grad_table = jnp.einsum("nb,nd->bd", onehot, grads, precision=high) * weighting
    return (
        output,
        grad_tokens,
        grad_w_time,
        grad_table,
        grad_w_qkv,
        jnp.stack(small[:2]),
        grad_w_out,
        small[2],
        small[3],
        small[4],
        grad_w_up,
        grad_b_up,
        grad_w_down,
        small[5],
        small[6],
        small[7],
    )


def solution(mesh):
    return jax.shard_map(
        on_device,
        mesh=mesh,
        in_specs=(
            P("mp", "dp", None),
            P("dp"),
            P("dp"),
            P(),
            P(),
            P(),
            P(None, None, "mp"),
            P(None, "mp"),
            P("mp", None),
            P(),
            P(),
            P(),
            P(None, "mp"),
            P("mp"),
            P("mp", None),
            P(),
            P(),
            P(),
            P("mp", "dp", None),
        ),
        out_specs=(
            P("mp", "dp", None),
            P("mp", "dp", None),
            P(None, ("dp", "mp")),
            P(None, ("dp", "mp")),
            P(None, "dp", "mp"),
            P(None, ("dp", "mp")),
            P("mp", "dp"),
            P(("dp", "mp")),
            P(("dp", "mp")),
            P(("dp", "mp")),
            P("dp", "mp"),
            P(("dp", "mp")),
            P("mp", "dp"),
            P(("dp", "mp")),
            P(("dp", "mp")),
            P(("dp", "mp")),
        ),
        check_vma=False,
    )
```

```python
import functools
import math

import jax
import jax.numpy as jnp
from jax import lax
from jax.experimental import pallas as pl
from jax.experimental.pallas import tpu as pltpu
from jax.sharding import PartitionSpec as P

HD = 64
f32 = jnp.float32
bf16 = jnp.bfloat16
VMEM_LIMIT = 56 * 2**20


def params(**more):
    return pltpu.CompilerParams(vmem_limit_bytes=VMEM_LIMIT, **more)


def dot(a, b, dims):
    return lax.dot_general(a, b, (dims, ((), ())), preferred_element_type=f32)


def sinusoid(steps, model_width):
    half_width = model_width // 2
    freqs = jnp.exp(-math.log(10000.0) * jnp.arange(half_width, dtype=f32) / half_width)
    angles = steps[:, None] * freqs[None, :]
    return jnp.concatenate([jnp.sin(angles), jnp.cos(angles)], axis=-1).astype(bf16)


def masks(place):
    first = 2 + 2 * (place & 1)
    return first, 6 - first


class Gathered:
    def __init__(self, own, pieces, lead, start):
        self.arrays = [own] + pieces
        self.lead = lead
        self.start = start
        self.dims = own.shape

    def scratch(self, shards):
        return [pltpu.VMEM((shards,) + self.dims, bf16), pltpu.SemaphoreType.DMA((shards, 8))]

    def copies_of(self, refs, place, into, sems, shard, slot):
        if isinstance(shard, int) and shard == 0:
            return [pltpu.make_async_copy(refs[0], into.at[slot], sems.at[slot, 0])]
        lead = (slice(None),) * self.lead
        first, second = masks(place)
        held = (place, place ^ first)
        far = (place ^ second, place ^ 6)
        held2 = (place ^ 1, place ^ 1 ^ second)
        far2 = (place ^ 1 ^ first, place ^ 7)
        made = []
        for ref, chunks in zip(refs[1:], (held, far, held2, far2)):
            for i, chunk in enumerate(chunks):
                at = lead + (pl.ds(self.start, self.dims[-2]),)
                made.append(
                    pltpu.make_async_copy(
                        ref.at[i, shard - 1].at[at],
                        into.at[(slot,) + lead + (chunk,)],
                        sems.at[slot, len(made)],
                    )
                )
        return made

    def start_all(self, refs, place, into, sems, shards):
        for shard in range(shards):
            for copy in self.copies_of(refs, place, into, sems, shard, shard):
                copy.start()

    def wait(self, refs, place, into, sems, shard):
        @pl.when(shard == 0)
        def _():
            for copy in self.copies_of(refs, place, into, sems, 0, 0):
                copy.wait()

        @pl.when(shard > 0)
        def _():
            for copy in self.copies_of(refs, place, into, sems, shard, shard):
                copy.wait()


HBM = pl.BlockSpec(memory_space=pl.ANY)
SMEM = pl.BlockSpec(memory_space=pltpu.SMEM)


def whole(shape):
    return pl.BlockSpec(shape, lambda *_: (0,) * len(shape))


def cost(micros):
    return pl.CostEstimate(flops=int(micros * 1.15e9), transcendentals=0, bytes_accessed=0)


def over_rows(length, step, body, init):
    def one(i, carry):
        return body(pl.ds(pl.multiple_of(i * step, step), step), carry)

    return lax.fori_loop(0, length // step, one, init)


def row_sum(v):
    return jnp.sum(v, axis=0, keepdims=True)


def pack_body(rows, n, *refs):
    out_ref = refs[n]
    for i, ref in enumerate(refs[:n]):
        out_ref[i] = ref[..., :rows, :]
        if len(refs) > n + 1:
            total = ref[..., rows : rows + 1, :].astype(f32)
            for part in range(1, 3):
                total += ref[..., rows + part : rows + part + 1, :].astype(f32)
            refs[n + 1][i] = total


def pack(covers, parts, rows=None):
    dims = parts[0].shape
    n = len(parts)
    out = [(n,) + dims[:-2] + (rows or dims[-2], dims[-1])]
    if rows:
        out.append((n,) + dims[:-2] + (1, dims[-1]))
    made = pl.pallas_call(
        functools.partial(pack_body, rows or dims[-2], n),
        out_shape=[jax.ShapeDtypeStruct(o, t) for o, t in zip(out, (bf16, f32))],
        compiler_params=params(),
        cost_estimate=cost(covers),
        name="pack",
    )(*parts)
    return made if rows else made[0]


def in_three(v):
    parts = []
    for _ in range(3):
        parts.append(lax.reduce_precision(v, 8, 7))
        v = v - parts[-1]
    return jnp.concatenate(parts + [jnp.zeros_like(v)] * 5, axis=-2).astype(bf16)


def embed_body(sinus_ref, w_ref, row_ref, out_ref):
    out_ref[...] = dot(sinus_ref[...], w_ref[...], ((1,), (0,)))[:1] + row_ref[...]


def embed(covers, sinus, w, row):
    return pl.pallas_call(
        embed_body,
        out_shape=jax.ShapeDtypeStruct(row.shape, f32),
        compiler_params=params(),
        cost_estimate=cost(covers),
        name="embed",
    )(jnp.broadcast_to(sinus, (16,) + sinus.shape[1:]), w, row)


def attend_body(shard, gathered, place_ref, x_ref, bias_ref, *refs):
    n = len(gathered.arrays)
    w_refs = refs[:n]
    qkv_ref, p_ref, c_ref, w, sems = refs[-5:]
    pair = pl.program_id(0)
    place = place_ref[0]
    cols = w.shape[-1]

    @pl.when(pair == 0)
    def _():
        copies = gathered.copies_of(w_refs, place, w, sems, shard, 0)
        for copy in copies:
            copy.start()
        for copy in copies:
            copy.wait()
        for c in range(3):
            wide = w[0, c].reshape(x_ref.shape[1], cols)
            out = dot(x_ref[...], wide, ((1,), (0,))) + bias_ref[0, c]
            qkv_ref[0, :, c * cols : (c + 1) * cols] = out.astype(bf16)

    at = pl.multiple_of(pair * 2 * HD, 2 * HD)
    q = qkv_ref[0, :, pl.ds(at, 2 * HD)]
    k = qkv_ref[0, :, pl.ds(cols + at, 2 * HD)]
    v = qkv_ref[0, :, pl.ds(2 * cols + at, 2 * HD)]
    lane = lax.broadcasted_iota(jnp.int32, q.shape, 1)
    joined = None
    for hh in range(2):
        mine = (lane // HD) == hh
        kh = jnp.where(mine, k, jnp.zeros_like(k))
        st = dot(kh, q, ((1,), (1,))) * 0.125
        top = jnp.max(st, axis=0, keepdims=True)
        e = jnp.exp(st - top)
        p = (e * (1.0 / jnp.sum(e, axis=0, keepdims=True))).astype(bf16)
        p_ref[0, hh] = p
        c = dot(p, v, ((0,), (0,)))
        joined = c if joined is None else jnp.where(mine, c, joined)
    c_ref[0] = joined.astype(bf16)


def attend(covers, shard, shards, gathered, place, x, bias, old):
    length, width = x.shape
    cols = gathered.dims[-1]
    pairs = cols // (2 * HD)
    n_w = len(gathered.arrays)
    return pl.pallas_call(
        functools.partial(attend_body, shard, gathered),
        grid=(pairs,),
        out_shape=[
            jax.ShapeDtypeStruct((shards, length, 3 * cols), bf16),
            jax.ShapeDtypeStruct((shards, 2 * pairs, length, length), bf16),
            jax.ShapeDtypeStruct((shards, length, cols), bf16),
        ],
        in_specs=[SMEM, whole(x.shape), pl.BlockSpec((1, 3, 1, cols), lambda i: (max(shard - 1, 0), 0, 0, 0))]
        + [HBM] * (n_w + len(old)),
        out_specs=[
            pl.BlockSpec((1, length, 3 * cols), lambda i: (shard, 0, 0)),
            pl.BlockSpec((1, 2, length, length), lambda i: (shard, i, 0, 0)),
            pl.BlockSpec((1, length, 2 * HD), lambda i: (shard, 0, i)),
        ],
        input_output_aliases={3 + n_w + i: i for i in range(len(old))},
        scratch_shapes=gathered.scratch(1),
        compiler_params=params(),
        cost_estimate=cost(covers),
        name="attend",
    )(place, x, bias, *gathered.arrays, *old)


def norm_stats(values):
    center = values - jnp.mean(values, axis=-1, keepdims=True)
    inv = lax.rsqrt(jnp.mean(center * center, axis=-1, keepdims=True) + 1e-05)
    return center * inv, inv


def norm_back(grad, n, inv, gain):
    gn = grad * gain
    return (gn - jnp.mean(gn, -1, keepdims=True) - n * jnp.mean(gn * n, -1, keepdims=True)) * inv


def up_body(
    shards, g_out, g_up, place_ref, ctx_ref, x_ref, te_ref, b_ref, gain_ref, shift_ref, bias_ref, *refs
):
    n_out = len(g_out.arrays)
    out_refs = list(refs[:n_out])
    up_refs = [refs[n_out]] + list(refs[1:n_out])
    n1_ref, inv_ref, low_ref, act_ref, slope_ref, wo_full, wu_full = refs[n_out + 1 : n_out + 8]
    wo, o_sems, wu, u_sems, acc, keep_o, keep_u = refs[n_out + 8 :]
    s = pl.program_id(0)
    place = place_ref[0]
    length, width = acc.shape

    def keep_out(shard):
        return pltpu.make_async_copy(wo.at[shard], wo_full.at[shard], keep_o.at[shard])

    def keep_up(shard):
        return pltpu.make_async_copy(wu.at[shard], wu_full.at[shard], keep_u.at[shard])

    @pl.when(s == 0)
    def _():
        g_out.start_all(out_refs, place, wo, o_sems, shards)
        g_up.start_all(up_refs, place, wu, u_sems, shards)
        for shard in range(shards):
            g_out.wait(out_refs, place, wo, o_sems, shard)
            keep_out(shard).start()
            part = dot(ctx_ref[shard], wo[shard].reshape(-1, width), ((1,), (0,)))
            if shard == 0:
                acc[...] = part
            else:
                acc[...] += part

        def rows(at, _):
            start = x_ref[at, :].astype(f32) + te_ref[...]
            n1, inv = norm_stats(start + (acc[at, :] + b_ref[...]))
            n1_ref[at, :] = n1
            inv_ref[at, :] = jnp.broadcast_to(inv, (64, inv_ref.shape[1]))
            low_ref[at, :] = (n1 * gain_ref[...] + shift_ref[...]).astype(bf16)
            return 0

        over_rows(length, 64, rows, 0)

    g_up.wait(up_refs, place, wu, u_sems, s)
    keep_up(s).start()
    units = wu.shape[-1]
    for n in range(units // 256):
        span = slice(n * 256, (n + 1) * 256)
        u = dot(low_ref[...], wu[s, :, :, span].reshape(width, 256), ((1,), (0,)))
        u = u + bias_ref[0, :, span]
        phi = 0.5 + 0.5 * lax.erf(u * (2.0**-0.5))
        act_ref[0, :, span] = (u * phi).astype(bf16)
        slope_ref[0, :, span] = (
            phi + u * jnp.exp(-0.5 * u * u) * (2.0 * math.pi) ** -0.5
        ).astype(bf16)

    @pl.when(s == shards - 1)
    def _():
        for shard in range(shards):
            keep_out(shard).wait()
            keep_up(shard).wait()


def up_project(g_out, g_up, place, ctx, x, time_embed, b_out, gain, shift, bias):
    length, width = x.shape
    shards = ctx.shape[0]
    units = g_up.dims[-1]
    block = pl.BlockSpec((1, length, units), lambda s: (s, 0, 0))
    row = whole((1, width))
    return pl.pallas_call(
        functools.partial(up_body, shards, g_out, g_up),
        grid=(shards,),
        out_shape=[
            jax.ShapeDtypeStruct((length, width), f32),
            jax.ShapeDtypeStruct((length, 128), f32),
            jax.ShapeDtypeStruct((length, width), bf16),
            jax.ShapeDtypeStruct((shards, length, units), bf16),
            jax.ShapeDtypeStruct((shards, length, units), bf16),
            jax.ShapeDtypeStruct((shards,) + g_out.dims, bf16),
            jax.ShapeDtypeStruct((shards,) + g_up.dims, bf16),
        ],
        in_specs=[
            SMEM,
            whole(ctx.shape),
            whole(x.shape),
            row,
            row,
            row,
            row,
            pl.BlockSpec((1, 1, units), lambda s: (s, 0, 0)),
        ]
        + [HBM] * (len(g_out.arrays) + 1),
        out_specs=[
            whole((length, width)),
            whole((length, 128)),
            whole((length, width)),
            block,
            block,
            HBM,
            HBM,
        ],
        scratch_shapes=g_out.scratch(shards)
        + g_up.scratch(shards)
        + [pltpu.VMEM((length, width), f32)]
        + [pltpu.SemaphoreType.DMA((shards,))] * 2,
        compiler_params=params(),
        cost_estimate=cost(300),
        name="up_project",
    )(place, ctx, x, time_embed, b_out, gain, shift, bias, *g_out.arrays, g_up.arrays[0])


def down_body(
    shards, gathered, place_ref, live_ref, act_ref, b_ref, gain1_ref, shift1_ref, gain2_ref, shift2_ref,
    n1_hbm, cot_hbm, *refs
):
    n = len(gathered.arrays)
    w_refs, (out_ref, gs_ref, bg_ref, sums_ref, w_full) = refs[:n], refs[n : n + 5]
    w, sems, acc, n1_ref, cot_ref, late, keep_sems = refs[n + 5 :]
    s = pl.program_id(0)
    place = place_ref[0]
    length, width = acc.shape

    def fetch(i):
        return pltpu.make_async_copy((n1_hbm, cot_hbm)[i], (n1_ref, cot_ref)[i], late.at[i])

    def keep(shard):
        return pltpu.make_async_copy(w.at[shard], w_full.at[shard], keep_sems.at[shard])

    @pl.when(s == 0)
    def _():
        gathered.start_all(w_refs, place, w, sems, shards)
        fetch(0).start()
        fetch(1).start()

    gathered.wait(w_refs, place, w, sems, s)
    keep(s).start()
    part = dot(act_ref[0], w[s].reshape(-1, width), ((1,), (0,)))

    @pl.when(s == 0)
    def _():
        acc[...] = part

    @pl.when(s > 0)
    def _():
        acc[...] += part

    @pl.when(s == shards - 1)
    def _():
        live = live_ref[0]
        fetch(0).wait()
        fetch(1).wait()

        def rows(at, sums):
            normed = n1_ref[at, :] * gain1_ref[...] + shift1_ref[...]
            n2, inv = norm_stats(normed + (acc[at, :] + b_ref[...]))
            out_ref[at, :] = (n2 * gain2_ref[...] + shift2_ref[...]).astype(bf16)
            grad = cot_ref[at, :].astype(f32) * live
            second = norm_back(grad, n2, inv, gain2_ref[...])
            gs_ref[at, :] = second
            low = second.astype(bf16)
            bg_ref[at, :] = low
            add = (low.astype(f32), grad * n2, grad)
            return tuple(a + row_sum(b) for a, b in zip(sums, add))

        zero = jnp.zeros((1, width), f32)
        sums = over_rows(length, 64, rows, (zero, zero, zero))
        for i, v in enumerate(sums):
            sums_ref[i : i + 1, :] = v
        for shard in range(shards):
            keep(shard).wait()


def down_project(gathered, place, live, act, n1, cot, b_down, gain1, shift1, gain2, shift2):
    shards, length, units = act.shape
    width = n1.shape[1]
    row = whole((1, width))
    return pl.pallas_call(
        functools.partial(down_body, shards, gathered),
        grid=(shards,),
        out_shape=[
            jax.ShapeDtypeStruct((length, width), bf16),
            jax.ShapeDtypeStruct((length, width), f32),
            jax.ShapeDtypeStruct((length, width), bf16),
            jax.ShapeDtypeStruct((3, width), f32),
            jax.ShapeDtypeStruct((shards,) + gathered.dims, bf16),
        ],
        in_specs=[SMEM, SMEM, pl.BlockSpec((1, length, units), lambda s: (s, 0, 0))]
        + [row] * 5
        + [HBM] * (2 + len(gathered.arrays)),
        out_specs=[whole((length, width))] * 3 + [whole((3, width)), HBM],
        scratch_shapes=gathered.scratch(shards)
        + [
            pltpu.VMEM((length, width), f32),
            pltpu.VMEM((length, width), f32),
            pltpu.VMEM((length, width), bf16),
            pltpu.SemaphoreType.DMA((2,)),
            pltpu.SemaphoreType.DMA((shards,)),
        ],
        compiler_params=params(),
        cost_estimate=cost(300),
        name="down_project",
    )(place, live, act, b_down, gain1, shift1, gain2, shift2, n1, cot, *gathered.arrays)


def up_back_body(
    shards, bg_ref, slope_ref, wd_ref, wu_ref, inv_ref, gain_ref, gs_hbm, n1_hbm,
    ug_ref, bias_ref, gf_ref, mg_ref, sums_ref, acc, gs_ref, n1_ref, late
):
    s = pl.program_id(0)
    length, width = acc.shape

    def fetch(i):
        return pltpu.make_async_copy((gs_hbm, n1_hbm)[i], (gs_ref, n1_ref)[i], late.at[i])

    @pl.when(s == 0)
    def _():
        fetch(0).start()
        fetch(1).start()

    units = ug_ref.shape[2]
    for n in range(units // 256):
        span = slice(n * 256, (n + 1) * 256)
        grad = dot(bg_ref[...], wd_ref[0, span, :], ((1,), (1,)))
        low = (grad * slope_ref[0, :, span].astype(f32)).astype(bf16)
        ug_ref[0, :, span] = low
        bias_ref[0, :, span] = row_sum(low.astype(f32))
    part = dot(ug_ref[0], wu_ref[0], ((1,), (1,)))

    @pl.when(s == 0)
    def _():
        acc[...] = part

    @pl.when(s > 0)
    def _():
        acc[...] += part

    @pl.when(s == shards - 1)
    def _():
        fetch(0).wait()
        fetch(1).wait()

        def rows(at, sums):
            n1, grad = n1_ref[at, :], acc[at, :] + gs_ref[at, :]
            first = norm_back(grad, n1, inv_ref[at, 0:1], gain_ref[...])
            gf_ref[at, :] = first
            low = first.astype(bf16)
            mg_ref[at, :] = low
            add = (low.astype(f32), grad * n1, grad)
            return tuple(a + row_sum(b) for a, b in zip(sums, add))

        zero = jnp.zeros((1, width), f32)
        sums = over_rows(length, 64, rows, (zero, zero, zero))
        for i, v in enumerate(sums):
            sums_ref[i : i + 1, :] = v


def up_back(w_down, w_up, bg, slope, gs, n1, inv, gain):
    shards, length, units = slope.shape
    width = n1.shape[1]
    block = pl.BlockSpec((1, length, units), lambda s: (s, 0, 0))
    return pl.pallas_call(
        functools.partial(up_back_body, shards),
        grid=(shards,),
        out_shape=[
            jax.ShapeDtypeStruct((shards, length, units), bf16),
            jax.ShapeDtypeStruct((shards, 1, units), f32),
            jax.ShapeDtypeStruct((length, width), f32),
            jax.ShapeDtypeStruct((length, width), bf16),
            jax.ShapeDtypeStruct((3, width), f32),
        ],
        in_specs=[
            whole(bg.shape),
            block,
            pl.BlockSpec((1, units, width), lambda s: (s, 0, 0)),
            pl.BlockSpec((1, width, units), lambda s: (s, 0, 0)),
            whole(inv.shape),
            whole((1, width)),
            HBM,
            HBM,
        ],
        out_specs=[
            block,
            pl.BlockSpec((1, 1, units), lambda s: (s, 0, 0)),
            whole((length, width)),
            whole((length, width)),
            whole((3, width)),
        ],
        scratch_shapes=[pltpu.VMEM((length, width), f32)] * 3 + [pltpu.SemaphoreType.DMA((2,))],
        compiler_params=params(),
        cost_estimate=cost(300),
        name="up_back",
    )(bg, slope, w_down, w_up, inv, gain, gs, n1)


def attend_back_body(mg_ref, wo_ref, qkv, p_of, *refs):
    pg_ref, bias_ref, cg = refs[-3:]
    pair = pl.program_id(1)
    cols = cg.shape[1]

    @pl.when(pair == 0)
    def _():
        cg[...] = dot(mg_ref[...], wo_ref[0], ((1,), (1,))).astype(bf16)

    at = pl.multiple_of(pair * 2 * HD, 2 * HD)
    q = qkv[0, :, pl.ds(at, 2 * HD)]
    k = qkv[0, :, pl.ds(cols + at, 2 * HD)]
    v = qkv[0, :, pl.ds(2 * cols + at, 2 * HD)]
    g = cg[:, pl.ds(at, 2 * HD)]
    lane = lax.broadcasted_iota(jnp.int32, q.shape, 1)
    dq = dk = dv = None
    for hh in range(2):
        mine = (lane // HD) == hh
        zero = jnp.zeros_like(q)
        gh = jnp.where(mine, g, zero)
        kh = jnp.where(mine, k, zero)
        qh = jnp.where(mine, q, zero)
        p = p_of[0, hh]
        dpt = dot(v, gh, ((1,), (1,)))
        pf = p.astype(f32)
        row = row_sum(pf * dpt)
        ds = (pf * (dpt - row)).astype(bf16)
        a = dot(p, gh, ((1,), (0,)))
        b = dot(ds, qh, ((1,), (0,)))
        c = dot(ds, kh, ((0,), (0,)))
        dv = a if dv is None else dv + a
        dk = b if dk is None else dk + b
        dq = c if dq is None else dq + c
    for c, g in enumerate((dq * 0.125, dk * 0.125, dv)):
        low = g.astype(bf16)
        pg_ref[0, :, pl.ds(c * cols + at, 2 * HD)] = low
        bias_ref[0, :, pl.ds(c * cols + at, 2 * HD)] = row_sum(low.astype(f32))


def attend_back(covers, base, count, w_out, mg, qkv, p, pg):
    length, width = mg.shape
    shards, cols = w_out.shape[:2]
    pairs = cols // (2 * HD)
    old = [] if pg is None else [pg]
    return pl.pallas_call(
        attend_back_body,
        grid=(count, pairs),
        out_shape=[
            jax.ShapeDtypeStruct((shards, length, 3 * cols), bf16),
            jax.ShapeDtypeStruct((count, 1, 3 * cols), f32),
        ],
        in_specs=[
            whole(mg.shape),
            pl.BlockSpec((1, cols, width), lambda s, i: (s + base, 0, 0)),
            pl.BlockSpec((1, length, 3 * cols), lambda s, i: (s + base, 0, 0)),
            pl.BlockSpec((1, 2, length, length), lambda s, i: (s + base, i, 0, 0)),
        ]
        + [HBM] * len(old),
        out_specs=[
            pl.BlockSpec((1, length, 3 * cols), lambda s, i: (s + base, 0, 0)),
            pl.BlockSpec((1, 1, 3 * cols), lambda s, i: (s, 0, 0)),
        ],
        input_output_aliases={4: 0} if old else {},
        scratch_shapes=[pltpu.VMEM((length, cols), bf16)],
        compiler_params=params(),
        cost_estimate=cost(covers),
        name="attend_back",
    )(mg, w_out, qkv, p, *old)


def input_back_body(shards, gathered, place_ref, pg_ref, gf_hbm, *refs):
    n = len(gathered.arrays)
    w_refs, (gt_ref, tg_ref, w, sems, acc, gf_ref, late) = refs[:n], refs[n:]
    s = pl.program_id(0)
    place = place_ref[0]
    cols = w.shape[-1]
    length, width = acc.shape
    fetch = pltpu.make_async_copy(gf_hbm, gf_ref, late.at[0])

    @pl.when(s == 0)
    def _():
        gathered.start_all(w_refs, place, w, sems, shards)
        fetch.start()
        acc[...] = jnp.zeros_like(acc)

    gathered.wait(w_refs, place, w, sems, s)
    part = None
    for c in range(3):
        new = dot(pg_ref[0, :, c * cols : (c + 1) * cols], w[s, c].reshape(width, cols), ((1,), (1,)))
        part = new if part is None else part + new
    acc[...] += part

    @pl.when(s == shards - 1)
    def _():
        fetch.wait()

        def rows(at, total):
            grad = acc[at, :] + gf_ref[at, :]
            gt_ref[at, :] = grad.astype(bf16)
            return total + row_sum(grad)

        tg_ref[...] = over_rows(length, 64, rows, jnp.zeros((1, width), f32))


def input_back(gathered, place, pg, gf):
    shards, length, cols3 = pg.shape
    width = gf.shape[1]
    return pl.pallas_call(
        functools.partial(input_back_body, shards, gathered),
        grid=(shards,),
        out_shape=[
            jax.ShapeDtypeStruct((length, width), bf16),
            jax.ShapeDtypeStruct((1, width), f32),
        ],
        in_specs=[SMEM, pl.BlockSpec((1, length, cols3), lambda s: (s, 0, 0)), HBM]
        + [HBM] * len(gathered.arrays),
        out_specs=[whole((length, width)), whole((1, width))],
        scratch_shapes=gathered.scratch(shards)
        + [pltpu.VMEM((length, width), f32)] * 2
        + [pltpu.SemaphoreType.DMA((1,))],
        compiler_params=params(),
        cost_estimate=cost(1),
        name="input_back",
    )(place, pg, gf, *gathered.arrays)


def weight_grad_body(n_pairs, place_ref, *refs):
    ins = refs[: 4 * n_pairs]
    keep_ref, send_ref = refs[4 * n_pairs : 4 * n_pairs + 2]
    turned = refs[4 * n_pairs + 2 :]
    place = place_ref[0]
    rows = keep_ref.shape[2]
    first, second = masks(place)

    @pl.when(pl.program_id(0) == 0)
    def _():
        for p in range(n_pairs):
            for core in range(2):
                feature_ref = ins[4 * p + core]
                length = feature_ref.shape[0]
                for j, mask in enumerate((0, second, first, 6)):
                    at = pl.multiple_of((place ^ mask) * rows, rows)
                    block = feature_ref[:, pl.ds(at, rows)]
                    turned[p][j * rows : (j + 1) * rows, core * length : (core + 1) * length] = block.T

    at = 0
    for p in range(n_pairs):
        b_ref, b2_ref = ins[4 * p + 2 : 4 * p + 4]
        length, cols = b_ref.shape[1:]
        for n in range(cols // 256):
            span = slice(n * 256, (n + 1) * 256)
            g = dot(turned[p][:, :length], b_ref[0, :, span], ((1,), (0,)))
            g += dot(turned[p][:, length:], b2_ref[0, :, span], ((1,), (0,)))
            g = g.astype(bf16)
            for i in range(2):
                keep_ref[i, 0, :, at : at + 256] = g[i * rows : (i + 1) * rows]
                send_ref[i, 0, :, at : at + 256] = g[(i + 2) * rows : (i + 3) * rows]
            at += 256


def weight_grad(covers, place, groups):
    shards, length, _ = groups[0][2].shape
    rows = groups[0][0].shape[1] // 8
    cols = sum(g[2].shape[2] for g in groups)
    specs, args, scratch = [], [], []
    for feature, feature2, b, b2 in groups:
        block = pl.BlockSpec((1,) + b.shape[1:], lambda s: (s, 0, 0))
        specs += [whole(feature.shape)] * 2 + [block] * 2
        args += [feature, feature2, b, b2]
        scratch.append(pltpu.VMEM((4 * rows, 2 * length), bf16))
    out = jax.ShapeDtypeStruct((2, shards, rows, cols), bf16)
    return pl.pallas_call(
        functools.partial(weight_grad_body, len(groups)),
        grid=(shards,),
        out_shape=[out] * 2,
        in_specs=[SMEM] + specs,
        out_specs=[pl.BlockSpec((2, 1, rows, cols), lambda s: (0, s, 0, 0))] * 2,
        scratch_shapes=scratch,
        compiler_params=params(),
        cost_estimate=cost(covers),
        name="weight_grad",
    )(place, *args)


def pass_on_body(keep_ref, came_ref, out_ref):
    out_ref[0] = (keep_ref[0, 0].astype(f32) + came_ref[0, 0].astype(f32)).astype(bf16)


def pass_on(keep, came):
    _, shards, rows, cols = keep.shape
    half = pl.BlockSpec((1, 1, rows, cols), lambda s: (1, s, 0, 0))
    return pl.pallas_call(
        pass_on_body,
        grid=(shards,),
        out_shape=jax.ShapeDtypeStruct((shards, rows, cols), bf16),
        in_specs=[half, half],
        out_specs=pl.BlockSpec((1, rows, cols), lambda s: (s, 0, 0)),
        compiler_params=params(),
        cost_estimate=cost(300),
        name="pass_on",
    )(keep, came)


def gather_up_body(keep_ref, came_ref, last_ref, own_ref, *out_refs):
    s = pl.program_id(0)
    part = keep_ref[0, 0].astype(f32) + came_ref[0, 0].astype(f32) + last_ref[0].astype(f32)

    @pl.when(s == 0)
    def _():
        own_ref[...] = part

    for i, ref in enumerate(out_refs):

        @pl.when(s == i + 1)
        def _():
            ref[...] = part.astype(bf16)


def gather_up(covers, keep, came, last):
    _, shards, rows, cols = keep.shape
    half = pl.BlockSpec((1, 1, rows, cols), lambda s: (0, s, 0, 0))
    out = pl.BlockSpec((rows, cols), lambda s: (0, 0))
    return pl.pallas_call(
        gather_up_body,
        grid=(shards,),
        out_shape=[jax.ShapeDtypeStruct((rows, cols), f32)]
        + [jax.ShapeDtypeStruct((rows, cols), bf16)] * (shards - 1),
        in_specs=[half, half, pl.BlockSpec((1, rows, cols), lambda s: (s, 0, 0))],
        out_specs=[out] * shards,
        compiler_params=params(),
        cost_estimate=cost(covers),
        name="gather_up",
    )(keep, came, last)


def finish_body(pieces, scale_ref, *refs):
    n = len(refs) - len(pieces)
    total = refs[0][...]
    for ref in refs[1:n]:
        total += ref[...].astype(f32)
    total *= scale_ref[0]
    for ref, (kind, low, high) in zip(refs[n:], pieces):
        part = total[:, low:high]
        if kind == "turned":
            ref[...] = part.T
        elif kind == "plain":
            ref[...] = part
        else:
            cols = ref.shape[2]
            for c in range(ref.shape[0]):
                ref[c] = part[:, c * cols : (c + 1) * cols]


def finish_all(scale, parts, pieces):
    rows = parts[0].shape[0]
    shapes = []
    for kind, low, high in pieces:
        cols = high - low
        shapes.append({"turned": (cols, rows), "plain": (rows, cols), "three": (3, rows, cols // 3)}[kind])
    return pl.pallas_call(
        functools.partial(finish_body, pieces),
        out_shape=[jax.ShapeDtypeStruct(v, f32) for v in shapes],
        in_specs=[SMEM] + [pl.BlockSpec(memory_space=pltpu.VMEM)] * len(parts),
        compiler_params=params(),
        cost_estimate=cost(300),
        name="finish",
    )(scale, *parts)


def after(x, *deps):
    return lax.optimization_barrier((x, deps))[0]


def on_device(
    tokens,
    timesteps,
    buckets,
    counts,
    w_time,
    table,
    w_qkv,
    b_qv,
    w_out,
    b_out,
    gain1,
    shift1,
    w_up,
    b_up,
    w_down,
    b_down,
    gain2,
    shift2,
    cotangent,
):
    mpn = lax.axis_size("mp")
    dpn = lax.axis_size("dp")
    extra = dpn.bit_length() - 4
    me = lax.axis_index("dp")
    z = lax.axis_index("mp")
    q8 = me >> extra
    width = w_time.shape[0]
    positions, slots = tokens.shape[:2]
    length = positions * mpn
    head_cols = w_qkv.shape[2]
    units = w_up.shape[1]

    def exchange(x, partner):
        low = (1 << extra) - 1
        pairs = [(i, (partner(i >> extra) << extra) | (i & low)) for i in range(dpn)]
        return lax.ppermute(x, "dp", pairs)

    def cores(x):
        return exchange(x, lambda p: p ^ 1)

    def first_link(x):
        return exchange(x, lambda p: p ^ masks(p)[0])

    def second_link(x):
        return exchange(x, lambda p: p ^ masks(p)[1])

    def shift(x, s):
        return lax.ppermute(x, "mp", [(i, (i + s) % mpn) for i in range(mpn)])

    def to_items(x):
        x = lax.all_to_all(jnp.moveaxis(x, 1, 0), "mp", 0, 0, tiled=False)
        return x.reshape(length, width)

    def to_positions(x):
        return lax.all_to_all(x.reshape(mpn, positions, width), "mp", 0, 0, tiled=False)

    def split(shard, axis):
        dims = shard.shape
        return shard.reshape(dims[:axis] + (8, dims[axis] // 8) + dims[axis + 1 :])

    def eighth(shaped, axis):
        return lax.dynamic_index_in_dim(shaped, q8, axis, False)

    def along_z(part):
        return [shift(part, s) for s in range(1, mpn)]

    place = q8.astype(jnp.int32)[None]
    own_qkv, own_out, own_up, own_down = split(w_qkv, 1), split(w_out, 0), split(w_up, 0), split(w_down, 0)
    b_out, gain1, shift1, b_down, gain2, shift2 = [
        v[None] for v in (b_out, gain1, shift1, b_down, gain2, shift2)
    ]

    own_bias = jnp.stack([b_qv[0], jnp.zeros_like(b_qv[0]), b_qv[1]])[:, None]
    z_qkv = along_z(jnp.concatenate([eighth(own_qkv, 1), in_three(own_bias)], axis=1))
    part_up = jnp.concatenate([eighth(own_out, 0), eighth(own_up, 0), in_three(b_up[None])])
    part_down = eighth(own_down, 0)
    mine_qkv, far_bias = pack(300, after(z_qkv, part_up, part_down), own_qkv.shape[2])
    came_qkv = first_link(mine_qkv)
    z_up = along_z(after(part_up, mine_qkv))

    x = to_items(after(tokens, mine_qkv))
    held_qkv = pack(300, [mine_qkv, came_qkv])
    far_qkv = second_link(held_qkv)
    held2_qkv = cores(held_qkv)
    mine_up, far_up_bias = pack(300, after(z_up, held_qkv), own_out.shape[1] + own_up.shape[1])
    came_up = first_link(mine_up)

    timesteps, buckets, counts = after((timesteps, buckets, counts), mine_up)
    total_live = jnp.sum(counts).astype(f32)
    weighting = 1.0 / total_live
    live = (z < lax.dynamic_index_in_dim(counts, me, 0, True)).astype(f32)
    my_step = lax.dynamic_index_in_dim(timesteps, z, 0, True)
    my_bucket = lax.dynamic_index_in_dim(buckets, z, 0, False)
    time_embed = embed(
        300,
        sinusoid(my_step.astype(f32), width), w_time, lax.dynamic_index_in_dim(table, my_bucket, 0, True)
    )

    far2_qkv = cores(after(far_qkv, mine_up))
    g_qkv = Gathered(own_qkv, [held_qkv, far_qkv, held2_qkv, far2_qkv], 1, 0)
    held_up = pack(300, [mine_up, after(came_up, far2_qkv, held2_qkv, time_embed)])
    far_up = second_link(held_up)
    held2_up = cores(held_up)
    x = after(x, held_up)
    hidden = (x.astype(f32) + time_embed).astype(bf16)
    z_down = along_z(after(part_down, hidden))

    done = attend(300, 0, mpn, Gathered(own_qkv, [], 1, 0), place, hidden, own_bias[None], [])
    done = attend(300, 1, mpn, g_qkv, place, after(hidden, held2_up), far_bias, done)
    far2_up = cores(after(far_up, done))
    done = attend(300, 2, mpn, g_qkv, place, hidden, far_bias, done)
    mine_down = pack(300, after(z_down, done, far2_up))
    came_down = first_link(mine_down)
    cot = to_items(after(cotangent, mine_down))
    qkv, probs, ctx = attend(300, 3, mpn, g_qkv, place, after(hidden, mine_down), far_bias, done)
    held_down = pack(300, [mine_down, after(came_down, ctx)])
    far_down = second_link(held_down)
    held2_down = cores(held_down)
    ctx2, hidden2 = cores(after(ctx, held_down)), cores(after(hidden, held_down))
    up_pieces = [held_up, far_up, held2_up, far2_up]
    g_out = Gathered(own_out, up_pieces, 0, 0)
    g_up = Gathered(own_up, up_pieces, 0, own_out.shape[1])
    n1, inv1, normed_low, active, slope, full_out, full_up = up_project(
        g_out,
        g_up,
        place,
        after(ctx, held_down),
        x,
        time_embed,
        b_out,
        gain1,
        shift1,
        jnp.concatenate([b_up[None, None], far_up_bias]),
    )
    full_out = full_out.reshape(mpn, head_cols, width)
    full_up = full_up.reshape(mpn, width, units)
    far2_down = cores(after(far_down, normed_low, held2_down, ctx2, hidden2))
    g_down = Gathered(own_down, [held_down, far_down, held2_down, far2_down], 0, 0)
    cot = after(cot, normed_low)
    active2 = cores(active)
    output, grad_second, branch_grad, sums2, full_down = down_project(
        g_down, place, live, active, n1, cot, b_down, gain1, shift1, gain2, shift2
    )
    full_down = full_down.reshape(mpn, units, width)

    def send_home(covers, keep, came, last):
        sums = gather_up(covers, keep, came, last)
        return [sums[0]] + [shift(v, -s - 1) for s, v in enumerate(sums[1:])], sums

    def finish(arrived, pieces):
        if extra == 0:
            return finish_all(weighting[None], arrived, pieces)
        total = sum(a.astype(f32) for a in arrived) * weighting
        for t in reversed(range(extra)):
            half = total.shape[0] // 2
            bit = (me >> t) & 1
            keep = lax.dynamic_slice_in_dim(total, bit * half, half, 0)
            sent = lax.dynamic_slice_in_dim(total, (1 - bit) * half, half, 0)
            total = keep + lax.ppermute(sent, "dp", [(i, i ^ (1 << t)) for i in range(dpn)])
        made = []
        for kind, low, high in pieces:
            part = total[:, low:high]
            if kind == "turned":
                part = part.T
            elif kind == "three":
                part = jnp.moveaxis(part.reshape(part.shape[0], 3, -1), 1, 0)
            made.append(part)
        return made

    devices = dpn * mpn
    both = ("dp", "mp")

    def in_order(parts):
        turned = jnp.stack([parts[-i % mpn] for i in range(mpn)] * 2)
        return lax.dynamic_slice_in_dim(turned, (mpn - z) % mpn, mpn, 0).reshape(-1)

    keep_d, send_d = weight_grad(300, place, [(branch_grad, cores(branch_grad), active, active2)])
    came_d = first_link(send_d)
    low2 = cores(after(normed_low, keep_d))
    up_grad, bias_up, grad_first, mixing_grad, sums1 = up_back(
        full_down, full_up, after(branch_grad, keep_d), slope, grad_second, n1, inv1, gain1
    )
    up_grad2, mixing_grad2 = cores(up_grad), cores(mixing_grad)
    pass_d = pass_on(keep_d, after(came_d, mixing_grad, low2))
    last_d = second_link(pass_d)
    out_items = to_positions(after(output, mixing_grad))
    keep_u, send_u = weight_grad(
        300,
        place,
        after([(normed_low, low2, up_grad, up_grad2), (mixing_grad, mixing_grad2, ctx, ctx2)], pass_d),
    )
    came_u = first_link(send_u)
    pg, bias_near = attend_back(300, 0, mpn // 2, full_out, after(mixing_grad, keep_u), qkv, probs, None)
    home_d, sent_d = send_home(1, keep_d, came_d, after(last_d, pg))
    pg, bias_far = attend_back(
        1, mpn // 2, mpn - mpn // 2, full_out, after(mixing_grad, sent_d, out_items), qkv, probs, pg
    )
    pg2 = cores(pg)
    grad_tokens, time_grad = input_back(g_qkv, place, pg, grad_first)
    pass_u = pass_on(keep_u, after(came_u, grad_tokens))
    last_u = second_link(pass_u)
    bias_proj = jnp.concatenate([bias_near, bias_far])
    vectors = [
        in_order(bias_proj[:, 0, :head_cols]),
        in_order(bias_proj[:, 0, 2 * head_cols :]),
        sums1[0],
        sums1[1],
        sums1[2],
        sums2[0],
        sums2[1],
        sums2[2],
        in_order(bias_up[:, 0]),
        time_grad,
    ]
    facts = jnp.stack([my_step[0].astype(f32), my_bucket.astype(f32)])
    facts = jnp.broadcast_to(facts[None], (devices, 2))
    vectors = jnp.concatenate([facts] + [v.reshape(devices, -1) for v in vectors], axis=1)
    back_items = to_positions(grad_tokens)
    keep_q, send_q = weight_grad(300, place, [(hidden, hidden2, after(pg, grad_tokens), pg2)])
    came_q = first_link(send_q)
    home_u, sent_u = send_home(300, keep_u, came_u, after(last_u, keep_q, home_d))
    pass_q = pass_on(keep_q, after(came_q, sent_u))
    last_q = second_link(pass_q)
    back_items = after(back_items, pass_q)
    gathered = lax.all_to_all(after(vectors, back_items), both, 0, 0, tiled=True)
    home_u = after(home_u, pass_q)
    (grad_w_down,) = finish(after(home_d, pass_q), [("turned", 0, units)])
    home_q, sent_q = send_home(300, keep_q, came_q, after(last_q, grad_w_down))
    grad_tokens = jnp.moveaxis(after(back_items, sent_q), 0, 1).astype(f32)
    output = jnp.moveaxis(after(out_items, sent_q), 0, 1)
    grad_w_up, grad_w_out = finish(
        after(home_u, sent_q), [("plain", 0, units), ("turned", units, units + head_cols)]
    )
    (grad_w_qkv,) = finish(home_q, [("three", 0, 3 * head_cols)])
    per = width // devices

    gathered = after(gathered, sent_q)
    grads = gathered[:, -per:]
    summed = jnp.sum(gathered[:, 2:-per], axis=0) * weighting
    steps, rows_of = gathered[:, 0], gathered[:, 1]
    small = [summed[i * per : (i + 1) * per] for i in range(8)]
    grad_b_up = summed[8 * per :]
    high = lax.Precision.HIGHEST
    grad_w_time = (
        jnp.einsum("nd,ne->de", sinusoid(steps, width).astype(f32), grads, precision=high)
        * weighting
    )
    onehot = (rows_of[:, None] == jnp.arange(table.shape[0], dtype=f32)[None, :]).astype(f32)
    grad_table = jnp.einsum("nb,nd->bd", onehot, grads, precision=high) * weighting
    return (
        output,
        grad_tokens,
        grad_w_time,
        grad_table,
        grad_w_qkv,
        jnp.stack(small[:2]),
        grad_w_out,
        small[2],
        small[3],
        small[4],
        grad_w_up,
        grad_b_up,
        grad_w_down,
        small[5],
        small[6],
        small[7],
    )


def solution(mesh):
    return jax.shard_map(
        on_device,
        mesh=mesh,
        in_specs=(
            P("mp", "dp", None),
            P("dp"),
            P("dp"),
            P(),
            P(),
            P(),
            P(None, None, "mp"),
            P(None, "mp"),
            P("mp", None),
            P(),
            P(),
            P(),
            P(None, "mp"),
            P("mp"),
            P("mp", None),
            P(),
            P(),
            P(),
            P("mp", "dp", None),
        ),
        out_specs=(
            P("mp", "dp", None),
            P("mp", "dp", None),
            P(None, ("dp", "mp")),
            P(None, ("dp", "mp")),
            P(None, "dp", "mp"),
            P(None, ("dp", "mp")),
            P("mp", "dp"),
            P(("dp", "mp")),
            P(("dp", "mp")),
            P(("dp", "mp")),
            P("dp", "mp"),
            P(("dp", "mp")),
            P("mp", "dp"),
            P(("dp", "mp")),
            P(("dp", "mp")),
            P(("dp", "mp")),
        ),
        check_vma=False,
    )
```

```python
import functools
import math

import jax
import jax.numpy as jnp
from jax import lax
from jax.experimental import pallas as pl
from jax.experimental.pallas import tpu as pltpu
from jax.sharding import PartitionSpec as P

HD = 64
f32 = jnp.float32
bf16 = jnp.bfloat16
VMEM_LIMIT = 56 * 2**20


def params(**more):
    return pltpu.CompilerParams(vmem_limit_bytes=VMEM_LIMIT, **more)


def dot(a, b, dims):
    return lax.dot_general(a, b, (dims, ((), ())), preferred_element_type=f32)


def sinusoid(steps, model_width):
    half_width = model_width // 2
    freqs = jnp.exp(-math.log(10000.0) * jnp.arange(half_width, dtype=f32) / half_width)
    angles = steps[:, None] * freqs[None, :]
    return jnp.concatenate([jnp.sin(angles), jnp.cos(angles)], axis=-1).astype(bf16)


def masks(place):
    first = 2 + 2 * (place & 1)
    return first, 6 - first


class Gathered:
    def __init__(self, own, pieces, lead, start):
        self.arrays = [own] + pieces
        self.lead = lead
        self.start = start
        self.dims = own.shape

    def scratch(self, shards):
        return [pltpu.VMEM((shards,) + self.dims, bf16), pltpu.SemaphoreType.DMA((shards, 8))]

    def copies_of(self, refs, place, into, sems, shard, slot):
        if isinstance(shard, int) and shard == 0:
            return [pltpu.make_async_copy(refs[0], into.at[slot], sems.at[slot, 0])]
        lead = (slice(None),) * self.lead
        first, second = masks(place)
        held = (place, place ^ first)
        far = (place ^ second, place ^ 6)
        held2 = (place ^ 1, place ^ 1 ^ second)
        far2 = (place ^ 1 ^ first, place ^ 7)
        made = []
        for ref, chunks in zip(refs[1:], (held, far, held2, far2)):
            for i, chunk in enumerate(chunks):
                at = lead + (pl.ds(self.start, self.dims[-2]),)
                made.append(
                    pltpu.make_async_copy(
                        ref.at[i, shard - 1].at[at],
                        into.at[(slot,) + lead + (chunk,)],
                        sems.at[slot, len(made)],
                    )
                )
        return made

    def start_all(self, refs, place, into, sems, shards):
        for shard in range(shards):
            for copy in self.copies_of(refs, place, into, sems, shard, shard):
                copy.start()

    def wait(self, refs, place, into, sems, shard):
        @pl.when(shard == 0)
        def _():
            for copy in self.copies_of(refs, place, into, sems, 0, 0):
                copy.wait()

        @pl.when(shard > 0)
        def _():
            for copy in self.copies_of(refs, place, into, sems, shard, shard):
                copy.wait()


HBM = pl.BlockSpec(memory_space=pl.ANY)
SMEM = pl.BlockSpec(memory_space=pltpu.SMEM)


def whole(shape):
    return pl.BlockSpec(shape, lambda *_: (0,) * len(shape))


def cost(micros):
    return pl.CostEstimate(flops=int(micros * 1.15e9), transcendentals=0, bytes_accessed=0)


def over_rows(length, step, body, init):
    def one(i, carry):
        return body(pl.ds(pl.multiple_of(i * step, step), step), carry)

    return lax.fori_loop(0, length // step, one, init)


def row_sum(v):
    return jnp.sum(v, axis=0, keepdims=True)


def pack_body(rows, n, *refs):
    out_ref = refs[n]
    for i, ref in enumerate(refs[:n]):
        out_ref[i] = ref[..., :rows, :]
        if len(refs) > n + 1:
            total = ref[..., rows : rows + 1, :].astype(f32)
            for part in range(1, 3):
                total += ref[..., rows + part : rows + part + 1, :].astype(f32)
            refs[n + 1][i] = total


def pack(covers, parts, rows=None):
    dims = parts[0].shape
    n = len(parts)
    out = [(n,) + dims[:-2] + (rows or dims[-2], dims[-1])]
    if rows:
        out.append((n,) + dims[:-2] + (1, dims[-1]))
    made = pl.pallas_call(
        functools.partial(pack_body, rows or dims[-2], n),
        out_shape=[jax.ShapeDtypeStruct(o, t) for o, t in zip(out, (bf16, f32))],
        compiler_params=params(),
        cost_estimate=cost(covers),
        name="pack",
    )(*parts)
    return made if rows else made[0]


def in_three(v):
    parts = []
    for _ in range(3):
        parts.append(lax.reduce_precision(v, 8, 7))
        v = v - parts[-1]
    return jnp.concatenate(parts + [jnp.zeros_like(v)] * 5, axis=-2).astype(bf16)


def embed_body(sinus_ref, w_ref, row_ref, out_ref):
    out_ref[...] = dot(sinus_ref[...], w_ref[...], ((1,), (0,)))[:1] + row_ref[...]


def embed(covers, sinus, w, row):
    return pl.pallas_call(
        embed_body,
        out_shape=jax.ShapeDtypeStruct(row.shape, f32),
        compiler_params=params(),
        cost_estimate=cost(covers),
        name="embed",
    )(jnp.broadcast_to(sinus, (16,) + sinus.shape[1:]), w, row)


def attend_body(shard, gathered, place_ref, x_ref, bias_ref, *refs):
    n = len(gathered.arrays)
    w_refs = refs[:n]
    qkv_ref, p_ref, c_ref, w, sems = refs[-5:]
    pair = pl.program_id(0)
    place = place_ref[0]
    cols = w.shape[-1]

    @pl.when(pair == 0)
    def _():
        copies = gathered.copies_of(w_refs, place, w, sems, shard, 0)
        for copy in copies:
            copy.start()
        for copy in copies:
            copy.wait()
        for c in range(3):
            wide = w[0, c].reshape(x_ref.shape[1], cols)
            out = dot(x_ref[...], wide, ((1,), (0,))) + bias_ref[0, c]
            qkv_ref[0, :, c * cols : (c + 1) * cols] = out.astype(bf16)

    at = pl.multiple_of(pair * 2 * HD, 2 * HD)
    q = qkv_ref[0, :, pl.ds(at, 2 * HD)]
    k = qkv_ref[0, :, pl.ds(cols + at, 2 * HD)]
    v = qkv_ref[0, :, pl.ds(2 * cols + at, 2 * HD)]
    lane = lax.broadcasted_iota(jnp.int32, q.shape, 1)
    joined = None
    for hh in range(2):
        mine = (lane // HD) == hh
        kh = jnp.where(mine, k, jnp.zeros_like(k))
        st = dot(kh, q, ((1,), (1,))) * 0.125
        top = jnp.max(st, axis=0, keepdims=True)
        e = jnp.exp(st - top)
        p = (e * (1.0 / jnp.sum(e, axis=0, keepdims=True))).astype(bf16)
        p_ref[0, hh] = p
        c = dot(p, v, ((0,), (0,)))
        joined = c if joined is None else jnp.where(mine, c, joined)
    c_ref[0] = joined.astype(bf16)


def attend(covers, shard, shards, gathered, place, x, bias, old):
    length, width = x.shape
    cols = gathered.dims[-1]
    pairs = cols // (2 * HD)
    n_w = len(gathered.arrays)
    return pl.pallas_call(
        functools.partial(attend_body, shard, gathered),
        grid=(pairs,),
        out_shape=[
            jax.ShapeDtypeStruct((shards, length, 3 * cols), bf16),
            jax.ShapeDtypeStruct((shards, 2 * pairs, length, length), bf16),
            jax.ShapeDtypeStruct((shards, length, cols), bf16),
        ],
        in_specs=[SMEM, whole(x.shape), pl.BlockSpec((1, 3, 1, cols), lambda i: (max(shard - 1, 0), 0, 0, 0))]
        + [HBM] * (n_w + len(old)),
        out_specs=[
            pl.BlockSpec((1, length, 3 * cols), lambda i: (shard, 0, 0)),
            pl.BlockSpec((1, 2, length, length), lambda i: (shard, i, 0, 0)),
            pl.BlockSpec((1, length, 2 * HD), lambda i: (shard, 0, i)),
        ],
        input_output_aliases={3 + n_w + i: i for i in range(len(old))},
        scratch_shapes=gathered.scratch(1),
        compiler_params=params(),
        cost_estimate=cost(covers),
        name="attend",
    )(place, x, bias, *gathered.arrays, *old)


def norm_stats(values):
    center = values - jnp.mean(values, axis=-1, keepdims=True)
    inv = lax.rsqrt(jnp.mean(center * center, axis=-1, keepdims=True) + 1e-05)
    return center * inv, inv


def norm_back(grad, n, inv, gain):
    gn = grad * gain
    return (gn - jnp.mean(gn, -1, keepdims=True) - n * jnp.mean(gn * n, -1, keepdims=True)) * inv


def up_body(
    shards, g_out, g_up, place_ref, ctx_ref, x_ref, te_ref, b_ref, gain_ref, shift_ref, bias_ref, *refs
):
    n_out = len(g_out.arrays)
    out_refs = list(refs[:n_out])
    up_refs = [refs[n_out]] + list(refs[1:n_out])
    n1_ref, inv_ref, low_ref, act_ref, slope_ref, wo_full = refs[n_out + 1 : n_out + 7]
    wo, o_sems, wu, u_sems, acc, keep_o = refs[n_out + 7 :]
    s = pl.program_id(0)
    place = place_ref[0]
    length, width = acc.shape

    def keep_out(shard):
        return pltpu.make_async_copy(wo.at[shard], wo_full.at[shard], keep_o.at[shard])

    @pl.when(s == 0)
    def _():
        g_out.start_all(out_refs, place, wo, o_sems, shards)
        g_up.start_all(up_refs, place, wu, u_sems, shards)
        for shard in range(shards):
            g_out.wait(out_refs, place, wo, o_sems, shard)
            keep_out(shard).start()
            part = dot(ctx_ref[shard], wo[shard].reshape(-1, width), ((1,), (0,)))
            if shard == 0:
                acc[...] = part
            else:
                acc[...] += part

        def rows(at, _):
            start = x_ref[at, :].astype(f32) + te_ref[...]
            n1, inv = norm_stats(start + (acc[at, :] + b_ref[...]))
            n1_ref[at, :] = n1
            inv_ref[at, :] = jnp.broadcast_to(inv, (64, inv_ref.shape[1]))
            low_ref[at, :] = (n1 * gain_ref[...] + shift_ref[...]).astype(bf16)
            return 0

        over_rows(length, 64, rows, 0)

    g_up.wait(up_refs, place, wu, u_sems, s)
    units = wu.shape[-1]
    for n in range(units // 256):
        span = slice(n * 256, (n + 1) * 256)
        u = dot(low_ref[...], wu[s, :, :, span].reshape(width, 256), ((1,), (0,)))
        u = u + bias_ref[0, :, span]
        phi = 0.5 + 0.5 * lax.erf(u * (2.0**-0.5))
        act_ref[0, :, span] = (u * phi).astype(bf16)
        slope_ref[0, :, span] = (
            phi + u * jnp.exp(-0.5 * u * u) * (2.0 * math.pi) ** -0.5
        ).astype(bf16)

    @pl.when(s == shards - 1)
    def _():
        for shard in range(shards):
            keep_out(shard).wait()


def up_project(g_out, g_up, place, ctx, x, time_embed, b_out, gain, shift, bias):
    length, width = x.shape
    shards = ctx.shape[0]
    units = g_up.dims[-1]
    block = pl.BlockSpec((1, length, units), lambda s: (s, 0, 0))
    row = whole((1, width))
    return pl.pallas_call(
        functools.partial(up_body, shards, g_out, g_up),
        grid=(shards,),
        out_shape=[
            jax.ShapeDtypeStruct((length, width), f32),
            jax.ShapeDtypeStruct((length, 128), f32),
            jax.ShapeDtypeStruct((length, width), bf16),
            jax.ShapeDtypeStruct((shards, length, units), bf16),
            jax.ShapeDtypeStruct((shards, length, units), bf16),
            jax.ShapeDtypeStruct((shards,) + g_out.dims, bf16),
        ],
        in_specs=[
            SMEM,
            whole(ctx.shape),
            whole(x.shape),
            row,
            row,
            row,
            row,
            pl.BlockSpec((1, 1, units), lambda s: (s, 0, 0)),
        ]
        + [HBM] * (len(g_out.arrays) + 1),
        out_specs=[
            whole((length, width)),
            whole((length, 128)),
            whole((length, width)),
            block,
            block,
            HBM,
        ],
        scratch_shapes=g_out.scratch(shards)
        + g_up.scratch(shards)
        + [pltpu.VMEM((length, width), f32)]
        + [pltpu.SemaphoreType.DMA((shards,))],
        compiler_params=params(),
        cost_estimate=cost(300),
        name="up_project",
    )(place, ctx, x, time_embed, b_out, gain, shift, bias, *g_out.arrays, g_up.arrays[0])


def down_body(
    shards, gathered, place_ref, live_ref, act_ref, b_ref, gain1_ref, shift1_ref, gain2_ref, shift2_ref,
    n1_hbm, cot_hbm, *refs
):
    n = len(gathered.arrays)
    w_refs, (out_hbm, bg_hbm, sums_ref) = refs[:n], refs[n : n + 3]
    w, sems, acc, n1_ref, cot_ref, late, out_ref, bg_ref, done = refs[n + 3 :]
    s = pl.program_id(0)
    place = place_ref[0]
    length, width = acc.shape

    def fetch(i):
        return pltpu.make_async_copy((n1_hbm, cot_hbm)[i], (n1_ref, cot_ref)[i], late.at[i])

    @pl.when(s == 0)
    def _():
        gathered.start_all(w_refs, place, w, sems, shards)
        fetch(0).start()
        fetch(1).start()

    gathered.wait(w_refs, place, w, sems, s)
    part = dot(act_ref[0], w[s].reshape(-1, width), ((1,), (0,)))

    @pl.when(s == 0)
    def _():
        acc[...] = part

    @pl.when(s > 0)
    def _():
        acc[...] += part

    @pl.when(s == shards - 1)
    def _():
        live = live_ref[0]
        fetch(0).wait()
        fetch(1).wait()

        def leave(i):
            at = pl.ds(i * 64, 64)
            return [
                pltpu.make_async_copy(out_ref.at[at], out_hbm.at[at], done.at[0, i]),
                pltpu.make_async_copy(bg_ref.at[at], bg_hbm.at[at], done.at[1, i]),
            ]

        def rows(i, sums):
            at = pl.ds(pl.multiple_of(i * 64, 64), 64)
            normed = n1_ref[at, :] * gain1_ref[...] + shift1_ref[...]
            n2, inv = norm_stats(normed + (acc[at, :] + b_ref[...]))
            out_ref[at, :] = (n2 * gain2_ref[...] + shift2_ref[...]).astype(bf16)
            grad = cot_ref[at, :].astype(f32) * live
            second = norm_back(grad, n2, inv, gain2_ref[...])
            low = second.astype(bf16)
            bg_ref[at, :] = low
            for copy in leave(i):
                copy.start()
            add = (low.astype(f32), grad * n2, grad)
            return tuple(a + row_sum(b) for a, b in zip(sums, add))

        zero = jnp.zeros((1, width), f32)
        sums = lax.fori_loop(0, length // 64, rows, (zero, zero, zero))
        for i, v in enumerate(sums):
            sums_ref[i : i + 1, :] = v
        for i in range(length // 64):
            for copy in leave(i):
                copy.wait()


def down_project(gathered, place, live, act, n1, cot, b_down, gain1, shift1, gain2, shift2):
    shards, length, units = act.shape
    width = n1.shape[1]
    row = whole((1, width))
    return pl.pallas_call(
        functools.partial(down_body, shards, gathered),
        grid=(shards,),
        out_shape=[
            jax.ShapeDtypeStruct((length, width), bf16),
            jax.ShapeDtypeStruct((length, width), bf16),
            jax.ShapeDtypeStruct((3, width), f32),
        ],
        in_specs=[SMEM, SMEM, pl.BlockSpec((1, length, units), lambda s: (s, 0, 0))]
        + [row] * 5
        + [HBM] * (2 + len(gathered.arrays)),
        out_specs=[HBM] * 2 + [whole((3, width))],
        scratch_shapes=gathered.scratch(shards)
        + [
            pltpu.VMEM((length, width), f32),
            pltpu.VMEM((length, width), f32),
            pltpu.VMEM((length, width), bf16),
            pltpu.SemaphoreType.DMA((2,)),
            pltpu.VMEM((length, width), bf16),
            pltpu.VMEM((length, width), bf16),
            pltpu.SemaphoreType.DMA((2, length // 64)),
        ],
        compiler_params=params(),
        cost_estimate=cost(300),
        name="down_project",
    )(place, live, act, b_down, gain1, shift1, gain2, shift2, n1, cot, *gathered.arrays)


def up_back_body(
    shards, g_down, g_up, place_ref, bg_ref, slope_ref, inv_ref, gain_ref, n1_hbm, *refs
):
    n = len(g_down.arrays)
    d_refs, u_refs = list(refs[:n]), [refs[n]] + list(refs[n + 1 : 2 * n])
    ug_ref, bias_ref, gf_ref, mg_ref, sums_ref = refs[2 * n : 2 * n + 5]
    wd, d_sems, wu, u_sems, acc, n1_ref, late = refs[2 * n + 5 :]
    s = pl.program_id(0)
    place = place_ref[0]
    length, width = acc.shape

    fetch = pltpu.make_async_copy(n1_hbm, n1_ref, late.at[0])

    @pl.when(s == 0)
    def _():
        for shard in range(shards):
            for copy in g_down.copies_of(d_refs, place, wd, d_sems, shard, shard):
                copy.start()
            for copy in g_up.copies_of(u_refs, place, wu, u_sems, shard, shard):
                copy.start()
        fetch.start()

    g_down.wait(d_refs, place, wd, d_sems, s)
    units = ug_ref.shape[2]
    for n in range(units // 256):
        span = slice(n * 256, (n + 1) * 256)
        rows = wd[s, 2 * n : 2 * n + 2].reshape(256, width)
        grad = dot(bg_ref[...], rows, ((1,), (1,)))
        low = (grad * slope_ref[0, :, span].astype(f32)).astype(bf16)
        ug_ref[0, :, span] = low
        bias_ref[0, :, span] = row_sum(low.astype(f32))
    g_up.wait(u_refs, place, wu, u_sems, s)
    part = dot(ug_ref[0], wu[s].reshape(width, units), ((1,), (1,)))

    @pl.when(s == 0)
    def _():
        acc[...] = part

    @pl.when(s > 0)
    def _():
        acc[...] += part

    @pl.when(s == shards - 1)
    def _():
        fetch.wait()

        def rows(at, sums):
            n1, grad = n1_ref[at, :], acc[at, :] + bg_ref[at, :].astype(f32)
            first = norm_back(grad, n1, inv_ref[at, 0:1], gain_ref[...])
            gf_ref[at, :] = first
            low = first.astype(bf16)
            mg_ref[at, :] = low
            add = (low.astype(f32), grad * n1, grad)
            return tuple(a + row_sum(b) for a, b in zip(sums, add))

        zero = jnp.zeros((1, width), f32)
        sums = over_rows(length, 64, rows, (zero, zero, zero))
        for i, v in enumerate(sums):
            sums_ref[i : i + 1, :] = v


def up_back(g_down, g_up, place, bg, slope, n1, inv, gain):
    shards, length, units = slope.shape
    width = n1.shape[1]
    block = pl.BlockSpec((1, length, units), lambda s: (s, 0, 0))
    return pl.pallas_call(
        functools.partial(up_back_body, shards, g_down, g_up),
        grid=(shards,),
        out_shape=[
            jax.ShapeDtypeStruct((shards, length, units), bf16),
            jax.ShapeDtypeStruct((shards, 1, units), f32),
            jax.ShapeDtypeStruct((length, width), f32),
            jax.ShapeDtypeStruct((length, width), bf16),
            jax.ShapeDtypeStruct((3, width), f32),
        ],
        in_specs=[SMEM, whole(bg.shape), block, whole(inv.shape), whole((1, width))]
        + [HBM] * (1 + len(g_down.arrays) + len(g_up.arrays)),
        out_specs=[
            block,
            pl.BlockSpec((1, 1, units), lambda s: (s, 0, 0)),
            whole((length, width)),
            whole((length, width)),
            whole((3, width)),
        ],
        scratch_shapes=g_down.scratch(shards)
        + g_up.scratch(shards)
        + [pltpu.VMEM((length, width), f32)] * 2
        + [pltpu.SemaphoreType.DMA((1,))],
        compiler_params=params(),
        cost_estimate=cost(300),
        name="up_back",
    )(place, bg, slope, inv, gain, n1, *g_down.arrays, *g_up.arrays)


def attend_back_body(mg_ref, wo_ref, qkv, p_of, *refs):
    pg_ref, bias_ref, cg = refs[-3:]
    pair = pl.program_id(1)
    cols = cg.shape[1]

    @pl.when(pair == 0)
    def _():
        cg[...] = dot(mg_ref[...], wo_ref[0], ((1,), (1,))).astype(bf16)

    at = pl.multiple_of(pair * 2 * HD, 2 * HD)
    q = qkv[0, :, pl.ds(at, 2 * HD)]
    k = qkv[0, :, pl.ds(cols + at, 2 * HD)]
    v = qkv[0, :, pl.ds(2 * cols + at, 2 * HD)]
    g = cg[:, pl.ds(at, 2 * HD)]
    lane = lax.broadcasted_iota(jnp.int32, q.shape, 1)
    dq = dk = dv = None
    for hh in range(2):
        mine = (lane // HD) == hh
        zero = jnp.zeros_like(q)
        gh = jnp.where(mine, g, zero)
        kh = jnp.where(mine, k, zero)
        qh = jnp.where(mine, q, zero)
        p = p_of[0, hh]
        dpt = dot(v, gh, ((1,), (1,)))
        pf = p.astype(f32)
        row = row_sum(pf * dpt)
        ds = (pf * (dpt - row)).astype(bf16)
        a = dot(p, gh, ((1,), (0,)))
        b = dot(ds, qh, ((1,), (0,)))
        c = dot(ds, kh, ((0,), (0,)))
        dv = a if dv is None else dv + a
        dk = b if dk is None else dk + b
        dq = c if dq is None else dq + c
    for c, g in enumerate((dq * 0.125, dk * 0.125, dv)):
        low = g.astype(bf16)
        pg_ref[0, :, pl.ds(c * cols + at, 2 * HD)] = low
        bias_ref[0, :, pl.ds(c * cols + at, 2 * HD)] = row_sum(low.astype(f32))


def attend_back(covers, base, count, w_out, mg, qkv, p, pg):
    length, width = mg.shape
    shards, cols = w_out.shape[:2]
    pairs = cols // (2 * HD)
    old = [] if pg is None else [pg]
    return pl.pallas_call(
        attend_back_body,
        grid=(count, pairs),
        out_shape=[
            jax.ShapeDtypeStruct((shards, length, 3 * cols), bf16),
            jax.ShapeDtypeStruct((count, 1, 3 * cols), f32),
        ],
        in_specs=[
            whole(mg.shape),
            pl.BlockSpec((1, cols, width), lambda s, i: (s + base, 0, 0)),
            pl.BlockSpec((1, length, 3 * cols), lambda s, i: (s + base, 0, 0)),
            pl.BlockSpec((1, 2, length, length), lambda s, i: (s + base, i, 0, 0)),
        ]
        + [HBM] * len(old),
        out_specs=[
            pl.BlockSpec((1, length, 3 * cols), lambda s, i: (s + base, 0, 0)),
            pl.BlockSpec((1, 1, 3 * cols), lambda s, i: (s, 0, 0)),
        ],
        input_output_aliases={4: 0} if old else {},
        scratch_shapes=[pltpu.VMEM((length, cols), bf16)],
        compiler_params=params(),
        cost_estimate=cost(covers),
        name="attend_back",
    )(mg, w_out, qkv, p, *old)


def input_back_body(shards, gathered, place_ref, pg_ref, gf_hbm, *refs):
    n = len(gathered.arrays)
    w_refs, (gt_ref, tg_ref, w, sems, acc, gf_ref, late) = refs[:n], refs[n:]
    s = pl.program_id(0)
    place = place_ref[0]
    cols = w.shape[-1]
    length, width = acc.shape
    fetch = pltpu.make_async_copy(gf_hbm, gf_ref, late.at[0])

    @pl.when(s == 0)
    def _():
        gathered.start_all(w_refs, place, w, sems, shards)
        fetch.start()
        acc[...] = jnp.zeros_like(acc)

    gathered.wait(w_refs, place, w, sems, s)
    part = None
    for c in range(3):
        new = dot(pg_ref[0, :, c * cols : (c + 1) * cols], w[s, c].reshape(width, cols), ((1,), (1,)))
        part = new if part is None else part + new
    acc[...] += part

    @pl.when(s == shards - 1)
    def _():
        fetch.wait()

        def rows(at, total):
            grad = acc[at, :] + gf_ref[at, :]
            gt_ref[at, :] = grad.astype(bf16)
            return total + row_sum(grad)

        tg_ref[...] = over_rows(length, 64, rows, jnp.zeros((1, width), f32))


def input_back(gathered, place, pg, gf):
    shards, length, cols3 = pg.shape
    width = gf.shape[1]
    return pl.pallas_call(
        functools.partial(input_back_body, shards, gathered),
        grid=(shards,),
        out_shape=[
            jax.ShapeDtypeStruct((length, width), bf16),
            jax.ShapeDtypeStruct((1, width), f32),
        ],
        in_specs=[SMEM, pl.BlockSpec((1, length, cols3), lambda s: (s, 0, 0)), HBM]
        + [HBM] * len(gathered.arrays),
        out_specs=[whole((length, width)), whole((1, width))],
        scratch_shapes=gathered.scratch(shards)
        + [pltpu.VMEM((length, width), f32)] * 2
        + [pltpu.SemaphoreType.DMA((1,))],
        compiler_params=params(),
        cost_estimate=cost(1),
        name="input_back",
    )(place, pg, gf, *gathered.arrays)


def weight_grad_body(n_pairs, place_ref, *refs):
    ins = refs[: 4 * n_pairs]
    keep_ref, send_ref = refs[4 * n_pairs : 4 * n_pairs + 2]
    turned = refs[4 * n_pairs + 2 :]
    place = place_ref[0]
    rows = keep_ref.shape[2]
    first, second = masks(place)

    @pl.when(pl.program_id(0) == 0)
    def _():
        for p in range(n_pairs):
            for core in range(2):
                feature_ref = ins[4 * p + core]
                length = feature_ref.shape[0]
                for j, mask in enumerate((0, second, first, 6)):
                    at = pl.multiple_of((place ^ mask) * rows, rows)
                    block = feature_ref[:, pl.ds(at, rows)]
                    turned[p][j * rows : (j + 1) * rows, core * length : (core + 1) * length] = block.T

    at = 0
    for p in range(n_pairs):
        b_ref, b2_ref = ins[4 * p + 2 : 4 * p + 4]
        length, cols = b_ref.shape[1:]
        for n in range(cols // 256):
            span = slice(n * 256, (n + 1) * 256)
            g = dot(turned[p][:, :length], b_ref[0, :, span], ((1,), (0,)))
            g += dot(turned[p][:, length:], b2_ref[0, :, span], ((1,), (0,)))
            g = g.astype(bf16)
            for i in range(2):
                keep_ref[i, 0, :, at : at + 256] = g[i * rows : (i + 1) * rows]
                send_ref[i, 0, :, at : at + 256] = g[(i + 2) * rows : (i + 3) * rows]
            at += 256


def weight_grad(covers, place, groups):
    shards, length, _ = groups[0][2].shape
    rows = groups[0][0].shape[1] // 8
    cols = sum(g[2].shape[2] for g in groups)
    specs, args, scratch = [], [], []
    for feature, feature2, b, b2 in groups:
        block = pl.BlockSpec((1,) + b.shape[1:], lambda s: (s, 0, 0))
        specs += [whole(feature.shape)] * 2 + [block] * 2
        args += [feature, feature2, b, b2]
        scratch.append(pltpu.VMEM((4 * rows, 2 * length), bf16))
    out = jax.ShapeDtypeStruct((2, shards, rows, cols), bf16)
    return pl.pallas_call(
        functools.partial(weight_grad_body, len(groups)),
        grid=(shards,),
        out_shape=[out] * 2,
        in_specs=[SMEM] + specs,
        out_specs=[pl.BlockSpec((2, 1, rows, cols), lambda s: (0, s, 0, 0))] * 2,
        scratch_shapes=scratch,
        compiler_params=params(),
        cost_estimate=cost(covers),
        name="weight_grad",
    )(place, *args)


def pass_on_body(keep_ref, came_ref, out_ref):
    out_ref[0] = (keep_ref[0, 0].astype(f32) + came_ref[0, 0].astype(f32)).astype(bf16)


def pass_on(keep, came):
    _, shards, rows, cols = keep.shape
    half = pl.BlockSpec((1, 1, rows, cols), lambda s: (1, s, 0, 0))
    return pl.pallas_call(
        pass_on_body,
        grid=(shards,),
        out_shape=jax.ShapeDtypeStruct((shards, rows, cols), bf16),
        in_specs=[half, half],
        out_specs=pl.BlockSpec((1, rows, cols), lambda s: (s, 0, 0)),
        compiler_params=params(),
        cost_estimate=cost(300),
        name="pass_on",
    )(keep, came)


def gather_up_body(keep_ref, came_ref, last_ref, own_ref, *out_refs):
    s = pl.program_id(0)
    part = keep_ref[0, 0].astype(f32) + came_ref[0, 0].astype(f32) + last_ref[0].astype(f32)

    @pl.when(s == 0)
    def _():
        own_ref[...] = part

    for i, ref in enumerate(out_refs):

        @pl.when(s == i + 1)
        def _():
            ref[...] = part.astype(bf16)


def gather_up(covers, keep, came, last):
    _, shards, rows, cols = keep.shape
    half = pl.BlockSpec((1, 1, rows, cols), lambda s: (0, s, 0, 0))
    out = pl.BlockSpec((rows, cols), lambda s: (0, 0))
    return pl.pallas_call(
        gather_up_body,
        grid=(shards,),
        out_shape=[jax.ShapeDtypeStruct((rows, cols), f32)]
        + [jax.ShapeDtypeStruct((rows, cols), bf16)] * (shards - 1),
        in_specs=[half, half, pl.BlockSpec((1, rows, cols), lambda s: (s, 0, 0))],
        out_specs=[out] * shards,
        compiler_params=params(),
        cost_estimate=cost(covers),
        name="gather_up",
    )(keep, came, last)


def finish_body(pieces, scale_ref, *refs):
    n = len(refs) - len(pieces)
    total = refs[0][...]
    for ref in refs[1:n]:
        total += ref[...].astype(f32)
    total *= scale_ref[0]
    for ref, (kind, low, high) in zip(refs[n:], pieces):
        part = total[:, low:high]
        if kind == "turned":
            ref[...] = part.T
        elif kind == "plain":
            ref[...] = part
        else:
            cols = ref.shape[2]
            for c in range(ref.shape[0]):
                ref[c] = part[:, c * cols : (c + 1) * cols]


def finish_all(scale, parts, pieces):
    rows = parts[0].shape[0]
    shapes = []
    for kind, low, high in pieces:
        cols = high - low
        shapes.append({"turned": (cols, rows), "plain": (rows, cols), "three": (3, rows, cols // 3)}[kind])
    return pl.pallas_call(
        functools.partial(finish_body, pieces),
        out_shape=[jax.ShapeDtypeStruct(v, f32) for v in shapes],
        in_specs=[SMEM] + [pl.BlockSpec(memory_space=pltpu.VMEM)] * len(parts),
        compiler_params=params(),
        cost_estimate=cost(300),
        name="finish",
    )(scale, *parts)


def after(x, *deps):
    return lax.optimization_barrier((x, deps))[0]


def on_device(
    tokens,
    timesteps,
    buckets,
    counts,
    w_time,
    table,
    w_qkv,
    b_qv,
    w_out,
    b_out,
    gain1,
    shift1,
    w_up,
    b_up,
    w_down,
    b_down,
    gain2,
    shift2,
    cotangent,
):
    mpn = lax.axis_size("mp")
    dpn = lax.axis_size("dp")
    extra = dpn.bit_length() - 4
    me = lax.axis_index("dp")
    z = lax.axis_index("mp")
    q8 = me >> extra
    width = w_time.shape[0]
    positions, slots = tokens.shape[:2]
    length = positions * mpn
    head_cols = w_qkv.shape[2]
    units = w_up.shape[1]

    def exchange(x, partner):
        low = (1 << extra) - 1
        pairs = [(i, (partner(i >> extra) << extra) | (i & low)) for i in range(dpn)]
        return lax.ppermute(x, "dp", pairs)

    def cores(x):
        return exchange(x, lambda p: p ^ 1)

    def first_link(x):
        return exchange(x, lambda p: p ^ masks(p)[0])

    def second_link(x):
        return exchange(x, lambda p: p ^ masks(p)[1])

    def shift(x, s):
        return lax.ppermute(x, "mp", [(i, (i + s) % mpn) for i in range(mpn)])

    def to_items(x):
        x = lax.all_to_all(jnp.moveaxis(x, 1, 0), "mp", 0, 0, tiled=False)
        return x.reshape(length, width)

    def to_positions(x):
        return lax.all_to_all(x.reshape(mpn, positions, width), "mp", 0, 0, tiled=False)

    def split(shard, axis):
        dims = shard.shape
        return shard.reshape(dims[:axis] + (8, dims[axis] // 8) + dims[axis + 1 :])

    def eighth(shaped, axis):
        return lax.dynamic_index_in_dim(shaped, q8, axis, False)

    def along_z(part):
        return [shift(part, s) for s in range(1, mpn)]

    place = q8.astype(jnp.int32)[None]
    own_qkv, own_out, own_up, own_down = split(w_qkv, 1), split(w_out, 0), split(w_up, 0), split(w_down, 0)
    b_out, gain1, shift1, b_down, gain2, shift2 = [
        v[None] for v in (b_out, gain1, shift1, b_down, gain2, shift2)
    ]

    own_bias = jnp.stack([b_qv[0], jnp.zeros_like(b_qv[0]), b_qv[1]])[:, None]
    z_qkv = along_z(jnp.concatenate([eighth(own_qkv, 1), in_three(own_bias)], axis=1))
    part_up = jnp.concatenate([eighth(own_out, 0), eighth(own_up, 0), in_three(b_up[None])])
    part_down = eighth(own_down, 0)
    mine_qkv, far_bias = pack(300, after(z_qkv, part_up, part_down), own_qkv.shape[2])
    came_qkv = first_link(mine_qkv)
    z_up = along_z(after(part_up, mine_qkv))

    x = to_items(after(tokens, mine_qkv))
    held_qkv = pack(300, [mine_qkv, came_qkv])
    far_qkv = second_link(held_qkv)
    held2_qkv = cores(held_qkv)
    mine_up, far_up_bias = pack(300, after(z_up, held_qkv), own_out.shape[1] + own_up.shape[1])
    came_up = first_link(mine_up)

    timesteps, buckets, counts = after((timesteps, buckets, counts), mine_up)
    total_live = jnp.sum(counts).astype(f32)
    weighting = 1.0 / total_live
    live = (z < lax.dynamic_index_in_dim(counts, me, 0, True)).astype(f32)
    my_step = lax.dynamic_index_in_dim(timesteps, z, 0, True)
    my_bucket = lax.dynamic_index_in_dim(buckets, z, 0, False)
    time_embed = embed(
        300,
        sinusoid(my_step.astype(f32), width), w_time, lax.dynamic_index_in_dim(table, my_bucket, 0, True)
    )

    far2_qkv = cores(after(far_qkv, mine_up))
    g_qkv = Gathered(own_qkv, [held_qkv, far_qkv, held2_qkv, far2_qkv], 1, 0)
    held_up = pack(300, [mine_up, after(came_up, far2_qkv, held2_qkv, time_embed)])
    far_up = second_link(held_up)
    held2_up = cores(held_up)
    x = after(x, held_up)
    hidden = (x.astype(f32) + time_embed).astype(bf16)
    z_down = along_z(after(part_down, hidden))

    done = attend(300, 0, mpn, Gathered(own_qkv, [], 1, 0), place, hidden, own_bias[None], [])
    done = attend(300, 1, mpn, g_qkv, place, after(hidden, held2_up), far_bias, done)
    far2_up = cores(after(far_up, done))
    done = attend(300, 2, mpn, g_qkv, place, hidden, far_bias, done)
    mine_down = pack(300, after(z_down, done, far2_up))
    came_down = first_link(mine_down)
    cot = to_items(after(cotangent, mine_down))
    qkv, probs, ctx = attend(300, 3, mpn, g_qkv, place, after(hidden, mine_down), far_bias, done)
    held_down = pack(300, [mine_down, after(came_down, ctx)])
    far_down = second_link(held_down)
    held2_down = cores(held_down)
    ctx2, hidden2 = cores(after(ctx, held_down)), cores(after(hidden, held_down))
    up_pieces = [held_up, far_up, held2_up, far2_up]
    g_out = Gathered(own_out, up_pieces, 0, 0)
    g_up = Gathered(own_up, up_pieces, 0, own_out.shape[1])
    n1, inv1, normed_low, active, slope, full_out = up_project(
        g_out,
        g_up,
        place,
        after(ctx, held_down),
        x,
        time_embed,
        b_out,
        gain1,
        shift1,
        jnp.concatenate([b_up[None, None], far_up_bias]),
    )
    full_out = full_out.reshape(mpn, head_cols, width)
    far2_down = cores(after(far_down, normed_low, held2_down, ctx2, hidden2))
    g_down = Gathered(own_down, [held_down, far_down, held2_down, far2_down], 0, 0)
    cot = after(cot, normed_low)
    active2 = cores(active)
    output, branch_grad, sums2 = down_project(
        g_down, place, live, active, n1, cot, b_down, gain1, shift1, gain2, shift2
    )
    def send_home(covers, keep, came, last):
        sums = gather_up(covers, keep, came, last)
        return [sums[0]] + [shift(v, -s - 1) for s, v in enumerate(sums[1:])], sums

    def finish(arrived, pieces):
        if extra == 0:
            return finish_all(weighting[None], arrived, pieces)
        total = sum(a.astype(f32) for a in arrived) * weighting
        for t in reversed(range(extra)):
            half = total.shape[0] // 2
            bit = (me >> t) & 1
            keep = lax.dynamic_slice_in_dim(total, bit * half, half, 0)
            sent = lax.dynamic_slice_in_dim(total, (1 - bit) * half, half, 0)
            total = keep + lax.ppermute(sent, "dp", [(i, i ^ (1 << t)) for i in range(dpn)])
        made = []
        for kind, low, high in pieces:
            part = total[:, low:high]
            if kind == "turned":
                part = part.T
            elif kind == "three":
                part = jnp.moveaxis(part.reshape(part.shape[0], 3, -1), 1, 0)
            made.append(part)
        return made

    devices = dpn * mpn
    both = ("dp", "mp")

    def in_order(parts):
        turned = jnp.stack([parts[-i % mpn] for i in range(mpn)] * 2)
        return lax.dynamic_slice_in_dim(turned, (mpn - z) % mpn, mpn, 0).reshape(-1)

    keep_d, send_d = weight_grad(300, place, [(branch_grad, cores(branch_grad), active, active2)])
    came_d = first_link(send_d)
    low2 = cores(after(normed_low, keep_d))
    up_grad, bias_up, grad_first, mixing_grad, sums1 = up_back(
        g_down, g_up, place, after(branch_grad, keep_d), slope, n1, inv1, gain1
    )
    up_grad2, mixing_grad2 = cores(up_grad), cores(mixing_grad)
    pass_d = pass_on(keep_d, after(came_d, mixing_grad, low2))
    last_d = second_link(pass_d)
    out_items = to_positions(after(output, mixing_grad))
    keep_u, send_u = weight_grad(
        300,
        place,
        after([(normed_low, low2, up_grad, up_grad2), (mixing_grad, mixing_grad2, ctx, ctx2)], pass_d),
    )
    came_u = first_link(send_u)
    pg, bias_near = attend_back(300, 0, mpn // 2, full_out, after(mixing_grad, keep_u), qkv, probs, None)
    home_d, sent_d = send_home(1, keep_d, came_d, after(last_d, pg))
    pg, bias_far = attend_back(
        1, mpn // 2, mpn - mpn // 2, full_out, after(mixing_grad, sent_d, out_items), qkv, probs, pg
    )
    pg2 = cores(pg)
    pass_u = pass_on(keep_u, after(came_u, pg))
    last_u = second_link(pass_u)
    grad_tokens, time_grad = input_back(g_qkv, place, after(pg, pass_u), grad_first)
    back_items = to_positions(grad_tokens)
    keep_q, send_q = weight_grad(300, place, [(hidden, hidden2, after(pg, grad_tokens), pg2)])
    bias_proj = jnp.concatenate([bias_near, bias_far])
    vectors = [
        in_order(bias_proj[:, 0, :head_cols]),
        in_order(bias_proj[:, 0, 2 * head_cols :]),
        sums1[0],
        sums1[1],
        sums1[2],
        sums2[0],
        sums2[1],
        sums2[2],
        in_order(bias_up[:, 0]),
        after(time_grad, keep_q),
    ]
    facts = jnp.stack([my_step[0].astype(f32), my_bucket.astype(f32)])
    facts = jnp.broadcast_to(facts[None], (devices, 2))
    vectors = jnp.concatenate([facts] + [v.reshape(devices, -1) for v in vectors], axis=1)
    came_q = first_link(send_q)
    home_u, sent_u = send_home(300, keep_u, came_u, after(last_u, keep_q, home_d))
    pass_q = pass_on(keep_q, after(came_q, sent_u))
    last_q = second_link(pass_q)
    back_items = after(back_items, pass_q)
    gathered = lax.all_to_all(after(vectors, back_items), both, 0, 0, tiled=True)
    home_u = after(home_u, pass_q)
    (grad_w_down,) = finish(after(home_d, pass_q), [("turned", 0, units)])
    home_q, sent_q = send_home(300, keep_q, came_q, after(last_q, grad_w_down))
    grad_tokens = jnp.moveaxis(after(back_items, sent_q), 0, 1).astype(f32)
    output = jnp.moveaxis(after(out_items, sent_q), 0, 1)
    grad_w_up, grad_w_out = finish(
        after(home_u, sent_q), [("plain", 0, units), ("turned", units, units + head_cols)]
    )
    (grad_w_qkv,) = finish(home_q, [("three", 0, 3 * head_cols)])
    per = width // devices

    gathered = after(gathered, sent_q)
    grads = gathered[:, -per:]
    summed = jnp.sum(gathered[:, 2:-per], axis=0) * weighting
    steps, rows_of = gathered[:, 0], gathered[:, 1]
    small = [summed[i * per : (i + 1) * per] for i in range(8)]
    grad_b_up = summed[8 * per :]
    high = lax.Precision.HIGHEST
    grad_w_time = (
        jnp.einsum("nd,ne->de", sinusoid(steps, width).astype(f32), grads, precision=high)
        * weighting
    )
    onehot = (rows_of[:, None] == jnp.arange(table.shape[0], dtype=f32)[None, :]).astype(f32)
    grad_table = jnp.einsum("nb,nd->bd", onehot, grads, precision=high) * weighting
    return (
        output,
        grad_tokens,
        grad_w_time,
        grad_table,
        grad_w_qkv,
        jnp.stack(small[:2]),
        grad_w_out,
        small[2],
        small[3],
        small[4],
        grad_w_up,
        grad_b_up,
        grad_w_down,
        small[5],
        small[6],
        small[7],
    )


def solution(mesh):
    return jax.shard_map(
        on_device,
        mesh=mesh,
        in_specs=(
            P("mp", "dp", None),
            P("dp"),
            P("dp"),
            P(),
            P(),
            P(),
            P(None, None, "mp"),
            P(None, "mp"),
            P("mp", None),
            P(),
            P(),
            P(),
            P(None, "mp"),
            P("mp"),
            P("mp", None),
            P(),
            P(),
            P(),
            P("mp", "dp", None),
        ),
        out_specs=(
            P("mp", "dp", None),
            P("mp", "dp", None),
            P(None, ("dp", "mp")),
            P(None, ("dp", "mp")),
            P(None, "dp", "mp"),
            P(None, ("dp", "mp")),
            P("mp", "dp"),
            P(("dp", "mp")),
            P(("dp", "mp")),
            P(("dp", "mp")),
            P("dp", "mp"),
            P(("dp", "mp")),
            P("mp", "dp"),
            P(("dp", "mp")),
            P(("dp", "mp")),
            P(("dp", "mp")),
        ),
        check_vma=False,
    )
```

```python
import functools
import math

import jax
import jax.numpy as jnp
from jax import lax
from jax.experimental import pallas as pl
from jax.experimental.pallas import tpu as pltpu
from jax.sharding import PartitionSpec as P

HD = 64
f32 = jnp.float32
bf16 = jnp.bfloat16
VMEM_LIMIT = 56 * 2**20


def params(**more):
    return pltpu.CompilerParams(vmem_limit_bytes=VMEM_LIMIT, **more)


def dot(a, b, dims):
    return lax.dot_general(a, b, (dims, ((), ())), preferred_element_type=f32)


def sinusoid(steps, model_width):
    half_width = model_width // 2
    freqs = jnp.exp(-math.log(10000.0) * jnp.arange(half_width, dtype=f32) / half_width)
    angles = steps[:, None] * freqs[None, :]
    return jnp.concatenate([jnp.sin(angles), jnp.cos(angles)], axis=-1).astype(bf16)


def masks(place):
    first = 2 + 2 * (place & 1)
    return first, 6 - first


class Gathered:
    def __init__(self, own, pieces, lead, start):
        self.arrays = [own] + pieces
        self.lead = lead
        self.start = start
        self.dims = own.shape

    def scratch(self, shards):
        return [pltpu.VMEM((shards,) + self.dims, bf16), pltpu.SemaphoreType.DMA((shards, 8))]

    def copies_of(self, refs, place, into, sems, shard, slot):
        if isinstance(shard, int) and shard == 0:
            return [pltpu.make_async_copy(refs[0], into.at[slot], sems.at[slot, 0])]
        lead = (slice(None),) * self.lead
        first, second = masks(place)
        held = (place, place ^ first)
        far = (place ^ second, place ^ 6)
        held2 = (place ^ 1, place ^ 1 ^ second)
        far2 = (place ^ 1 ^ first, place ^ 7)
        made = []
        for ref, chunks in zip(refs[1:], (held, far, held2, far2)):
            for i, chunk in enumerate(chunks):
                at = lead + (pl.ds(self.start, self.dims[-2]),)
                made.append(
                    pltpu.make_async_copy(
                        ref.at[i, shard - 1].at[at],
                        into.at[(slot,) + lead + (chunk,)],
                        sems.at[slot, len(made)],
                    )
                )
        return made

    def start_all(self, refs, place, into, sems, shards):
        for shard in range(shards):
            for copy in self.copies_of(refs, place, into, sems, shard, shard):
                copy.start()

    def wait(self, refs, place, into, sems, shard):
        @pl.when(shard == 0)
        def _():
            for copy in self.copies_of(refs, place, into, sems, 0, 0):
                copy.wait()

        @pl.when(shard > 0)
        def _():
            for copy in self.copies_of(refs, place, into, sems, shard, shard):
                copy.wait()


HBM = pl.BlockSpec(memory_space=pl.ANY)
SMEM = pl.BlockSpec(memory_space=pltpu.SMEM)


def whole(shape):
    return pl.BlockSpec(shape, lambda *_: (0,) * len(shape))


def cost(micros):
    return pl.CostEstimate(flops=int(micros * 1.15e9), transcendentals=0, bytes_accessed=0)


def over_rows(length, step, body, init):
    def one(i, carry):
        return body(pl.ds(pl.multiple_of(i * step, step), step), carry)

    return lax.fori_loop(0, length // step, one, init)


def row_sum(v):
    return jnp.sum(v, axis=0, keepdims=True)


def pack_body(rows, n, with_sum, *refs):
    parts, out_ref = refs[:n], refs[n]
    sems = refs[-1]
    lead = (slice(None),) * (len(parts[0].shape) - 2)
    copies = []
    for i, ref in enumerate(parts):
        at = lead + (pl.ds(0, rows),)
        copies.append(pltpu.make_async_copy(ref.at[at], out_ref.at[i], sems.at[len(copies)]))
        if with_sum:
            at = lead + (pl.ds(rows, 8),)
            copies.append(pltpu.make_async_copy(ref.at[at], refs[-2].at[i], sems.at[len(copies)]))
    for copy in copies:
        copy.start()
    for copy in copies:
        copy.wait()
    if with_sum:
        extra = refs[-2][...].astype(f32)
        refs[n + 1][...] = sum(extra[..., i : i + 1, :] for i in range(3))


def pack(covers, parts, rows=None):
    dims = parts[0].shape
    n = len(parts)
    lead = (n,) + dims[:-2]
    out = [jax.ShapeDtypeStruct(lead + (rows or dims[-2], dims[-1]), bf16)]
    scratch = []
    if rows:
        out.append(jax.ShapeDtypeStruct(lead + (1, dims[-1]), f32))
        scratch.append(pltpu.VMEM(lead + (8, dims[-1]), bf16))
    made = pl.pallas_call(
        functools.partial(pack_body, rows or dims[-2], n, bool(rows)),
        out_shape=out,
        in_specs=[HBM] * n,
        out_specs=[pl.BlockSpec(memory_space=pltpu.VMEM)] * len(out),
        scratch_shapes=scratch + [pltpu.SemaphoreType.DMA((2 * n,))],
        compiler_params=params(),
        cost_estimate=cost(covers),
        name="pack",
    )(*parts)
    return made if rows else made[0]


def in_three(v):
    parts = []
    for _ in range(3):
        parts.append(lax.reduce_precision(v, 8, 7))
        v = v - parts[-1]
    return jnp.concatenate(parts + [jnp.zeros_like(v)] * 5, axis=-2).astype(bf16)


def embed_body(sinus_ref, w_ref, row_ref, out_ref):
    out_ref[...] = dot(sinus_ref[...], w_ref[...], ((1,), (0,)))[:1] + row_ref[...]


def embed(covers, sinus, w, row):
    return pl.pallas_call(
        embed_body,
        out_shape=jax.ShapeDtypeStruct(row.shape, f32),
        compiler_params=params(),
        cost_estimate=cost(covers),
        name="embed",
    )(jnp.broadcast_to(sinus, (16,) + sinus.shape[1:]), w, row)


def attend_body(shard, gathered, place_ref, x_hbm, bias_ref, *refs):
    n = len(gathered.arrays)
    w_refs = refs[:n]
    qkv_ref, p_ref, c_ref, w, sems, x_ref, x_sem = refs[-7:]
    pair = pl.program_id(0)
    place = place_ref[0]
    cols = w.shape[-1]

    @pl.when(pair == 0)
    def _():
        copies = [pltpu.make_async_copy(x_hbm, x_ref, x_sem.at[0])]
        copies += gathered.copies_of(w_refs, place, w, sems, shard, 0)
        for copy in copies:
            copy.start()
        for copy in copies:
            copy.wait()
        for c in range(3):
            wide = w[0, c].reshape(x_ref.shape[1], cols)
            out = dot(x_ref[...], wide, ((1,), (0,))) + bias_ref[0, c]
            qkv_ref[0, :, c * cols : (c + 1) * cols] = out.astype(bf16)

    at = pl.multiple_of(pair * 2 * HD, 2 * HD)
    q = qkv_ref[0, :, pl.ds(at, 2 * HD)]
    k = qkv_ref[0, :, pl.ds(cols + at, 2 * HD)]
    v = qkv_ref[0, :, pl.ds(2 * cols + at, 2 * HD)]
    lane = lax.broadcasted_iota(jnp.int32, q.shape, 1)
    joined = None
    for hh in range(2):
        mine = (lane // HD) == hh
        kh = jnp.where(mine, k, jnp.zeros_like(k))
        st = dot(kh, q, ((1,), (1,))) * 0.125
        top = jnp.max(st, axis=0, keepdims=True)
        e = jnp.exp(st - top)
        p = (e * (1.0 / jnp.sum(e, axis=0, keepdims=True))).astype(bf16)
        p_ref[0, hh] = p
        c = dot(p, v, ((0,), (0,)))
        joined = c if joined is None else jnp.where(mine, c, joined)
    c_ref[0] = joined.astype(bf16)


def attend(covers, shard, shards, gathered, place, x, bias, old):
    length, width = x.shape
    cols = gathered.dims[-1]
    pairs = cols // (2 * HD)
    n_w = len(gathered.arrays)
    return pl.pallas_call(
        functools.partial(attend_body, shard, gathered),
        grid=(pairs,),
        out_shape=[
            jax.ShapeDtypeStruct((shards, length, 3 * cols), bf16),
            jax.ShapeDtypeStruct((shards, 2 * pairs, length, length), bf16),
            jax.ShapeDtypeStruct((shards, length, cols), bf16),
        ],
        in_specs=[SMEM, HBM, pl.BlockSpec((1, 3, 1, cols), lambda i: (max(shard - 1, 0), 0, 0, 0))]
        + [HBM] * (n_w + len(old)),
        out_specs=[
            pl.BlockSpec((1, length, 3 * cols), lambda i: (shard, 0, 0)),
            pl.BlockSpec((1, 2, length, length), lambda i: (shard, i, 0, 0)),
            pl.BlockSpec((1, length, 2 * HD), lambda i: (shard, 0, i)),
        ],
        input_output_aliases={3 + n_w + i: i for i in range(len(old))},
        scratch_shapes=gathered.scratch(1) + [pltpu.VMEM(x.shape, bf16), pltpu.SemaphoreType.DMA((1,))],
        compiler_params=params(),
        cost_estimate=cost(covers),
        name="attend",
    )(place, x, bias, *gathered.arrays, *old)


def norm_stats(values):
    center = values - jnp.mean(values, axis=-1, keepdims=True)
    inv = lax.rsqrt(jnp.mean(center * center, axis=-1, keepdims=True) + 1e-05)
    return center * inv, inv


def norm_back(grad, n, inv, gain):
    gn = grad * gain
    return (gn - jnp.mean(gn, -1, keepdims=True) - n * jnp.mean(gn * n, -1, keepdims=True)) * inv


def up_body(
    shards, g_out, g_up, place_ref, ctx_ref, x_ref, te_ref, b_ref, gain_ref, shift_ref, bias_ref, *refs
):
    n_out = len(g_out.arrays)
    out_refs = list(refs[:n_out])
    up_refs = [refs[n_out]] + list(refs[1:n_out])
    n1_ref, inv_ref, low_ref, act_ref, slope_ref, wo_full = refs[n_out + 1 : n_out + 7]
    wo, o_sems, wu, u_sems, acc, keep_o = refs[n_out + 7 :]
    s = pl.program_id(0)
    place = place_ref[0]
    length, width = acc.shape

    def keep_out(shard):
        return pltpu.make_async_copy(wo.at[shard], wo_full.at[shard], keep_o.at[shard])

    @pl.when(s == 0)
    def _():
        g_out.start_all(out_refs, place, wo, o_sems, shards)
        g_up.start_all(up_refs, place, wu, u_sems, shards)
        for shard in range(shards):
            g_out.wait(out_refs, place, wo, o_sems, shard)
            keep_out(shard).start()
            part = dot(ctx_ref[shard], wo[shard].reshape(-1, width), ((1,), (0,)))
            if shard == 0:
                acc[...] = part
            else:
                acc[...] += part

        def rows(at, _):
            start = x_ref[at, :].astype(f32) + te_ref[...]
            n1, inv = norm_stats(start + (acc[at, :] + b_ref[...]))
            n1_ref[at, :] = n1
            inv_ref[at, :] = jnp.broadcast_to(inv, (64, inv_ref.shape[1]))
            low_ref[at, :] = (n1 * gain_ref[...] + shift_ref[...]).astype(bf16)
            return 0

        over_rows(length, 64, rows, 0)

    g_up.wait(up_refs, place, wu, u_sems, s)
    units = wu.shape[-1]

    def columns(n, _):
        span = pl.ds(pl.multiple_of(n * 256, 256), 256)
        u = dot(low_ref[...], wu[s, :, :, span].reshape(width, 256), ((1,), (0,)))
        u = u + bias_ref[0, :, span]
        phi = 0.5 + 0.5 * lax.erf(u * (2.0**-0.5))
        act_ref[0, :, span] = (u * phi).astype(bf16)
        slope = phi + u * jnp.exp(-0.5 * u * u) * (2.0 * math.pi) ** -0.5
        slope_ref[0, :, span] = slope.astype(bf16)
        return 0

    lax.fori_loop(0, units // 256, columns, 0)

    @pl.when(s == shards - 1)
    def _():
        for shard in range(shards):
            keep_out(shard).wait()


def up_project(g_out, g_up, place, ctx, x, time_embed, b_out, gain, shift, bias):
    length, width = x.shape
    shards = ctx.shape[0]
    units = g_up.dims[-1]
    block = pl.BlockSpec((1, length, units), lambda s: (s, 0, 0))
    row = whole((1, width))
    return pl.pallas_call(
        functools.partial(up_body, shards, g_out, g_up),
        grid=(shards,),
        out_shape=[
            jax.ShapeDtypeStruct((length, width), f32),
            jax.ShapeDtypeStruct((length, 128), f32),
            jax.ShapeDtypeStruct((length, width), bf16),
            jax.ShapeDtypeStruct((shards, length, units), bf16),
            jax.ShapeDtypeStruct((shards, length, units), bf16),
            jax.ShapeDtypeStruct((shards,) + g_out.dims, bf16),
        ],
        in_specs=[
            SMEM,
            whole(ctx.shape),
            whole(x.shape),
            row,
            row,
            row,
            row,
            pl.BlockSpec((1, 1, units), lambda s: (s, 0, 0)),
        ]
        + [HBM] * (len(g_out.arrays) + 1),
        out_specs=[
            whole((length, width)),
            whole((length, 128)),
            whole((length, width)),
            block,
            block,
            HBM,
        ],
        scratch_shapes=g_out.scratch(shards)
        + g_up.scratch(shards)
        + [pltpu.VMEM((length, width), f32)]
        + [pltpu.SemaphoreType.DMA((shards,))],
        compiler_params=params(),
        cost_estimate=cost(300),
        name="up_project",
    )(place, ctx, x, time_embed, b_out, gain, shift, bias, *g_out.arrays, g_up.arrays[0])


def down_body(
    shards, gathered, place_ref, live_ref, act_ref, b_ref, gain1_ref, shift1_ref, gain2_ref, shift2_ref,
    n1_hbm, cot_hbm, *refs
):
    n = len(gathered.arrays)
    w_refs, (out_hbm, bg_hbm, sums_ref) = refs[:n], refs[n : n + 3]
    w, sems, acc, n1_ref, cot_ref, late, out_ref, bg_ref, done = refs[n + 3 :]
    s = pl.program_id(0)
    place = place_ref[0]
    length, width = acc.shape

    def fetch(i):
        return pltpu.make_async_copy((n1_hbm, cot_hbm)[i], (n1_ref, cot_ref)[i], late.at[i])

    @pl.when(s == 0)
    def _():
        gathered.start_all(w_refs, place, w, sems, shards)
        fetch(0).start()
        fetch(1).start()

    gathered.wait(w_refs, place, w, sems, s)
    part = dot(act_ref[0], w[s].reshape(-1, width), ((1,), (0,)))

    @pl.when(s == 0)
    def _():
        acc[...] = part

    @pl.when(s > 0)
    def _():
        acc[...] += part

    @pl.when(s == shards - 1)
    def _():
        live = live_ref[0]
        fetch(0).wait()
        fetch(1).wait()

        def leave(i):
            at = pl.ds(i * 64, 64)
            return [
                pltpu.make_async_copy(out_ref.at[at], out_hbm.at[at], done.at[0, i]),
                pltpu.make_async_copy(bg_ref.at[at], bg_hbm.at[at], done.at[1, i]),
            ]

        def rows(i, sums):
            at = pl.ds(pl.multiple_of(i * 64, 64), 64)
            normed = n1_ref[at, :] * gain1_ref[...] + shift1_ref[...]
            n2, inv = norm_stats(normed + (acc[at, :] + b_ref[...]))
            out_ref[at, :] = (n2 * gain2_ref[...] + shift2_ref[...]).astype(bf16)
            grad = cot_ref[at, :].astype(f32) * live
            second = norm_back(grad, n2, inv, gain2_ref[...])
            low = second.astype(bf16)
            bg_ref[at, :] = low
            for copy in leave(i):
                copy.start()
            add = (low.astype(f32), grad * n2, grad)
            return tuple(a + row_sum(b) for a, b in zip(sums, add))

        zero = jnp.zeros((1, width), f32)
        sums = lax.fori_loop(0, length // 64, rows, (zero, zero, zero))
        for i, v in enumerate(sums):
            sums_ref[i : i + 1, :] = v
        for i in range(length // 64):
            for copy in leave(i):
                copy.wait()


def down_project(gathered, place, live, act, n1, cot, b_down, gain1, shift1, gain2, shift2):
    shards, length, units = act.shape
    width = n1.shape[1]
    row = whole((1, width))
    return pl.pallas_call(
        functools.partial(down_body, shards, gathered),
        grid=(shards,),
        out_shape=[
            jax.ShapeDtypeStruct((length, width), bf16),
            jax.ShapeDtypeStruct((length, width), bf16),
            jax.ShapeDtypeStruct((3, width), f32),
        ],
        in_specs=[SMEM, SMEM, pl.BlockSpec((1, length, units), lambda s: (s, 0, 0))]
        + [row] * 5
        + [HBM] * (2 + len(gathered.arrays)),
        out_specs=[HBM] * 2 + [whole((3, width))],
        scratch_shapes=gathered.scratch(shards)
        + [
            pltpu.VMEM((length, width), f32),
            pltpu.VMEM((length, width), f32),
            pltpu.VMEM((length, width), bf16),
            pltpu.SemaphoreType.DMA((2,)),
            pltpu.VMEM((length, width), bf16),
            pltpu.VMEM((length, width), bf16),
            pltpu.SemaphoreType.DMA((2, length // 64)),
        ],
        compiler_params=params(),
        cost_estimate=cost(300),
        name="down_project",
    )(place, live, act, b_down, gain1, shift1, gain2, shift2, n1, cot, *gathered.arrays)


def up_back_body(
    shards, g_down, g_up, place_ref, bg_ref, slope_ref, inv_ref, gain_ref, n1_hbm, *refs
):
    n = len(g_down.arrays)
    d_refs, u_refs = list(refs[:n]), [refs[n]] + list(refs[n + 1 : 2 * n])
    ug_ref, bias_ref, gf_ref, mg_ref, sums_ref = refs[2 * n : 2 * n + 5]
    wd, d_sems, wu, u_sems, acc, n1_ref, late = refs[2 * n + 5 :]
    s = pl.program_id(0)
    place = place_ref[0]
    length, width = acc.shape

    fetch = pltpu.make_async_copy(n1_hbm, n1_ref, late.at[0])

    @pl.when(s == 0)
    def _():
        for shard in range(shards):
            for copy in g_down.copies_of(d_refs, place, wd, d_sems, shard, shard):
                copy.start()
            for copy in g_up.copies_of(u_refs, place, wu, u_sems, shard, shard):
                copy.start()
        fetch.start()

    g_down.wait(d_refs, place, wd, d_sems, s)
    units = ug_ref.shape[2]

    def columns(n, _):
        span = pl.ds(pl.multiple_of(n * 256, 256), 256)
        rows = wd[s, pl.ds(2 * n, 2)].reshape(256, width)
        grad = dot(bg_ref[...], rows, ((1,), (1,)))
        low = (grad * slope_ref[0, :, span].astype(f32)).astype(bf16)
        ug_ref[0, :, span] = low
        bias_ref[0, :, span] = row_sum(low.astype(f32))
        return 0

    lax.fori_loop(0, units // 256, columns, 0)
    g_up.wait(u_refs, place, wu, u_sems, s)
    part = dot(ug_ref[0], wu[s].reshape(width, units), ((1,), (1,)))

    @pl.when(s == 0)
    def _():
        acc[...] = part

    @pl.when(s > 0)
    def _():
        acc[...] += part

    @pl.when(s == shards - 1)
    def _():
        fetch.wait()

        def rows(at, sums):
            n1, grad = n1_ref[at, :], acc[at, :] + bg_ref[at, :].astype(f32)
            first = norm_back(grad, n1, inv_ref[at, 0:1], gain_ref[...])
            gf_ref[at, :] = first
            low = first.astype(bf16)
            mg_ref[at, :] = low
            add = (low.astype(f32), grad * n1, grad)
            return tuple(a + row_sum(b) for a, b in zip(sums, add))

        zero = jnp.zeros((1, width), f32)
        sums = over_rows(length, 64, rows, (zero, zero, zero))
        for i, v in enumerate(sums):
            sums_ref[i : i + 1, :] = v


def up_back(g_down, g_up, place, bg, slope, n1, inv, gain):
    shards, length, units = slope.shape
    width = n1.shape[1]
    block = pl.BlockSpec((1, length, units), lambda s: (s, 0, 0))
    return pl.pallas_call(
        functools.partial(up_back_body, shards, g_down, g_up),
        grid=(shards,),
        out_shape=[
            jax.ShapeDtypeStruct((shards, length, units), bf16),
            jax.ShapeDtypeStruct((shards, 1, units), f32),
            jax.ShapeDtypeStruct((length, width), f32),
            jax.ShapeDtypeStruct((length, width), bf16),
            jax.ShapeDtypeStruct((3, width), f32),
        ],
        in_specs=[SMEM, whole(bg.shape), block, whole(inv.shape), whole((1, width))]
        + [HBM] * (1 + len(g_down.arrays) + len(g_up.arrays)),
        out_specs=[
            block,
            pl.BlockSpec((1, 1, units), lambda s: (s, 0, 0)),
            whole((length, width)),
            whole((length, width)),
            whole((3, width)),
        ],
        scratch_shapes=g_down.scratch(shards)
        + g_up.scratch(shards)
        + [pltpu.VMEM((length, width), f32)] * 2
        + [pltpu.SemaphoreType.DMA((1,))],
        compiler_params=params(),
        cost_estimate=cost(300),
        name="up_back",
    )(place, bg, slope, inv, gain, n1, *g_down.arrays, *g_up.arrays)


def attend_back_body(mg_ref, wo_ref, qkv, p_of, *refs):
    pg_ref, bias_ref, cg = refs[-3:]
    pair = pl.program_id(1)
    cols = cg.shape[1]

    @pl.when(pair == 0)
    def _():
        cg[...] = dot(mg_ref[...], wo_ref[0], ((1,), (1,))).astype(bf16)

    at = pl.multiple_of(pair * 2 * HD, 2 * HD)
    q = qkv[0, :, pl.ds(at, 2 * HD)]
    k = qkv[0, :, pl.ds(cols + at, 2 * HD)]
    v = qkv[0, :, pl.ds(2 * cols + at, 2 * HD)]
    g = cg[:, pl.ds(at, 2 * HD)]
    lane = lax.broadcasted_iota(jnp.int32, q.shape, 1)
    dq = dk = dv = None
    for hh in range(2):
        mine = (lane // HD) == hh
        zero = jnp.zeros_like(q)
        gh = jnp.where(mine, g, zero)
        kh = jnp.where(mine, k, zero)
        qh = jnp.where(mine, q, zero)
        p = p_of[0, hh]
        dpt = dot(v, gh, ((1,), (1,)))
        pf = p.astype(f32)
        row = row_sum(pf * dpt)
        ds = (pf * (dpt - row)).astype(bf16)
        a = dot(p, gh, ((1,), (0,)))
        b = dot(ds, qh, ((1,), (0,)))
        c = dot(ds, kh, ((0,), (0,)))
        dv = a if dv is None else dv + a
        dk = b if dk is None else dk + b
        dq = c if dq is None else dq + c
    for c, g in enumerate((dq * 0.125, dk * 0.125, dv)):
        low = g.astype(bf16)
        pg_ref[0, :, pl.ds(c * cols + at, 2 * HD)] = low
        bias_ref[0, :, pl.ds(c * cols + at, 2 * HD)] = row_sum(low.astype(f32))


def attend_back(covers, base, count, w_out, mg, qkv, p, pg):
    length, width = mg.shape
    shards, cols = w_out.shape[:2]
    pairs = cols // (2 * HD)
    old = [] if pg is None else [pg]
    return pl.pallas_call(
        attend_back_body,
        grid=(count, pairs),
        out_shape=[
            jax.ShapeDtypeStruct((shards, length, 3 * cols), bf16),
            jax.ShapeDtypeStruct((count, 1, 3 * cols), f32),
        ],
        in_specs=[
            whole(mg.shape),
            pl.BlockSpec((1, cols, width), lambda s, i: (s + base, 0, 0)),
            pl.BlockSpec((1, length, 3 * cols), lambda s, i: (s + base, 0, 0)),
            pl.BlockSpec((1, 2, length, length), lambda s, i: (s + base, i, 0, 0)),
        ]
        + [HBM] * len(old),
        out_specs=[
            pl.BlockSpec((1, length, 3 * cols), lambda s, i: (s + base, 0, 0)),
            pl.BlockSpec((1, 1, 3 * cols), lambda s, i: (s, 0, 0)),
        ],
        input_output_aliases={4: 0} if old else {},
        scratch_shapes=[pltpu.VMEM((length, cols), bf16)],
        compiler_params=params(),
        cost_estimate=cost(covers),
        name="attend_back",
    )(mg, w_out, qkv, p, *old)


def input_back_body(shards, gathered, place_ref, pg_ref, gf_hbm, *refs):
    n = len(gathered.arrays)
    w_refs, (gt_ref, tg_ref, w, sems, acc, gf_ref, late) = refs[:n], refs[n:]
    s = pl.program_id(0)
    place = place_ref[0]
    cols = w.shape[-1]
    length, width = acc.shape
    fetch = pltpu.make_async_copy(gf_hbm, gf_ref, late.at[0])

    @pl.when(s == 0)
    def _():
        gathered.start_all(w_refs, place, w, sems, shards)
        fetch.start()
        acc[...] = jnp.zeros_like(acc)

    gathered.wait(w_refs, place, w, sems, s)
    part = None
    for c in range(3):
        new = dot(pg_ref[0, :, c * cols : (c + 1) * cols], w[s, c].reshape(width, cols), ((1,), (1,)))
        part = new if part is None else part + new
    acc[...] += part

    @pl.when(s == shards - 1)
    def _():
        fetch.wait()

        def rows(at, total):
            grad = acc[at, :] + gf_ref[at, :]
            gt_ref[at, :] = grad.astype(bf16)
            return total + row_sum(grad)

        tg_ref[...] = over_rows(length, 64, rows, jnp.zeros((1, width), f32))


def input_back(gathered, place, pg, gf):
    shards, length, cols3 = pg.shape
    width = gf.shape[1]
    return pl.pallas_call(
        functools.partial(input_back_body, shards, gathered),
        grid=(shards,),
        out_shape=[
            jax.ShapeDtypeStruct((length, width), bf16),
            jax.ShapeDtypeStruct((1, width), f32),
        ],
        in_specs=[SMEM, pl.BlockSpec((1, length, cols3), lambda s: (s, 0, 0)), HBM]
        + [HBM] * len(gathered.arrays),
        out_specs=[whole((length, width)), whole((1, width))],
        scratch_shapes=gathered.scratch(shards)
        + [pltpu.VMEM((length, width), f32)] * 2
        + [pltpu.SemaphoreType.DMA((1,))],
        compiler_params=params(),
        cost_estimate=cost(1),
        name="input_back",
    )(place, pg, gf, *gathered.arrays)


def weight_grad_body(n_pairs, looped, place_ref, *refs):
    ins = refs[: 4 * n_pairs]
    keep_ref, send_ref = refs[4 * n_pairs : 4 * n_pairs + 2]
    turned = refs[4 * n_pairs + 2 :]
    place = place_ref[0]
    rows = keep_ref.shape[2]
    first, second = masks(place)

    @pl.when(pl.program_id(0) == 0)
    def _():
        for p in range(n_pairs):
            for core in range(2):
                feature_ref = ins[4 * p + core]
                length = feature_ref.shape[0]
                for j, mask in enumerate((0, second, first, 6)):
                    at = pl.multiple_of((place ^ mask) * rows, rows)
                    block = feature_ref[:, pl.ds(at, rows)]
                    turned[p][j * rows : (j + 1) * rows, core * length : (core + 1) * length] = block.T

    at = 0
    for p in range(n_pairs):
        b_ref, b2_ref = ins[4 * p + 2 : 4 * p + 4]
        length, cols = b_ref.shape[1:]

        def columns(n, _, p=p, b_ref=b_ref, b2_ref=b2_ref, length=length, at=at):
            start = n * 256 if isinstance(n, int) else pl.multiple_of(n * 256, 256)
            g = dot(turned[p][:, :length], b_ref[0, :, pl.ds(start, 256)], ((1,), (0,)))
            g += dot(turned[p][:, length:], b2_ref[0, :, pl.ds(start, 256)], ((1,), (0,)))
            g = g.astype(bf16)
            to = pl.ds(at + start if isinstance(n, int) else pl.multiple_of(at + start, 256), 256)
            for i in range(2):
                keep_ref[i, 0, :, to] = g[i * rows : (i + 1) * rows]
                send_ref[i, 0, :, to] = g[(i + 2) * rows : (i + 3) * rows]
            return 0

        if looped:
            lax.fori_loop(0, cols // 256, columns, 0)
        else:
            for n in range(cols // 256):
                columns(n, 0)
        at += cols


def weight_grad(covers, place, groups, looped=False):
    shards, length, _ = groups[0][2].shape
    rows = groups[0][0].shape[1] // 8
    cols = sum(g[2].shape[2] for g in groups)
    specs, args, scratch = [], [], []
    for feature, feature2, b, b2 in groups:
        block = pl.BlockSpec((1,) + b.shape[1:], lambda s: (s, 0, 0))
        specs += [whole(feature.shape)] * 2 + [block] * 2
        args += [feature, feature2, b, b2]
        scratch.append(pltpu.VMEM((4 * rows, 2 * length), bf16))
    out = jax.ShapeDtypeStruct((2, shards, rows, cols), bf16)
    return pl.pallas_call(
        functools.partial(weight_grad_body, len(groups), looped),
        grid=(shards,),
        out_shape=[out] * 2,
        in_specs=[SMEM] + specs,
        out_specs=[pl.BlockSpec((2, 1, rows, cols), lambda s: (0, s, 0, 0))] * 2,
        scratch_shapes=scratch,
        compiler_params=params(),
        cost_estimate=cost(covers),
        name="weight_grad",
    )(place, *args)


def pass_on_body(keep_ref, came_ref, out_ref):
    def rows(at, _):
        total = keep_ref[0, 0, at, :].astype(f32) + came_ref[0, 0, at, :].astype(f32)
        out_ref[0, at, :] = total.astype(bf16)
        return 0

    over_rows(out_ref.shape[1], 32, rows, 0)


def pass_on(keep, came):
    _, shards, rows, cols = keep.shape
    half = pl.BlockSpec((1, 1, rows, cols), lambda s: (1, s, 0, 0))
    return pl.pallas_call(
        pass_on_body,
        grid=(shards,),
        out_shape=jax.ShapeDtypeStruct((shards, rows, cols), bf16),
        in_specs=[half, half],
        out_specs=pl.BlockSpec((1, rows, cols), lambda s: (s, 0, 0)),
        compiler_params=params(),
        cost_estimate=cost(300),
        name="pass_on",
    )(keep, came)


def gather_up_body(keep_ref, came_ref, last_ref, own_ref, *out_refs):
    s = pl.program_id(0)

    def rows(at, _):
        part = keep_ref[0, 0, at, :].astype(f32) + came_ref[0, 0, at, :].astype(f32)
        part += last_ref[0, at, :].astype(f32)

        @pl.when(s == 0)
        def _():
            own_ref[at, :] = part

        low = part.astype(bf16)
        for i, ref in enumerate(out_refs):

            @pl.when(s == i + 1)
            def _():
                ref[at, :] = low

        return 0

    over_rows(own_ref.shape[0], 32, rows, 0)


def gather_up(covers, keep, came, last):
    _, shards, rows, cols = keep.shape
    half = pl.BlockSpec((1, 1, rows, cols), lambda s: (0, s, 0, 0))
    out = pl.BlockSpec((rows, cols), lambda s: (0, 0))
    return pl.pallas_call(
        gather_up_body,
        grid=(shards,),
        out_shape=[jax.ShapeDtypeStruct((rows, cols), f32)]
        + [jax.ShapeDtypeStruct((rows, cols), bf16)] * (shards - 1),
        in_specs=[half, half, pl.BlockSpec((1, rows, cols), lambda s: (s, 0, 0))],
        out_specs=[out] * shards,
        compiler_params=params(),
        cost_estimate=cost(covers),
        name="gather_up",
    )(keep, came, last)


def finish_body(pieces, scale_ref, *refs):
    n = len(refs) - len(pieces)
    total = refs[0][...]
    for ref in refs[1:n]:
        total += ref[...].astype(f32)
    total *= scale_ref[0]
    for ref, (kind, low, high) in zip(refs[n:], pieces):
        part = total[:, low:high]
        if kind == "turned":
            ref[...] = part.T
        elif kind == "plain":
            ref[...] = part
        else:
            cols = ref.shape[2]
            for c in range(ref.shape[0]):
                ref[c] = part[:, c * cols : (c + 1) * cols]


def finish_all(scale, parts, pieces):
    rows = parts[0].shape[0]
    shapes = []
    for kind, low, high in pieces:
        cols = high - low
        shapes.append({"turned": (cols, rows), "plain": (rows, cols), "three": (3, rows, cols // 3)}[kind])
    return pl.pallas_call(
        functools.partial(finish_body, pieces),
        out_shape=[jax.ShapeDtypeStruct(v, f32) for v in shapes],
        in_specs=[SMEM] + [pl.BlockSpec(memory_space=pltpu.VMEM)] * len(parts),
        compiler_params=params(),
        cost_estimate=cost(300),
        name="finish",
    )(scale, *parts)


def after(x, *deps):
    return lax.optimization_barrier((x, deps))[0]


def on_device(
    tokens,
    timesteps,
    buckets,
    counts,
    w_time,
    table,
    w_qkv,
    b_qv,
    w_out,
    b_out,
    gain1,
    shift1,
    w_up,
    b_up,
    w_down,
    b_down,
    gain2,
    shift2,
    cotangent,
):
    mpn = lax.axis_size("mp")
    dpn = lax.axis_size("dp")
    extra = dpn.bit_length() - 4
    me = lax.axis_index("dp")
    z = lax.axis_index("mp")
    q8 = me >> extra
    width = w_time.shape[0]
    positions, slots = tokens.shape[:2]
    length = positions * mpn
    head_cols = w_qkv.shape[2]
    units = w_up.shape[1]

    def exchange(x, partner):
        low = (1 << extra) - 1
        pairs = [(i, (partner(i >> extra) << extra) | (i & low)) for i in range(dpn)]
        return lax.ppermute(x, "dp", pairs)

    def cores(x):
        return exchange(x, lambda p: p ^ 1)

    def first_link(x):
        return exchange(x, lambda p: p ^ masks(p)[0])

    def second_link(x):
        return exchange(x, lambda p: p ^ masks(p)[1])

    def shift(x, s):
        return lax.ppermute(x, "mp", [(i, (i + s) % mpn) for i in range(mpn)])

    def to_items(x):
        x = lax.all_to_all(jnp.moveaxis(x, 1, 0), "mp", 0, 0, tiled=False)
        return x.reshape(length, width)

    def to_positions(x):
        return lax.all_to_all(x.reshape(mpn, positions, width), "mp", 0, 0, tiled=False)

    def split(shard, axis):
        dims = shard.shape
        return shard.reshape(dims[:axis] + (8, dims[axis] // 8) + dims[axis + 1 :])

    def eighth(shaped, axis):
        return lax.dynamic_index_in_dim(shaped, q8, axis, False)

    def along_z(part):
        return [shift(part, s) for s in range(1, mpn)]

    place = q8.astype(jnp.int32)[None]
    own_qkv, own_out, own_up, own_down = split(w_qkv, 1), split(w_out, 0), split(w_up, 0), split(w_down, 0)
    b_out, gain1, shift1, b_down, gain2, shift2 = [
        v[None] for v in (b_out, gain1, shift1, b_down, gain2, shift2)
    ]

    own_bias = jnp.stack([b_qv[0], jnp.zeros_like(b_qv[0]), b_qv[1]])[:, None]
    z_qkv = along_z(jnp.concatenate([eighth(own_qkv, 1), in_three(own_bias)], axis=1))
    part_up = jnp.concatenate([eighth(own_out, 0), eighth(own_up, 0), in_three(b_up[None])])
    part_down = eighth(own_down, 0)
    mine_qkv, far_bias = pack(300, after(z_qkv, part_up, part_down), own_qkv.shape[2])
    came_qkv = first_link(mine_qkv)
    z_up = along_z(after(part_up, mine_qkv))

    x = to_items(after(tokens, mine_qkv))
    held_qkv = pack(300, [mine_qkv, came_qkv])
    far_qkv = second_link(held_qkv)
    held2_qkv = cores(held_qkv)
    mine_up, far_up_bias = pack(300, after(z_up, held_qkv), own_out.shape[1] + own_up.shape[1])
    came_up = first_link(mine_up)

    timesteps, buckets, counts = after((timesteps, buckets, counts), mine_up)
    total_live = jnp.sum(counts).astype(f32)
    weighting = 1.0 / total_live
    live = (z < lax.dynamic_index_in_dim(counts, me, 0, True)).astype(f32)
    my_step = lax.dynamic_index_in_dim(timesteps, z, 0, True)
    my_bucket = lax.dynamic_index_in_dim(buckets, z, 0, False)
    time_embed = embed(
        300,
        sinusoid(my_step.astype(f32), width), w_time, lax.dynamic_index_in_dim(table, my_bucket, 0, True)
    )

    far2_qkv = cores(after(far_qkv, mine_up))
    g_qkv = Gathered(own_qkv, [held_qkv, far_qkv, held2_qkv, far2_qkv], 1, 0)
    held_up = pack(300, [mine_up, after(came_up, far2_qkv, held2_qkv, time_embed)])
    far_up = second_link(held_up)
    held2_up = cores(held_up)
    x = after(x, held_up)
    hidden = (x.astype(f32) + time_embed).astype(bf16)
    z_down = along_z(after(part_down, hidden))

    done = attend(300, 0, mpn, Gathered(own_qkv, [], 1, 0), place, hidden, own_bias[None], [])
    done = attend(300, 1, mpn, g_qkv, place, after(hidden, held2_up), far_bias, done)
    far2_up = cores(after(far_up, done))
    done = attend(300, 2, mpn, g_qkv, place, hidden, far_bias, done)
    mine_down = pack(300, after(z_down, done, far2_up))
    came_down = first_link(mine_down)
    qkv, probs, ctx = attend(300, 3, mpn, g_qkv, place, after(hidden, mine_down), far_bias, done)
    cot = to_items(after(cotangent, ctx))
    held_down = pack(300, [mine_down, after(came_down, ctx)])
    far_down = second_link(held_down)
    held2_down = cores(held_down)
    ctx2, hidden2 = cores(after(ctx, held_down)), cores(after(hidden, held_down))
    up_pieces = [held_up, far_up, held2_up, far2_up]
    g_out = Gathered(own_out, up_pieces, 0, 0)
    g_up = Gathered(own_up, up_pieces, 0, own_out.shape[1])
    n1, inv1, normed_low, active, slope, full_out = up_project(
        g_out,
        g_up,
        place,
        after(ctx, held_down),
        x,
        time_embed,
        b_out,
        gain1,
        shift1,
        jnp.concatenate([b_up[None, None], far_up_bias]),
    )
    full_out = full_out.reshape(mpn, head_cols, width)
    far2_down = cores(after(far_down, normed_low, held2_down, ctx2, hidden2))
    g_down = Gathered(own_down, [held_down, far_down, held2_down, far2_down], 0, 0)
    cot = after(cot, normed_low)
    active2 = cores(active)
    output, branch_grad, sums2 = down_project(
        g_down, place, live, active, n1, cot, b_down, gain1, shift1, gain2, shift2
    )
    def send_home(covers, keep, came, last):
        sums = gather_up(covers, keep, came, last)
        return [sums[0]] + [shift(v, -s - 1) for s, v in enumerate(sums[1:])], sums

    def finish(arrived, pieces):
        if extra == 0:
            return finish_all(weighting[None], arrived, pieces)
        total = sum(a.astype(f32) for a in arrived) * weighting
        for t in reversed(range(extra)):
            half = total.shape[0] // 2
            bit = (me >> t) & 1
            keep = lax.dynamic_slice_in_dim(total, bit * half, half, 0)
            sent = lax.dynamic_slice_in_dim(total, (1 - bit) * half, half, 0)
            total = keep + lax.ppermute(sent, "dp", [(i, i ^ (1 << t)) for i in range(dpn)])
        made = []
        for kind, low, high in pieces:
            part = total[:, low:high]
            if kind == "turned":
                part = part.T
            elif kind == "three":
                part = jnp.moveaxis(part.reshape(part.shape[0], 3, -1), 1, 0)
            made.append(part)
        return made

    devices = dpn * mpn
    both = ("dp", "mp")

    def in_order(parts):
        turned = jnp.stack([parts[-i % mpn] for i in range(mpn)] * 2)
        return lax.dynamic_slice_in_dim(turned, (mpn - z) % mpn, mpn, 0).reshape(-1)

    keep_d, send_d = weight_grad(300, place, [(branch_grad, cores(branch_grad), active, active2)])
    came_d = first_link(send_d)
    low2 = cores(after(normed_low, keep_d))
    up_grad, bias_up, grad_first, mixing_grad, sums1 = up_back(
        g_down, g_up, place, after(branch_grad, keep_d), slope, n1, inv1, gain1
    )
    up_grad2, mixing_grad2 = cores(up_grad), cores(mixing_grad)
    pass_d = pass_on(keep_d, after(came_d, mixing_grad, low2))
    last_d = second_link(pass_d)
    out_items = to_positions(after(output, mixing_grad))
    keep_u, send_u = weight_grad(
        300,
        place,
        after([(normed_low, low2, up_grad, up_grad2), (mixing_grad, mixing_grad2, ctx, ctx2)], pass_d),
    )
    came_u = first_link(send_u)
    pg, bias_near = attend_back(300, 0, mpn // 2, full_out, after(mixing_grad, keep_u), qkv, probs, None)
    home_d, sent_d = send_home(1, keep_d, came_d, after(last_d, pg))
    pg, bias_far = attend_back(
        1, mpn // 2, mpn - mpn // 2, full_out, after(mixing_grad, sent_d, out_items), qkv, probs, pg
    )
    pg2 = cores(pg)
    pass_u = pass_on(keep_u, after(came_u, pg))
    last_u = second_link(pass_u)
    grad_tokens, time_grad = input_back(g_qkv, place, after(pg, pass_u), grad_first)
    back_items = to_positions(grad_tokens)
    keep_q, send_q = weight_grad(300, place, [(hidden, hidden2, after(pg, grad_tokens), pg2)], looped=True)
    bias_proj = jnp.concatenate([bias_near, bias_far])
    vectors = [
        in_order(bias_proj[:, 0, :head_cols]),
        in_order(bias_proj[:, 0, 2 * head_cols :]),
        sums1[0],
        sums1[1],
        sums1[2],
        sums2[0],
        sums2[1],
        sums2[2],
        in_order(bias_up[:, 0]),
        after(time_grad, keep_q),
    ]
    facts = jnp.stack([my_step[0].astype(f32), my_bucket.astype(f32)])
    facts = jnp.broadcast_to(facts[None], (devices, 2))
    vectors = jnp.concatenate([facts] + [v.reshape(devices, -1) for v in vectors], axis=1)
    came_q = first_link(send_q)
    home_u, sent_u = send_home(300, keep_u, came_u, after(last_u, keep_q, home_d))
    pass_q = pass_on(keep_q, after(came_q, sent_u))
    last_q = second_link(pass_q)
    back_items = after(back_items, pass_q)
    gathered = lax.all_to_all(after(vectors, back_items), both, 0, 0, tiled=True)
    home_u = after(home_u, pass_q)
    (grad_w_down,) = finish(after(home_d, pass_q), [("turned", 0, units)])
    home_q, sent_q = send_home(300, keep_q, came_q, after(last_q, grad_w_down))
    grad_tokens = jnp.moveaxis(after(back_items, sent_q), 0, 1).astype(f32)
    output = jnp.moveaxis(after(out_items, sent_q), 0, 1)
    grad_w_up, grad_w_out = finish(
        after(home_u, sent_q), [("plain", 0, units), ("turned", units, units + head_cols)]
    )
    (grad_w_qkv,) = finish(home_q, [("three", 0, 3 * head_cols)])
    per = width // devices

    gathered = after(gathered, sent_q)
    grads = gathered[:, -per:]
    summed = jnp.sum(gathered[:, 2:-per], axis=0) * weighting
    steps, rows_of = gathered[:, 0], gathered[:, 1]
    small = [summed[i * per : (i + 1) * per] for i in range(8)]
    grad_b_up = summed[8 * per :]
    high = lax.Precision.HIGHEST
    grad_w_time = (
        jnp.einsum("nd,ne->de", sinusoid(steps, width).astype(f32), grads, precision=high)
        * weighting
    )
    onehot = (rows_of[:, None] == jnp.arange(table.shape[0], dtype=f32)[None, :]).astype(f32)
    grad_table = jnp.einsum("nb,nd->bd", onehot, grads, precision=high) * weighting
    return (
        output,
        grad_tokens,
        grad_w_time,
        grad_table,
        grad_w_qkv,
        jnp.stack(small[:2]),
        grad_w_out,
        small[2],
        small[3],
        small[4],
        grad_w_up,
        grad_b_up,
        grad_w_down,
        small[5],
        small[6],
        small[7],
    )


def solution(mesh):
    return jax.shard_map(
        on_device,
        mesh=mesh,
        in_specs=(
            P("mp", "dp", None),
            P("dp"),
            P("dp"),
            P(),
            P(),
            P(),
            P(None, None, "mp"),
            P(None, "mp"),
            P("mp", None),
            P(),
            P(),
            P(),
            P(None, "mp"),
            P("mp"),
            P("mp", None),
            P(),
            P(),
            P(),
            P("mp", "dp", None),
        ),
        out_specs=(
            P("mp", "dp", None),
            P("mp", "dp", None),
            P(None, ("dp", "mp")),
            P(None, ("dp", "mp")),
            P(None, "dp", "mp"),
            P(None, ("dp", "mp")),
            P("mp", "dp"),
            P(("dp", "mp")),
            P(("dp", "mp")),
            P(("dp", "mp")),
            P("dp", "mp"),
            P(("dp", "mp")),
            P("mp", "dp"),
            P(("dp", "mp")),
            P(("dp", "mp")),
            P(("dp", "mp")),
        ),
        check_vma=False,
    )
```

```python
import functools
import math

import jax
import jax.numpy as jnp
from jax import lax
from jax.experimental import pallas as pl
from jax.experimental.pallas import tpu as pltpu
from jax.sharding import PartitionSpec as P

HD = 64
f32 = jnp.float32
bf16 = jnp.bfloat16
VMEM_LIMIT = 56 * 2**20


def params(**more):
    return pltpu.CompilerParams(vmem_limit_bytes=VMEM_LIMIT, **more)


def dot(a, b, dims):
    return lax.dot_general(a, b, (dims, ((), ())), preferred_element_type=f32)


def sinusoid(steps, model_width):
    half_width = model_width // 2
    freqs = jnp.exp(-math.log(10000.0) * jnp.arange(half_width, dtype=f32) / half_width)
    angles = steps[:, None] * freqs[None, :]
    return jnp.concatenate([jnp.sin(angles), jnp.cos(angles)], axis=-1).astype(bf16)


def masks(place):
    first = 2 + 2 * (place & 1)
    return first, 6 - first


class Gathered:
    def __init__(self, own, pieces, lead, start):
        self.arrays = [own] + pieces
        self.lead = lead
        self.start = start
        self.dims = own.shape

    def scratch(self, shards):
        return [pltpu.VMEM((shards,) + self.dims, bf16), pltpu.SemaphoreType.DMA((shards, 8))]

    def copies_of(self, refs, place, into, sems, shard, slot):
        if isinstance(shard, int) and shard == 0:
            return [pltpu.make_async_copy(refs[0], into.at[slot], sems.at[slot, 0])]
        lead = (slice(None),) * self.lead
        first, second = masks(place)
        held = (place, place ^ first)
        far = (place ^ second, place ^ 6)
        held2 = (place ^ 1, place ^ 1 ^ second)
        far2 = (place ^ 1 ^ first, place ^ 7)
        made = []
        for ref, chunks in zip(refs[1:], (held, far, held2, far2)):
            for i, chunk in enumerate(chunks):
                at = lead + (pl.ds(self.start, self.dims[-2]),)
                made.append(
                    pltpu.make_async_copy(
                        ref.at[i, shard - 1].at[at],
                        into.at[(slot,) + lead + (chunk,)],
                        sems.at[slot, len(made)],
                    )
                )
        return made

    def start_all(self, refs, place, into, sems, shards):
        for shard in range(shards):
            for copy in self.copies_of(refs, place, into, sems, shard, shard):
                copy.start()

    def wait(self, refs, place, into, sems, shard):
        @pl.when(shard == 0)
        def _():
            for copy in self.copies_of(refs, place, into, sems, 0, 0):
                copy.wait()

        @pl.when(shard > 0)
        def _():
            for copy in self.copies_of(refs, place, into, sems, shard, shard):
                copy.wait()


HBM = pl.BlockSpec(memory_space=pl.ANY)
SMEM = pl.BlockSpec(memory_space=pltpu.SMEM)


def whole(shape):
    return pl.BlockSpec(shape, lambda *_: (0,) * len(shape))


def cost(micros):
    return pl.CostEstimate(flops=int(micros * 1.15e9), transcendentals=0, bytes_accessed=0)


def over_rows(length, step, body, init):
    def one(i, carry):
        return body(pl.ds(pl.multiple_of(i * step, step), step), carry)

    return lax.fori_loop(0, length // step, one, init)


def row_sum(v):
    return jnp.sum(v, axis=0, keepdims=True)


def pack_body(rows, n, with_sum, *refs):
    parts, out_ref = refs[:n], refs[n]
    sems = refs[-1]
    lead = (slice(None),) * (len(parts[0].shape) - 2)
    copies = []
    for i, ref in enumerate(parts):
        at = lead + (pl.ds(0, rows),)
        copies.append(pltpu.make_async_copy(ref.at[at], out_ref.at[i], sems.at[len(copies)]))
        if with_sum:
            at = lead + (pl.ds(rows, 8),)
            copies.append(pltpu.make_async_copy(ref.at[at], refs[-2].at[i], sems.at[len(copies)]))
    for copy in copies:
        copy.start()
    for copy in copies:
        copy.wait()
    if with_sum:
        extra = refs[-2][...].astype(f32)
        refs[n + 1][...] = sum(extra[..., i : i + 1, :] for i in range(3))


def pack(covers, parts, rows=None):
    dims = parts[0].shape
    n = len(parts)
    lead = (n,) + dims[:-2]
    out = [jax.ShapeDtypeStruct(lead + (rows or dims[-2], dims[-1]), bf16)]
    scratch = []
    if rows:
        out.append(jax.ShapeDtypeStruct(lead + (1, dims[-1]), f32))
        scratch.append(pltpu.VMEM(lead + (8, dims[-1]), bf16))
    made = pl.pallas_call(
        functools.partial(pack_body, rows or dims[-2], n, bool(rows)),
        out_shape=out,
        in_specs=[HBM] * n,
        out_specs=[pl.BlockSpec(memory_space=pltpu.VMEM)] * len(out),
        scratch_shapes=scratch + [pltpu.SemaphoreType.DMA((2 * n,))],
        compiler_params=params(),
        cost_estimate=cost(covers),
        name="pack",
    )(*parts)
    return made if rows else made[0]


def in_three(v):
    parts = []
    for _ in range(3):
        parts.append(lax.reduce_precision(v, 8, 7))
        v = v - parts[-1]
    return jnp.concatenate(parts + [jnp.zeros_like(v)] * 5, axis=-2).astype(bf16)


def embed_body(sinus_ref, w_ref, row_ref, out_ref):
    out_ref[...] = dot(sinus_ref[...], w_ref[...], ((1,), (0,)))[:1] + row_ref[...]


def embed(covers, sinus, w, row):
    return pl.pallas_call(
        embed_body,
        out_shape=jax.ShapeDtypeStruct(row.shape, f32),
        compiler_params=params(),
        cost_estimate=cost(covers),
        name="embed",
    )(jnp.broadcast_to(sinus, (16,) + sinus.shape[1:]), w, row)


def attend_body(shard, gathered, place_ref, x_hbm, bias_ref, *refs):
    n = len(gathered.arrays)
    w_refs = refs[:n]
    qkv_ref, p_ref, c_ref, w, sems, x_ref, x_sem = refs[-7:]
    pair = pl.program_id(0)
    place = place_ref[0]
    cols = w.shape[-1]

    @pl.when(pair == 0)
    def _():
        copies = [pltpu.make_async_copy(x_hbm, x_ref, x_sem.at[0])]
        copies += gathered.copies_of(w_refs, place, w, sems, shard, 0)
        for copy in copies:
            copy.start()
        for copy in copies:
            copy.wait()
        for c in range(3):
            wide = w[0, c].reshape(x_ref.shape[1], cols)
            out = dot(x_ref[...], wide, ((1,), (0,))) + bias_ref[0, c]
            qkv_ref[0, :, c * cols : (c + 1) * cols] = out.astype(bf16)

    at = pl.multiple_of(pair * 2 * HD, 2 * HD)
    q = qkv_ref[0, :, pl.ds(at, 2 * HD)]
    k = qkv_ref[0, :, pl.ds(cols + at, 2 * HD)]
    v = qkv_ref[0, :, pl.ds(2 * cols + at, 2 * HD)]
    lane = lax.broadcasted_iota(jnp.int32, q.shape, 1)
    joined = None
    for hh in range(2):
        mine = (lane // HD) == hh
        kh = jnp.where(mine, k, jnp.zeros_like(k))
        st = dot(kh, q, ((1,), (1,))) * 0.125
        top = jnp.max(st, axis=0, keepdims=True)
        e = jnp.exp(st - top)
        p = (e * (1.0 / jnp.sum(e, axis=0, keepdims=True))).astype(bf16)
        p_ref[0, hh] = p
        c = dot(p, v, ((0,), (0,)))
        joined = c if joined is None else jnp.where(mine, c, joined)
    c_ref[0] = joined.astype(bf16)


def attend(covers, shard, shards, gathered, place, x, bias, old):
    length, width = x.shape
    cols = gathered.dims[-1]
    pairs = cols // (2 * HD)
    n_w = len(gathered.arrays)
    return pl.pallas_call(
        functools.partial(attend_body, shard, gathered),
        grid=(pairs,),
        out_shape=[
            jax.ShapeDtypeStruct((shards, length, 3 * cols), bf16),
            jax.ShapeDtypeStruct((shards, 2 * pairs, length, length), bf16),
            jax.ShapeDtypeStruct((shards, length, cols), bf16),
        ],
        in_specs=[SMEM, HBM, pl.BlockSpec((1, 3, 1, cols), lambda i: (max(shard - 1, 0), 0, 0, 0))]
        + [HBM] * (n_w + len(old)),
        out_specs=[
            pl.BlockSpec((1, length, 3 * cols), lambda i: (shard, 0, 0)),
            pl.BlockSpec((1, 2, length, length), lambda i: (shard, i, 0, 0)),
            pl.BlockSpec((1, length, 2 * HD), lambda i: (shard, 0, i)),
        ],
        input_output_aliases={3 + n_w + i: i for i in range(len(old))},
        scratch_shapes=gathered.scratch(1) + [pltpu.VMEM(x.shape, bf16), pltpu.SemaphoreType.DMA((1,))],
        compiler_params=params(),
        cost_estimate=cost(covers),
        name="attend",
    )(place, x, bias, *gathered.arrays, *old)


def norm_stats(values):
    center = values - jnp.mean(values, axis=-1, keepdims=True)
    inv = lax.rsqrt(jnp.mean(center * center, axis=-1, keepdims=True) + 1e-05)
    return center * inv, inv


def norm_back(grad, n, inv, gain):
    gn = grad * gain
    return (gn - jnp.mean(gn, -1, keepdims=True) - n * jnp.mean(gn * n, -1, keepdims=True)) * inv


def up_body(
    shards, g_out, g_up, place_ref, ctx_ref, x_ref, te_ref, b_ref, gain_ref, shift_ref, bias_ref, *refs
):
    n_out = len(g_out.arrays)
    out_refs = list(refs[:n_out])
    up_refs = [refs[n_out]] + list(refs[1:n_out])
    n1_ref, inv_ref, low_ref, act_ref, slope_ref, wo_full = refs[n_out + 1 : n_out + 7]
    wo, o_sems, wu, u_sems, acc, keep_o = refs[n_out + 7 :]
    s = pl.program_id(0)
    place = place_ref[0]
    length, width = acc.shape

    def keep_out(shard):
        return pltpu.make_async_copy(wo.at[shard], wo_full.at[shard], keep_o.at[shard])

    @pl.when(s == 0)
    def _():
        g_out.start_all(out_refs, place, wo, o_sems, shards)
        g_up.start_all(up_refs, place, wu, u_sems, shards)
        for shard in range(shards):
            g_out.wait(out_refs, place, wo, o_sems, shard)
            keep_out(shard).start()
            part = dot(ctx_ref[shard], wo[shard].reshape(-1, width), ((1,), (0,)))
            if shard == 0:
                acc[...] = part
            else:
                acc[...] += part

        def rows(at, _):
            start = x_ref[at, :].astype(f32) + te_ref[...]
            n1, inv = norm_stats(start + (acc[at, :] + b_ref[...]))
            n1_ref[at, :] = n1
            inv_ref[at, :] = jnp.broadcast_to(inv, (64, inv_ref.shape[1]))
            low_ref[at, :] = (n1 * gain_ref[...] + shift_ref[...]).astype(bf16)
            return 0

        over_rows(length, 64, rows, 0)

    g_up.wait(up_refs, place, wu, u_sems, s)
    units = wu.shape[-1]

    def columns(n, _):
        span = pl.ds(pl.multiple_of(n * 512, 512), 512)
        u = dot(low_ref[...], wu[s, :, :, span].reshape(width, 512), ((1,), (0,)))
        u = u + bias_ref[0, :, span]
        phi = 0.5 + 0.5 * lax.erf(u * (2.0**-0.5))
        act_ref[0, :, span] = (u * phi).astype(bf16)
        slope = phi + u * jnp.exp(-0.5 * u * u) * (2.0 * math.pi) ** -0.5
        slope_ref[0, :, span] = slope.astype(bf16)
        return 0

    lax.fori_loop(0, units // 512, columns, 0)

    @pl.when(s == shards - 1)
    def _():
        for shard in range(shards):
            keep_out(shard).wait()


def up_project(g_out, g_up, place, ctx, x, time_embed, b_out, gain, shift, bias):
    length, width = x.shape
    shards = ctx.shape[0]
    units = g_up.dims[-1]
    block = pl.BlockSpec((1, length, units), lambda s: (s, 0, 0))
    row = whole((1, width))
    return pl.pallas_call(
        functools.partial(up_body, shards, g_out, g_up),
        grid=(shards,),
        out_shape=[
            jax.ShapeDtypeStruct((length, width), f32),
            jax.ShapeDtypeStruct((length, 128), f32),
            jax.ShapeDtypeStruct((length, width), bf16),
            jax.ShapeDtypeStruct((shards, length, units), bf16),
            jax.ShapeDtypeStruct((shards, length, units), bf16),
            jax.ShapeDtypeStruct((shards,) + g_out.dims, bf16),
        ],
        in_specs=[
            SMEM,
            whole(ctx.shape),
            whole(x.shape),
            row,
            row,
            row,
            row,
            pl.BlockSpec((1, 1, units), lambda s: (s, 0, 0)),
        ]
        + [HBM] * (len(g_out.arrays) + 1),
        out_specs=[
            whole((length, width)),
            whole((length, 128)),
            whole((length, width)),
            block,
            block,
            HBM,
        ],
        scratch_shapes=g_out.scratch(shards)
        + g_up.scratch(shards)
        + [pltpu.VMEM((length, width), f32)]
        + [pltpu.SemaphoreType.DMA((shards,))],
        compiler_params=params(),
        cost_estimate=cost(300),
        name="up_project",
    )(place, ctx, x, time_embed, b_out, gain, shift, bias, *g_out.arrays, g_up.arrays[0])


def down_body(
    shards, gathered, place_ref, live_ref, act_ref, b_ref, gain1_ref, shift1_ref, gain2_ref, shift2_ref,
    n1_hbm, cot_hbm, *refs
):
    n = len(gathered.arrays)
    w_refs, (out_hbm, bg_hbm, sums_ref) = refs[:n], refs[n : n + 3]
    w, sems, acc, n1_ref, cot_ref, late, out_ref, bg_ref, done = refs[n + 3 :]
    s = pl.program_id(0)
    place = place_ref[0]
    length, width = acc.shape

    def fetch(i):
        return pltpu.make_async_copy((n1_hbm, cot_hbm)[i], (n1_ref, cot_ref)[i], late.at[i])

    @pl.when(s == 0)
    def _():
        gathered.start_all(w_refs, place, w, sems, shards)
        fetch(0).start()
        fetch(1).start()

    gathered.wait(w_refs, place, w, sems, s)
    part = dot(act_ref[0], w[s].reshape(-1, width), ((1,), (0,)))

    @pl.when(s == 0)
    def _():
        acc[...] = part

    @pl.when(s > 0)
    def _():
        acc[...] += part

    @pl.when(s == shards - 1)
    def _():
        live = live_ref[0]
        fetch(0).wait()
        fetch(1).wait()

        def leave(i):
            at = pl.ds(i * 64, 64)
            return [
                pltpu.make_async_copy(out_ref.at[at], out_hbm.at[at], done.at[0, i]),
                pltpu.make_async_copy(bg_ref.at[at], bg_hbm.at[at], done.at[1, i]),
            ]

        def rows(i, sums):
            at = pl.ds(pl.multiple_of(i * 64, 64), 64)
            normed = n1_ref[at, :] * gain1_ref[...] + shift1_ref[...]
            n2, inv = norm_stats(normed + (acc[at, :] + b_ref[...]))
            out_ref[at, :] = (n2 * gain2_ref[...] + shift2_ref[...]).astype(bf16)
            grad = cot_ref[at, :].astype(f32) * live
            second = norm_back(grad, n2, inv, gain2_ref[...])
            low = second.astype(bf16)
            bg_ref[at, :] = low
            for copy in leave(i):
                copy.start()
            add = (low.astype(f32), grad * n2, grad)
            return tuple(a + row_sum(b) for a, b in zip(sums, add))

        zero = jnp.zeros((1, width), f32)
        sums = lax.fori_loop(0, length // 64, rows, (zero, zero, zero))
        for i, v in enumerate(sums):
            sums_ref[i : i + 1, :] = v
        for i in range(length // 64):
            for copy in leave(i):
                copy.wait()


def down_project(gathered, place, live, act, n1, cot, b_down, gain1, shift1, gain2, shift2):
    shards, length, units = act.shape
    width = n1.shape[1]
    row = whole((1, width))
    return pl.pallas_call(
        functools.partial(down_body, shards, gathered),
        grid=(shards,),
        out_shape=[
            jax.ShapeDtypeStruct((length, width), bf16),
            jax.ShapeDtypeStruct((length, width), bf16),
            jax.ShapeDtypeStruct((3, width), f32),
        ],
        in_specs=[SMEM, SMEM, pl.BlockSpec((1, length, units), lambda s: (s, 0, 0))]
        + [row] * 5
        + [HBM] * (2 + len(gathered.arrays)),
        out_specs=[HBM] * 2 + [whole((3, width))],
        scratch_shapes=gathered.scratch(shards)
        + [
            pltpu.VMEM((length, width), f32),
            pltpu.VMEM((length, width), f32),
            pltpu.VMEM((length, width), bf16),
            pltpu.SemaphoreType.DMA((2,)),
            pltpu.VMEM((length, width), bf16),
            pltpu.VMEM((length, width), bf16),
            pltpu.SemaphoreType.DMA((2, length // 64)),
        ],
        compiler_params=params(),
        cost_estimate=cost(300),
        name="down_project",
    )(place, live, act, b_down, gain1, shift1, gain2, shift2, n1, cot, *gathered.arrays)


def up_back_body(
    shards, g_down, g_up, place_ref, bg_ref, slope_ref, inv_ref, gain_ref, n1_hbm, *refs
):
    n = len(g_down.arrays)
    d_refs, u_refs = list(refs[:n]), [refs[n]] + list(refs[n + 1 : 2 * n])
    ug_ref, bias_ref, gf_ref, mg_ref, sums_ref = refs[2 * n : 2 * n + 5]
    wd, d_sems, wu, u_sems, acc, n1_ref, late = refs[2 * n + 5 :]
    s = pl.program_id(0)
    place = place_ref[0]
    length, width = acc.shape

    fetch = pltpu.make_async_copy(n1_hbm, n1_ref, late.at[0])

    @pl.when(s == 0)
    def _():
        for shard in range(shards):
            for copy in g_down.copies_of(d_refs, place, wd, d_sems, shard, shard):
                copy.start()
            for copy in g_up.copies_of(u_refs, place, wu, u_sems, shard, shard):
                copy.start()
        fetch.start()

    g_down.wait(d_refs, place, wd, d_sems, s)
    units = ug_ref.shape[2]

    def columns(n, _):
        span = pl.ds(pl.multiple_of(n * 256, 256), 256)
        rows = wd[s, pl.ds(2 * n, 2)].reshape(256, width)
        grad = dot(bg_ref[...], rows, ((1,), (1,)))
        low = (grad * slope_ref[0, :, span].astype(f32)).astype(bf16)
        ug_ref[0, :, span] = low
        bias_ref[0, :, span] = row_sum(low.astype(f32))
        return 0

    lax.fori_loop(0, units // 256, columns, 0)
    g_up.wait(u_refs, place, wu, u_sems, s)
    part = dot(ug_ref[0], wu[s].reshape(width, units), ((1,), (1,)))

    @pl.when(s == 0)
    def _():
        acc[...] = part

    @pl.when(s > 0)
    def _():
        acc[...] += part

    @pl.when(s == shards - 1)
    def _():
        fetch.wait()

        def rows(at, sums):
            n1, grad = n1_ref[at, :], acc[at, :] + bg_ref[at, :].astype(f32)
            first = norm_back(grad, n1, inv_ref[at, 0:1], gain_ref[...])
            gf_ref[at, :] = first
            low = first.astype(bf16)
            mg_ref[at, :] = low
            add = (low.astype(f32), grad * n1, grad)
            return tuple(a + row_sum(b) for a, b in zip(sums, add))

        zero = jnp.zeros((1, width), f32)
        sums = over_rows(length, 64, rows, (zero, zero, zero))
        for i, v in enumerate(sums):
            sums_ref[i : i + 1, :] = v


def up_back(g_down, g_up, place, bg, slope, n1, inv, gain):
    shards, length, units = slope.shape
    width = n1.shape[1]
    block = pl.BlockSpec((1, length, units), lambda s: (s, 0, 0))
    return pl.pallas_call(
        functools.partial(up_back_body, shards, g_down, g_up),
        grid=(shards,),
        out_shape=[
            jax.ShapeDtypeStruct((shards, length, units), bf16),
            jax.ShapeDtypeStruct((shards, 1, units), f32),
            jax.ShapeDtypeStruct((length, width), f32),
            jax.ShapeDtypeStruct((length, width), bf16),
            jax.ShapeDtypeStruct((3, width), f32),
        ],
        in_specs=[SMEM, whole(bg.shape), block, whole(inv.shape), whole((1, width))]
        + [HBM] * (1 + len(g_down.arrays) + len(g_up.arrays)),
        out_specs=[
            block,
            pl.BlockSpec((1, 1, units), lambda s: (s, 0, 0)),
            whole((length, width)),
            whole((length, width)),
            whole((3, width)),
        ],
        scratch_shapes=g_down.scratch(shards)
        + g_up.scratch(shards)
        + [pltpu.VMEM((length, width), f32)] * 2
        + [pltpu.SemaphoreType.DMA((1,))],
        compiler_params=params(),
        cost_estimate=cost(300),
        name="up_back",
    )(place, bg, slope, inv, gain, n1, *g_down.arrays, *g_up.arrays)


def attend_back_body(mg_ref, wo_ref, qkv, p_of, *refs):
    pg_ref, bias_ref, cg = refs[-3:]
    pair = pl.program_id(1)
    cols = cg.shape[1]

    @pl.when(pair == 0)
    def _():
        cg[...] = dot(mg_ref[...], wo_ref[0], ((1,), (1,))).astype(bf16)

    at = pl.multiple_of(pair * 2 * HD, 2 * HD)
    q = qkv[0, :, pl.ds(at, 2 * HD)]
    k = qkv[0, :, pl.ds(cols + at, 2 * HD)]
    v = qkv[0, :, pl.ds(2 * cols + at, 2 * HD)]
    g = cg[:, pl.ds(at, 2 * HD)]
    lane = lax.broadcasted_iota(jnp.int32, q.shape, 1)
    dq = dk = dv = None
    for hh in range(2):
        mine = (lane // HD) == hh
        zero = jnp.zeros_like(q)
        gh = jnp.where(mine, g, zero)
        kh = jnp.where(mine, k, zero)
        qh = jnp.where(mine, q, zero)
        p = p_of[0, hh]
        dpt = dot(v, gh, ((1,), (1,)))
        pf = p.astype(f32)
        row = row_sum(pf * dpt)
        ds = (pf * (dpt - row)).astype(bf16)
        a = dot(p, gh, ((1,), (0,)))
        b = dot(ds, qh, ((1,), (0,)))
        c = dot(ds, kh, ((0,), (0,)))
        dv = a if dv is None else dv + a
        dk = b if dk is None else dk + b
        dq = c if dq is None else dq + c
    for c, g in enumerate((dq * 0.125, dk * 0.125, dv)):
        low = g.astype(bf16)
        pg_ref[0, :, pl.ds(c * cols + at, 2 * HD)] = low
        bias_ref[0, :, pl.ds(c * cols + at, 2 * HD)] = row_sum(low.astype(f32))


def attend_back(covers, base, count, w_out, mg, qkv, p, pg):
    length, width = mg.shape
    shards, cols = w_out.shape[:2]
    pairs = cols // (2 * HD)
    old = [] if pg is None else [pg]
    return pl.pallas_call(
        attend_back_body,
        grid=(count, pairs),
        out_shape=[
            jax.ShapeDtypeStruct((shards, length, 3 * cols), bf16),
            jax.ShapeDtypeStruct((count, 1, 3 * cols), f32),
        ],
        in_specs=[
            whole(mg.shape),
            pl.BlockSpec((1, cols, width), lambda s, i: (s + base, 0, 0)),
            pl.BlockSpec((1, length, 3 * cols), lambda s, i: (s + base, 0, 0)),
            pl.BlockSpec((1, 2, length, length), lambda s, i: (s + base, i, 0, 0)),
        ]
        + [HBM] * len(old),
        out_specs=[
            pl.BlockSpec((1, length, 3 * cols), lambda s, i: (s + base, 0, 0)),
            pl.BlockSpec((1, 1, 3 * cols), lambda s, i: (s, 0, 0)),
        ],
        input_output_aliases={4: 0} if old else {},
        scratch_shapes=[pltpu.VMEM((length, cols), bf16)],
        compiler_params=params(),
        cost_estimate=cost(covers),
        name="attend_back",
    )(mg, w_out, qkv, p, *old)


def input_back_body(shards, gathered, place_ref, pg_ref, gf_hbm, *refs):
    n = len(gathered.arrays)
    w_refs, (gt_ref, tg_ref, w, sems, acc, gf_ref, late) = refs[:n], refs[n:]
    s = pl.program_id(0)
    place = place_ref[0]
    cols = w.shape[-1]
    length, width = acc.shape
    fetch = pltpu.make_async_copy(gf_hbm, gf_ref, late.at[0])

    @pl.when(s == 0)
    def _():
        gathered.start_all(w_refs, place, w, sems, shards)
        fetch.start()
        acc[...] = jnp.zeros_like(acc)

    gathered.wait(w_refs, place, w, sems, s)
    part = None
    for c in range(3):
        new = dot(pg_ref[0, :, c * cols : (c + 1) * cols], w[s, c].reshape(width, cols), ((1,), (1,)))
        part = new if part is None else part + new
    acc[...] += part

    @pl.when(s == shards - 1)
    def _():
        fetch.wait()

        def rows(at, total):
            grad = acc[at, :] + gf_ref[at, :]
            gt_ref[at, :] = grad.astype(bf16)
            return total + row_sum(grad)

        tg_ref[...] = over_rows(length, 64, rows, jnp.zeros((1, width), f32))


def input_back(gathered, place, pg, gf):
    shards, length, cols3 = pg.shape
    width = gf.shape[1]
    return pl.pallas_call(
        functools.partial(input_back_body, shards, gathered),
        grid=(shards,),
        out_shape=[
            jax.ShapeDtypeStruct((length, width), bf16),
            jax.ShapeDtypeStruct((1, width), f32),
        ],
        in_specs=[SMEM, pl.BlockSpec((1, length, cols3), lambda s: (s, 0, 0)), HBM]
        + [HBM] * len(gathered.arrays),
        out_specs=[whole((length, width)), whole((1, width))],
        scratch_shapes=gathered.scratch(shards)
        + [pltpu.VMEM((length, width), f32)] * 2
        + [pltpu.SemaphoreType.DMA((1,))],
        compiler_params=params(),
        cost_estimate=cost(1),
        name="input_back",
    )(place, pg, gf, *gathered.arrays)


def weight_grad_body(n_pairs, looped, place_ref, *refs):
    ins = refs[: 4 * n_pairs]
    keep_ref, send_ref = refs[4 * n_pairs : 4 * n_pairs + 2]
    turned = refs[4 * n_pairs + 2 :]
    place = place_ref[0]
    rows = keep_ref.shape[2]
    first, second = masks(place)

    @pl.when(pl.program_id(0) == 0)
    def _():
        for p in range(n_pairs):
            for core in range(2):
                feature_ref = ins[4 * p + core]
                length = feature_ref.shape[0]
                for j, mask in enumerate((0, second, first, 6)):
                    at = pl.multiple_of((place ^ mask) * rows, rows)
                    block = feature_ref[:, pl.ds(at, rows)]
                    turned[p][j * rows : (j + 1) * rows, core * length : (core + 1) * length] = block.T

    at = 0
    for p in range(n_pairs):
        b_ref, b2_ref = ins[4 * p + 2 : 4 * p + 4]
        length, cols = b_ref.shape[1:]

        def columns(n, _, p=p, b_ref=b_ref, b2_ref=b2_ref, length=length, at=at):
            start = n * 256 if isinstance(n, int) else pl.multiple_of(n * 256, 256)
            g = dot(turned[p][:, :length], b_ref[0, :, pl.ds(start, 256)], ((1,), (0,)))
            g += dot(turned[p][:, length:], b2_ref[0, :, pl.ds(start, 256)], ((1,), (0,)))
            g = g.astype(bf16)
            to = pl.ds(at + start if isinstance(n, int) else pl.multiple_of(at + start, 256), 256)
            for i in range(2):
                keep_ref[i, 0, :, to] = g[i * rows : (i + 1) * rows]
                send_ref[i, 0, :, to] = g[(i + 2) * rows : (i + 3) * rows]
            return 0

        if looped:
            lax.fori_loop(0, cols // 256, columns, 0)
        else:
            for n in range(cols // 256):
                columns(n, 0)
        at += cols


def weight_grad(covers, place, groups, looped=False):
    shards, length, _ = groups[0][2].shape
    rows = groups[0][0].shape[1] // 8
    cols = sum(g[2].shape[2] for g in groups)
    specs, args, scratch = [], [], []
    for feature, feature2, b, b2 in groups:
        block = pl.BlockSpec((1,) + b.shape[1:], lambda s: (s, 0, 0))
        specs += [whole(feature.shape)] * 2 + [block] * 2
        args += [feature, feature2, b, b2]
        scratch.append(pltpu.VMEM((4 * rows, 2 * length), bf16))
    out = jax.ShapeDtypeStruct((2, shards, rows, cols), bf16)
    return pl.pallas_call(
        functools.partial(weight_grad_body, len(groups), looped),
        grid=(shards,),
        out_shape=[out] * 2,
        in_specs=[SMEM] + specs,
        out_specs=[pl.BlockSpec((2, 1, rows, cols), lambda s: (0, s, 0, 0))] * 2,
        scratch_shapes=scratch,
        compiler_params=params(),
        cost_estimate=cost(covers),
        name="weight_grad",
    )(place, *args)


def pass_on_body(keep_ref, came_ref, out_ref):
    def rows(at, _):
        total = keep_ref[0, 0, at, :].astype(f32) + came_ref[0, 0, at, :].astype(f32)
        out_ref[0, at, :] = total.astype(bf16)
        return 0

    over_rows(out_ref.shape[1], 32, rows, 0)


def pass_on(keep, came):
    _, shards, rows, cols = keep.shape
    half = pl.BlockSpec((1, 1, rows, cols), lambda s: (1, s, 0, 0))
    return pl.pallas_call(
        pass_on_body,
        grid=(shards,),
        out_shape=jax.ShapeDtypeStruct((shards, rows, cols), bf16),
        in_specs=[half, half],
        out_specs=pl.BlockSpec((1, rows, cols), lambda s: (s, 0, 0)),
        compiler_params=params(),
        cost_estimate=cost(300),
        name="pass_on",
    )(keep, came)


def gather_up_body(keep_ref, came_ref, last_ref, own_ref, *out_refs):
    s = pl.program_id(0)

    def rows(at, _):
        part = keep_ref[0, 0, at, :].astype(f32) + came_ref[0, 0, at, :].astype(f32)
        part += last_ref[0, at, :].astype(f32)

        @pl.when(s == 0)
        def _():
            own_ref[at, :] = part

        low = part.astype(bf16)
        for i, ref in enumerate(out_refs):

            @pl.when(s == i + 1)
            def _():
                ref[at, :] = low

        return 0

    over_rows(own_ref.shape[0], 32, rows, 0)


def gather_up(covers, keep, came, last):
    _, shards, rows, cols = keep.shape
    half = pl.BlockSpec((1, 1, rows, cols), lambda s: (0, s, 0, 0))
    out = pl.BlockSpec((rows, cols), lambda s: (0, 0))
    return pl.pallas_call(
        gather_up_body,
        grid=(shards,),
        out_shape=[jax.ShapeDtypeStruct((rows, cols), f32)]
        + [jax.ShapeDtypeStruct((rows, cols), bf16)] * (shards - 1),
        in_specs=[half, half, pl.BlockSpec((1, rows, cols), lambda s: (s, 0, 0))],
        out_specs=[out] * shards,
        compiler_params=params(),
        cost_estimate=cost(covers),
        name="gather_up",
    )(keep, came, last)


def finish_body(pieces, scale_ref, *refs):
    n = len(refs) - len(pieces)
    total = refs[0][...]
    for ref in refs[1:n]:
        total += ref[...].astype(f32)
    total *= scale_ref[0]
    for ref, (kind, low, high) in zip(refs[n:], pieces):
        part = total[:, low:high]
        if kind == "turned":
            ref[...] = part.T
        elif kind == "plain":
            ref[...] = part
        else:
            cols = ref.shape[2]
            for c in range(ref.shape[0]):
                ref[c] = part[:, c * cols : (c + 1) * cols]


def finish_all(scale, parts, pieces):
    rows = parts[0].shape[0]
    shapes = []
    for kind, low, high in pieces:
        cols = high - low
        shapes.append({"turned": (cols, rows), "plain": (rows, cols), "three": (3, rows, cols // 3)}[kind])
    return pl.pallas_call(
        functools.partial(finish_body, pieces),
        out_shape=[jax.ShapeDtypeStruct(v, f32) for v in shapes],
        in_specs=[SMEM] + [pl.BlockSpec(memory_space=pltpu.VMEM)] * len(parts),
        compiler_params=params(),
        cost_estimate=cost(300),
        name="finish",
    )(scale, *parts)


def after(x, *deps):
    return lax.optimization_barrier((x, deps))[0]


def on_device(
    tokens,
    timesteps,
    buckets,
    counts,
    w_time,
    table,
    w_qkv,
    b_qv,
    w_out,
    b_out,
    gain1,
    shift1,
    w_up,
    b_up,
    w_down,
    b_down,
    gain2,
    shift2,
    cotangent,
):
    mpn = lax.axis_size("mp")
    dpn = lax.axis_size("dp")
    extra = dpn.bit_length() - 4
    me = lax.axis_index("dp")
    z = lax.axis_index("mp")
    q8 = me >> extra
    width = w_time.shape[0]
    positions, slots = tokens.shape[:2]
    length = positions * mpn
    head_cols = w_qkv.shape[2]
    units = w_up.shape[1]

    def exchange(x, partner):
        low = (1 << extra) - 1
        pairs = [(i, (partner(i >> extra) << extra) | (i & low)) for i in range(dpn)]
        return lax.ppermute(x, "dp", pairs)

    def cores(x):
        return exchange(x, lambda p: p ^ 1)

    def first_link(x):
        return exchange(x, lambda p: p ^ masks(p)[0])

    def second_link(x):
        return exchange(x, lambda p: p ^ masks(p)[1])

    def shift(x, s):
        return lax.ppermute(x, "mp", [(i, (i + s) % mpn) for i in range(mpn)])

    def to_items(x):
        x = lax.all_to_all(jnp.moveaxis(x, 1, 0), "mp", 0, 0, tiled=False)
        return x.reshape(length, width)

    def to_positions(x):
        return lax.all_to_all(x.reshape(mpn, positions, width), "mp", 0, 0, tiled=False)

    def split(shard, axis):
        dims = shard.shape
        return shard.reshape(dims[:axis] + (8, dims[axis] // 8) + dims[axis + 1 :])

    def eighth(shaped, axis):
        return lax.dynamic_index_in_dim(shaped, q8, axis, False)

    def along_z(part):
        return [shift(part, s) for s in range(1, mpn)]

    place = q8.astype(jnp.int32)[None]
    own_qkv, own_out, own_up, own_down = split(w_qkv, 1), split(w_out, 0), split(w_up, 0), split(w_down, 0)
    b_out, gain1, shift1, b_down, gain2, shift2 = [
        v[None] for v in (b_out, gain1, shift1, b_down, gain2, shift2)
    ]

    own_bias = jnp.stack([b_qv[0], jnp.zeros_like(b_qv[0]), b_qv[1]])[:, None]
    z_qkv = along_z(jnp.concatenate([eighth(own_qkv, 1), in_three(own_bias)], axis=1))
    part_up = jnp.concatenate([eighth(own_out, 0), eighth(own_up, 0), in_three(b_up[None])])
    part_down = eighth(own_down, 0)
    mine_qkv, far_bias = pack(300, after(z_qkv, part_up, part_down), own_qkv.shape[2])
    came_qkv = first_link(mine_qkv)
    z_up = along_z(after(part_up, mine_qkv))

    x = to_items(after(tokens, mine_qkv))
    held_qkv = pack(300, [mine_qkv, came_qkv])
    far_qkv = second_link(held_qkv)
    held2_qkv = cores(held_qkv)
    mine_up, far_up_bias = pack(300, after(z_up, held_qkv), own_out.shape[1] + own_up.shape[1])
    came_up = first_link(mine_up)

    timesteps, buckets, counts = after((timesteps, buckets, counts), mine_up)
    total_live = jnp.sum(counts).astype(f32)
    weighting = 1.0 / total_live
    live = (z < lax.dynamic_index_in_dim(counts, me, 0, True)).astype(f32)
    my_step = lax.dynamic_index_in_dim(timesteps, z, 0, True)
    my_bucket = lax.dynamic_index_in_dim(buckets, z, 0, False)
    time_embed = embed(
        300,
        sinusoid(my_step.astype(f32), width), w_time, lax.dynamic_index_in_dim(table, my_bucket, 0, True)
    )

    far2_qkv = cores(after(far_qkv, mine_up))
    g_qkv = Gathered(own_qkv, [held_qkv, far_qkv, held2_qkv, far2_qkv], 1, 0)
    held_up = pack(300, [mine_up, after(came_up, far2_qkv, held2_qkv, time_embed)])
    far_up = second_link(held_up)
    held2_up = cores(held_up)
    x = after(x, held_up)
    hidden = (x.astype(f32) + time_embed).astype(bf16)
    z_down = along_z(after(part_down, hidden))

    done = attend(300, 0, mpn, Gathered(own_qkv, [], 1, 0), place, hidden, own_bias[None], [])
    done = attend(300, 1, mpn, g_qkv, place, after(hidden, held2_up), far_bias, done)
    far2_up = cores(after(far_up, done))
    done = attend(300, 2, mpn, g_qkv, place, hidden, far_bias, done)
    mine_down = pack(300, after(z_down, done, far2_up))
    came_down = first_link(mine_down)
    qkv, probs, ctx = attend(300, 3, mpn, g_qkv, place, after(hidden, mine_down), far_bias, done)
    cot = to_items(after(cotangent, ctx))
    held_down = pack(300, [mine_down, after(came_down, ctx)])
    far_down = second_link(held_down)
    held2_down = cores(held_down)
    ctx2, hidden2 = cores(after(ctx, held_down)), cores(after(hidden, held_down))
    up_pieces = [held_up, far_up, held2_up, far2_up]
    g_out = Gathered(own_out, up_pieces, 0, 0)
    g_up = Gathered(own_up, up_pieces, 0, own_out.shape[1])
    n1, inv1, normed_low, active, slope, full_out = up_project(
        g_out,
        g_up,
        place,
        after(ctx, held_down),
        x,
        time_embed,
        b_out,
        gain1,
        shift1,
        jnp.concatenate([b_up[None, None], far_up_bias]),
    )
    full_out = full_out.reshape(mpn, head_cols, width)
    far2_down = cores(after(far_down, normed_low, held2_down, ctx2, hidden2))
    g_down = Gathered(own_down, [held_down, far_down, held2_down, far2_down], 0, 0)
    cot = after(cot, normed_low)
    active2 = cores(active)
    output, branch_grad, sums2 = down_project(
        g_down, place, live, active, n1, cot, b_down, gain1, shift1, gain2, shift2
    )
    def send_home(covers, keep, came, last):
        sums = gather_up(covers, keep, came, last)
        return [sums[0]] + [shift(v, -s - 1) for s, v in enumerate(sums[1:])], sums

    def finish(arrived, pieces):
        if extra == 0:
            return finish_all(weighting[None], arrived, pieces)
        total = sum(a.astype(f32) for a in arrived) * weighting
        for t in reversed(range(extra)):
            half = total.shape[0] // 2
            bit = (me >> t) & 1
            keep = lax.dynamic_slice_in_dim(total, bit * half, half, 0)
            sent = lax.dynamic_slice_in_dim(total, (1 - bit) * half, half, 0)
            total = keep + lax.ppermute(sent, "dp", [(i, i ^ (1 << t)) for i in range(dpn)])
        made = []
        for kind, low, high in pieces:
            part = total[:, low:high]
            if kind == "turned":
                part = part.T
            elif kind == "three":
                part = jnp.moveaxis(part.reshape(part.shape[0], 3, -1), 1, 0)
            made.append(part)
        return made

    devices = dpn * mpn
    both = ("dp", "mp")

    def in_order(parts):
        turned = jnp.stack([parts[-i % mpn] for i in range(mpn)] * 2)
        return lax.dynamic_slice_in_dim(turned, (mpn - z) % mpn, mpn, 0).reshape(-1)

    keep_d, send_d = weight_grad(300, place, [(branch_grad, cores(branch_grad), active, active2)])
    came_d = first_link(send_d)
    low2 = cores(after(normed_low, keep_d))
    up_grad, bias_up, grad_first, mixing_grad, sums1 = up_back(
        g_down, g_up, place, after(branch_grad, keep_d), slope, n1, inv1, gain1
    )
    up_grad2, mixing_grad2 = cores(up_grad), cores(mixing_grad)
    pass_d = pass_on(keep_d, after(came_d, mixing_grad, low2))
    last_d = second_link(pass_d)
    out_items = to_positions(after(output, mixing_grad))
    keep_u, send_u = weight_grad(
        300,
        place,
        after([(normed_low, low2, up_grad, up_grad2), (mixing_grad, mixing_grad2, ctx, ctx2)], pass_d),
    )
    came_u = first_link(send_u)
    pg, bias_near = attend_back(300, 0, mpn // 2, full_out, after(mixing_grad, keep_u), qkv, probs, None)
    home_d, sent_d = send_home(1, keep_d, came_d, after(last_d, pg))
    pg, bias_far = attend_back(
        1, mpn // 2, mpn - mpn // 2, full_out, after(mixing_grad, sent_d, out_items), qkv, probs, pg
    )
    pg2 = cores(pg)
    pass_u = pass_on(keep_u, after(came_u, pg))
    last_u = second_link(pass_u)
    grad_tokens, time_grad = input_back(g_qkv, place, after(pg, pass_u), grad_first)
    back_items = to_positions(grad_tokens)
    keep_q, send_q = weight_grad(300, place, [(hidden, hidden2, after(pg, grad_tokens), pg2)], looped=True)
    bias_proj = jnp.concatenate([bias_near, bias_far])
    vectors = [
        in_order(bias_proj[:, 0, :head_cols]),
        in_order(bias_proj[:, 0, 2 * head_cols :]),
        sums1[0],
        sums1[1],
        sums1[2],
        sums2[0],
        sums2[1],
        sums2[2],
        in_order(bias_up[:, 0]),
        after(time_grad, keep_q),
    ]
    facts = jnp.stack([my_step[0].astype(f32), my_bucket.astype(f32)])
    facts = jnp.broadcast_to(facts[None], (devices, 2))
    vectors = jnp.concatenate([facts] + [v.reshape(devices, -1) for v in vectors], axis=1)
    came_q = first_link(send_q)
    home_u, sent_u = send_home(300, keep_u, came_u, after(last_u, keep_q, home_d))
    pass_q = pass_on(keep_q, after(came_q, sent_u))
    last_q = second_link(pass_q)
    back_items = after(back_items, pass_q)
    gathered = lax.all_to_all(after(vectors, back_items), both, 0, 0, tiled=True)
    home_u = after(home_u, pass_q)
    (grad_w_down,) = finish(after(home_d, pass_q), [("turned", 0, units)])
    home_q, sent_q = send_home(300, keep_q, came_q, after(last_q, grad_w_down))
    grad_tokens = jnp.moveaxis(after(back_items, sent_q), 0, 1).astype(f32)
    output = jnp.moveaxis(after(out_items, sent_q), 0, 1)
    grad_w_up, grad_w_out = finish(
        after(home_u, sent_q), [("plain", 0, units), ("turned", units, units + head_cols)]
    )
    (grad_w_qkv,) = finish(home_q, [("three", 0, 3 * head_cols)])
    per = width // devices

    gathered = after(gathered, sent_q)
    grads = gathered[:, -per:]
    summed = jnp.sum(gathered[:, 2:-per], axis=0) * weighting
    steps, rows_of = gathered[:, 0], gathered[:, 1]
    small = [summed[i * per : (i + 1) * per] for i in range(8)]
    grad_b_up = summed[8 * per :]
    high = lax.Precision.HIGHEST
    grad_w_time = (
        jnp.einsum("nd,ne->de", sinusoid(steps, width).astype(f32), grads, precision=high)
        * weighting
    )
    onehot = (rows_of[:, None] == jnp.arange(table.shape[0], dtype=f32)[None, :]).astype(f32)
    grad_table = jnp.einsum("nb,nd->bd", onehot, grads, precision=high) * weighting
    return (
        output,
        grad_tokens,
        grad_w_time,
        grad_table,
        grad_w_qkv,
        jnp.stack(small[:2]),
        grad_w_out,
        small[2],
        small[3],
        small[4],
        grad_w_up,
        grad_b_up,
        grad_w_down,
        small[5],
        small[6],
        small[7],
    )


def solution(mesh):
    return jax.shard_map(
        on_device,
        mesh=mesh,
        in_specs=(
            P("mp", "dp", None),
            P("dp"),
            P("dp"),
            P(),
            P(),
            P(),
            P(None, None, "mp"),
            P(None, "mp"),
            P("mp", None),
            P(),
            P(),
            P(),
            P(None, "mp"),
            P("mp"),
            P("mp", None),
            P(),
            P(),
            P(),
            P("mp", "dp", None),
        ),
        out_specs=(
            P("mp", "dp", None),
            P("mp", "dp", None),
            P(None, ("dp", "mp")),
            P(None, ("dp", "mp")),
            P(None, "dp", "mp"),
            P(None, ("dp", "mp")),
            P("mp", "dp"),
            P(("dp", "mp")),
            P(("dp", "mp")),
            P(("dp", "mp")),
            P("dp", "mp"),
            P(("dp", "mp")),
            P("mp", "dp"),
            P(("dp", "mp")),
            P(("dp", "mp")),
            P(("dp", "mp")),
        ),
        check_vma=False,
    )
```

```python
import functools
import math

import jax
import jax.numpy as jnp
from jax import lax
from jax.experimental import pallas as pl
from jax.experimental.pallas import tpu as pltpu
from jax.sharding import PartitionSpec as P

HD = 64
f32 = jnp.float32
bf16 = jnp.bfloat16
VMEM_LIMIT = 56 * 2**20


def params(**more):
    return pltpu.CompilerParams(vmem_limit_bytes=VMEM_LIMIT, **more)


def dot(a, b, dims):
    return lax.dot_general(a, b, (dims, ((), ())), preferred_element_type=f32)


def sinusoid(steps, model_width):
    half_width = model_width // 2
    freqs = jnp.exp(-math.log(10000.0) * jnp.arange(half_width, dtype=f32) / half_width)
    angles = steps[:, None] * freqs[None, :]
    return jnp.concatenate([jnp.sin(angles), jnp.cos(angles)], axis=-1).astype(bf16)


def masks(place):
    first = 2 + 2 * (place & 1)
    return first, 6 - first


class Gathered:
    def __init__(self, own, pieces, lead, start):
        self.arrays = [own] + pieces
        self.lead = lead
        self.start = start
        self.dims = own.shape

    def scratch(self, shards):
        return [pltpu.VMEM((shards,) + self.dims, bf16), pltpu.SemaphoreType.DMA((shards, 8))]

    def copies_of(self, refs, place, into, sems, shard, slot):
        if isinstance(shard, int) and shard == 0:
            return [pltpu.make_async_copy(refs[0], into.at[slot], sems.at[slot, 0])]
        lead = (slice(None),) * self.lead
        first, second = masks(place)
        held = (place, place ^ first)
        far = (place ^ second, place ^ 6)
        held2 = (place ^ 1, place ^ 1 ^ second)
        far2 = (place ^ 1 ^ first, place ^ 7)
        made = []
        for ref, chunks in zip(refs[1:], (held, far, held2, far2)):
            for i, chunk in enumerate(chunks):
                at = lead + (pl.ds(self.start, self.dims[-2]),)
                made.append(
                    pltpu.make_async_copy(
                        ref.at[i, shard - 1].at[at],
                        into.at[(slot,) + lead + (chunk,)],
                        sems.at[slot, len(made)],
                    )
                )
        return made

    def start_all(self, refs, place, into, sems, shards):
        for shard in range(shards):
            for copy in self.copies_of(refs, place, into, sems, shard, shard):
                copy.start()

    def wait(self, refs, place, into, sems, shard):
        @pl.when(shard == 0)
        def _():
            for copy in self.copies_of(refs, place, into, sems, 0, 0):
                copy.wait()

        @pl.when(shard > 0)
        def _():
            for copy in self.copies_of(refs, place, into, sems, shard, shard):
                copy.wait()


HBM = pl.BlockSpec(memory_space=pl.ANY)
SMEM = pl.BlockSpec(memory_space=pltpu.SMEM)


def whole(shape):
    return pl.BlockSpec(shape, lambda *_: (0,) * len(shape))


def cost(micros):
    return pl.CostEstimate(flops=int(micros * 1.15e9), transcendentals=0, bytes_accessed=0)


def over_rows(length, step, body, init):
    def one(i, carry):
        return body(pl.ds(pl.multiple_of(i * step, step), step), carry)

    return lax.fori_loop(0, length // step, one, init)


def row_sum(v):
    return jnp.sum(v, axis=0, keepdims=True)


def pack_body(rows, n, with_sum, *refs):
    parts, out_ref = refs[:n], refs[n]
    sems = refs[-1]
    lead = (slice(None),) * (len(parts[0].shape) - 2)
    copies = []
    for i, ref in enumerate(parts):
        at = lead + (pl.ds(0, rows),)
        copies.append(pltpu.make_async_copy(ref.at[at], out_ref.at[i], sems.at[len(copies)]))
        if with_sum:
            at = lead + (pl.ds(rows, 8),)
            copies.append(pltpu.make_async_copy(ref.at[at], refs[-2].at[i], sems.at[len(copies)]))
    for copy in copies:
        copy.start()
    for copy in copies:
        copy.wait()
    if with_sum:
        extra = refs[-2][...].astype(f32)
        refs[n + 1][...] = sum(extra[..., i : i + 1, :] for i in range(3))


def pack(covers, parts, rows=None):
    dims = parts[0].shape
    n = len(parts)
    lead = (n,) + dims[:-2]
    out = [jax.ShapeDtypeStruct(lead + (rows or dims[-2], dims[-1]), bf16)]
    scratch = []
    if rows:
        out.append(jax.ShapeDtypeStruct(lead + (1, dims[-1]), f32))
        scratch.append(pltpu.VMEM(lead + (8, dims[-1]), bf16))
    made = pl.pallas_call(
        functools.partial(pack_body, rows or dims[-2], n, bool(rows)),
        out_shape=out,
        in_specs=[HBM] * n,
        out_specs=[pl.BlockSpec(memory_space=pltpu.VMEM)] * len(out),
        scratch_shapes=scratch + [pltpu.SemaphoreType.DMA((2 * n,))],
        compiler_params=params(),
        cost_estimate=cost(covers),
        name="pack",
    )(*parts)
    return made if rows else made[0]


def in_three(v):
    parts = []
    for _ in range(3):
        parts.append(lax.reduce_precision(v, 8, 7))
        v = v - parts[-1]
    return jnp.concatenate(parts + [jnp.zeros_like(v)] * 5, axis=-2).astype(bf16)


def embed_body(sinus_ref, w_ref, row_ref, out_ref):
    out_ref[...] = dot(sinus_ref[...], w_ref[...], ((1,), (0,)))[:1] + row_ref[...]


def embed(covers, sinus, w, row):
    return pl.pallas_call(
        embed_body,
        out_shape=jax.ShapeDtypeStruct(row.shape, f32),
        compiler_params=params(),
        cost_estimate=cost(covers),
        name="embed",
    )(jnp.broadcast_to(sinus, (16,) + sinus.shape[1:]), w, row)


def attend_body(shard, gathered, place_ref, x_hbm, bias_ref, *refs):
    n = len(gathered.arrays)
    w_refs = refs[:n]
    qkv_ref, p_ref, c_ref, w, sems, x_ref, x_sem = refs[-7:]
    pair = pl.program_id(0)
    place = place_ref[0]
    cols = w.shape[-1]

    @pl.when(pair == 0)
    def _():
        copies = [pltpu.make_async_copy(x_hbm, x_ref, x_sem.at[0])]
        copies += gathered.copies_of(w_refs, place, w, sems, shard, 0)
        for copy in copies:
            copy.start()
        for copy in copies:
            copy.wait()
        for c in range(3):
            wide = w[0, c].reshape(x_ref.shape[1], cols)
            out = dot(x_ref[...], wide, ((1,), (0,))) + bias_ref[0, c]
            qkv_ref[0, :, c * cols : (c + 1) * cols] = out.astype(bf16)

    at = pl.multiple_of(pair * 2 * HD, 2 * HD)
    q = qkv_ref[0, :, pl.ds(at, 2 * HD)]
    k = qkv_ref[0, :, pl.ds(cols + at, 2 * HD)]
    v = qkv_ref[0, :, pl.ds(2 * cols + at, 2 * HD)]
    lane = lax.broadcasted_iota(jnp.int32, q.shape, 1)
    joined = None
    for hh in range(2):
        mine = (lane // HD) == hh
        kh = jnp.where(mine, k, jnp.zeros_like(k))
        st = dot(kh, q, ((1,), (1,))) * 0.125
        top = jnp.max(st, axis=0, keepdims=True)
        e = jnp.exp(st - top)
        p = (e * (1.0 / jnp.sum(e, axis=0, keepdims=True))).astype(bf16)
        p_ref[0, hh] = p
        c = dot(p, v, ((0,), (0,)))
        joined = c if joined is None else jnp.where(mine, c, joined)
    c_ref[0] = joined.astype(bf16)


def attend(covers, shard, shards, gathered, place, x, bias, old):
    length, width = x.shape
    cols = gathered.dims[-1]
    pairs = cols // (2 * HD)
    n_w = len(gathered.arrays)
    return pl.pallas_call(
        functools.partial(attend_body, shard, gathered),
        grid=(pairs,),
        out_shape=[
            jax.ShapeDtypeStruct((shards, length, 3 * cols), bf16),
            jax.ShapeDtypeStruct((shards, 2 * pairs, length, length), bf16),
            jax.ShapeDtypeStruct((shards, length, cols), bf16),
        ],
        in_specs=[SMEM, HBM, pl.BlockSpec((1, 3, 1, cols), lambda i: (max(shard - 1, 0), 0, 0, 0))]
        + [HBM] * (n_w + len(old)),
        out_specs=[
            pl.BlockSpec((1, length, 3 * cols), lambda i: (shard, 0, 0)),
            pl.BlockSpec((1, 2, length, length), lambda i: (shard, i, 0, 0)),
            pl.BlockSpec((1, length, 2 * HD), lambda i: (shard, 0, i)),
        ],
        input_output_aliases={3 + n_w + i: i for i in range(len(old))},
        scratch_shapes=gathered.scratch(1) + [pltpu.VMEM(x.shape, bf16), pltpu.SemaphoreType.DMA((1,))],
        compiler_params=params(),
        cost_estimate=cost(covers),
        name="attend",
    )(place, x, bias, *gathered.arrays, *old)


def norm_stats(values):
    center = values - jnp.mean(values, axis=-1, keepdims=True)
    inv = lax.rsqrt(jnp.mean(center * center, axis=-1, keepdims=True) + 1e-05)
    return center * inv, inv


def norm_back(grad, n, inv, gain):
    gn = grad * gain
    return (gn - jnp.mean(gn, -1, keepdims=True) - n * jnp.mean(gn * n, -1, keepdims=True)) * inv


def up_body(
    shards, g_out, g_up, place_ref, ctx_ref, x_ref, te_ref, b_ref, gain_ref, shift_ref, bias_ref, *refs
):
    n_out = len(g_out.arrays)
    out_refs = list(refs[:n_out])
    up_refs = [refs[n_out]] + list(refs[1:n_out])
    n1_ref, inv_ref, low_ref, act_ref, slope_ref, wo_full = refs[n_out + 1 : n_out + 7]
    wo, o_sems, wu, u_sems, acc, keep_o = refs[n_out + 7 :]
    s = pl.program_id(0)
    place = place_ref[0]
    length, width = acc.shape

    def keep_out(shard):
        return pltpu.make_async_copy(wo.at[shard], wo_full.at[shard], keep_o.at[shard])

    @pl.when(s == 0)
    def _():
        g_out.start_all(out_refs, place, wo, o_sems, shards)
        g_up.start_all(up_refs, place, wu, u_sems, shards)
        for shard in range(shards):
            g_out.wait(out_refs, place, wo, o_sems, shard)
            keep_out(shard).start()
            part = dot(ctx_ref[shard], wo[shard].reshape(-1, width), ((1,), (0,)))
            if shard == 0:
                acc[...] = part
            else:
                acc[...] += part

        def rows(at, _):
            start = x_ref[at, :].astype(f32) + te_ref[...]
            n1, inv = norm_stats(start + (acc[at, :] + b_ref[...]))
            n1_ref[at, :] = n1
            inv_ref[at, :] = jnp.broadcast_to(inv, (64, inv_ref.shape[1]))
            low_ref[at, :] = (n1 * gain_ref[...] + shift_ref[...]).astype(bf16)
            return 0

        over_rows(length, 64, rows, 0)

    g_up.wait(up_refs, place, wu, u_sems, s)
    units = wu.shape[-1]
    for n in range(units // 256):
        span = slice(n * 256, (n + 1) * 256)
        u = dot(low_ref[...], wu[s, :, :, span].reshape(width, 256), ((1,), (0,)))
        u = u + bias_ref[0, :, span]
        phi = 0.5 + 0.5 * lax.erf(u * (2.0**-0.5))
        act_ref[0, :, span] = (u * phi).astype(bf16)
        slope_ref[0, :, span] = (
            phi + u * jnp.exp(-0.5 * u * u) * (2.0 * math.pi) ** -0.5
        ).astype(bf16)

    @pl.when(s == shards - 1)
    def _():
        for shard in range(shards):
            keep_out(shard).wait()


def up_project(g_out, g_up, place, ctx, x, time_embed, b_out, gain, shift, bias):
    length, width = x.shape
    shards = ctx.shape[0]
    units = g_up.dims[-1]
    block = pl.BlockSpec((1, length, units), lambda s: (s, 0, 0))
    row = whole((1, width))
    return pl.pallas_call(
        functools.partial(up_body, shards, g_out, g_up),
        grid=(shards,),
        out_shape=[
            jax.ShapeDtypeStruct((length, width), f32),
            jax.ShapeDtypeStruct((length, 128), f32),
            jax.ShapeDtypeStruct((length, width), bf16),
            jax.ShapeDtypeStruct((shards, length, units), bf16),
            jax.ShapeDtypeStruct((shards, length, units), bf16),
            jax.ShapeDtypeStruct((shards,) + g_out.dims, bf16),
        ],
        in_specs=[
            SMEM,
            whole(ctx.shape),
            whole(x.shape),
            row,
            row,
            row,
            row,
            pl.BlockSpec((1, 1, units), lambda s: (s, 0, 0)),
        ]
        + [HBM] * (len(g_out.arrays) + 1),
        out_specs=[
            whole((length, width)),
            whole((length, 128)),
            whole((length, width)),
            block,
            block,
            HBM,
        ],
        scratch_shapes=g_out.scratch(shards)
        + g_up.scratch(shards)
        + [pltpu.VMEM((length, width), f32)]
        + [pltpu.SemaphoreType.DMA((shards,))],
        compiler_params=params(),
        cost_estimate=cost(300),
        name="up_project",
    )(place, ctx, x, time_embed, b_out, gain, shift, bias, *g_out.arrays, g_up.arrays[0])


def down_body(
    shards, gathered, place_ref, live_ref, act_ref, b_ref, gain1_ref, shift1_ref, gain2_ref, shift2_ref,
    n1_hbm, cot_hbm, *refs
):
    n = len(gathered.arrays)
    w_refs, (out_hbm, bg_hbm, sums_ref) = refs[:n], refs[n : n + 3]
    w, sems, acc, n1_ref, cot_ref, late, out_ref, bg_ref, done = refs[n + 3 :]
    s = pl.program_id(0)
    place = place_ref[0]
    length, width = acc.shape

    def fetch(i):
        return pltpu.make_async_copy((n1_hbm, cot_hbm)[i], (n1_ref, cot_ref)[i], late.at[i])

    @pl.when(s == 0)
    def _():
        gathered.start_all(w_refs, place, w, sems, shards)
        fetch(0).start()
        fetch(1).start()

    gathered.wait(w_refs, place, w, sems, s)
    part = dot(act_ref[0], w[s].reshape(-1, width), ((1,), (0,)))

    @pl.when(s == 0)
    def _():
        acc[...] = part

    @pl.when(s > 0)
    def _():
        acc[...] += part

    @pl.when(s == shards - 1)
    def _():
        live = live_ref[0]
        fetch(0).wait()
        fetch(1).wait()

        def leave(i):
            at = pl.ds(i * 64, 64)
            return [
                pltpu.make_async_copy(out_ref.at[at], out_hbm.at[at], done.at[0, i]),
                pltpu.make_async_copy(bg_ref.at[at], bg_hbm.at[at], done.at[1, i]),
            ]

        def rows(i, sums):
            at = pl.ds(pl.multiple_of(i * 64, 64), 64)
            normed = n1_ref[at, :] * gain1_ref[...] + shift1_ref[...]
            n2, inv = norm_stats(normed + (acc[at, :] + b_ref[...]))
            out_ref[at, :] = (n2 * gain2_ref[...] + shift2_ref[...]).astype(bf16)
            grad = cot_ref[at, :].astype(f32) * live
            second = norm_back(grad, n2, inv, gain2_ref[...])
            low = second.astype(bf16)
            bg_ref[at, :] = low
            for copy in leave(i):
                copy.start()
            add = (low.astype(f32), grad * n2, grad)
            return tuple(a + row_sum(b) for a, b in zip(sums, add))

        zero = jnp.zeros((1, width), f32)
        sums = lax.fori_loop(0, length // 64, rows, (zero, zero, zero))
        for i, v in enumerate(sums):
            sums_ref[i : i + 1, :] = v
        for i in range(length // 64):
            for copy in leave(i):
                copy.wait()


def down_project(gathered, place, live, act, n1, cot, b_down, gain1, shift1, gain2, shift2):
    shards, length, units = act.shape
    width = n1.shape[1]
    row = whole((1, width))
    return pl.pallas_call(
        functools.partial(down_body, shards, gathered),
        grid=(shards,),
        out_shape=[
            jax.ShapeDtypeStruct((length, width), bf16),
            jax.ShapeDtypeStruct((length, width), bf16),
            jax.ShapeDtypeStruct((3, width), f32),
        ],
        in_specs=[SMEM, SMEM, pl.BlockSpec((1, length, units), lambda s: (s, 0, 0))]
        + [row] * 5
        + [HBM] * (2 + len(gathered.arrays)),
        out_specs=[HBM] * 2 + [whole((3, width))],
        scratch_shapes=gathered.scratch(shards)
        + [
            pltpu.VMEM((length, width), f32),
            pltpu.VMEM((length, width), f32),
            pltpu.VMEM((length, width), bf16),
            pltpu.SemaphoreType.DMA((2,)),
            pltpu.VMEM((length, width), bf16),
            pltpu.VMEM((length, width), bf16),
            pltpu.SemaphoreType.DMA((2, length // 64)),
        ],
        compiler_params=params(),
        cost_estimate=cost(300),
        name="down_project",
    )(place, live, act, b_down, gain1, shift1, gain2, shift2, n1, cot, *gathered.arrays)


def up_back_body(
    shards, g_down, g_up, place_ref, bg_ref, slope_ref, inv_ref, gain_ref, n1_hbm, *refs
):
    n = len(g_down.arrays)
    d_refs, u_refs = list(refs[:n]), [refs[n]] + list(refs[n + 1 : 2 * n])
    ug_ref, bias_ref, gf_ref, mg_ref, sums_ref = refs[2 * n : 2 * n + 5]
    wd, d_sems, wu, u_sems, acc, n1_ref, late = refs[2 * n + 5 :]
    s = pl.program_id(0)
    place = place_ref[0]
    length, width = acc.shape

    fetch = pltpu.make_async_copy(n1_hbm, n1_ref, late.at[0])

    @pl.when(s == 0)
    def _():
        for shard in range(shards):
            for copy in g_down.copies_of(d_refs, place, wd, d_sems, shard, shard):
                copy.start()
            for copy in g_up.copies_of(u_refs, place, wu, u_sems, shard, shard):
                copy.start()
        fetch.start()

    g_down.wait(d_refs, place, wd, d_sems, s)
    units = ug_ref.shape[2]

    def columns(n, _):
        span = pl.ds(pl.multiple_of(n * 256, 256), 256)
        rows = wd[s, pl.ds(2 * n, 2)].reshape(256, width)
        grad = dot(bg_ref[...], rows, ((1,), (1,)))
        low = (grad * slope_ref[0, :, span].astype(f32)).astype(bf16)
        ug_ref[0, :, span] = low
        bias_ref[0, :, span] = row_sum(low.astype(f32))
        return 0

    lax.fori_loop(0, units // 256, columns, 0)
    g_up.wait(u_refs, place, wu, u_sems, s)
    part = dot(ug_ref[0], wu[s].reshape(width, units), ((1,), (1,)))

    @pl.when(s == 0)
    def _():
        acc[...] = part

    @pl.when(s > 0)
    def _():
        acc[...] += part

    @pl.when(s == shards - 1)
    def _():
        fetch.wait()

        def rows(at, sums):
            n1, grad = n1_ref[at, :], acc[at, :] + bg_ref[at, :].astype(f32)
            first = norm_back(grad, n1, inv_ref[at, 0:1], gain_ref[...])
            gf_ref[at, :] = first
            low = first.astype(bf16)
            mg_ref[at, :] = low
            add = (low.astype(f32), grad * n1, grad)
            return tuple(a + row_sum(b) for a, b in zip(sums, add))

        zero = jnp.zeros((1, width), f32)
        sums = over_rows(length, 64, rows, (zero, zero, zero))
        for i, v in enumerate(sums):
            sums_ref[i : i + 1, :] = v


def up_back(g_down, g_up, place, bg, slope, n1, inv, gain):
    shards, length, units = slope.shape
    width = n1.shape[1]
    block = pl.BlockSpec((1, length, units), lambda s: (s, 0, 0))
    return pl.pallas_call(
        functools.partial(up_back_body, shards, g_down, g_up),
        grid=(shards,),
        out_shape=[
            jax.ShapeDtypeStruct((shards, length, units), bf16),
            jax.ShapeDtypeStruct((shards, 1, units), f32),
            jax.ShapeDtypeStruct((length, width), f32),
            jax.ShapeDtypeStruct((length, width), bf16),
            jax.ShapeDtypeStruct((3, width), f32),
        ],
        in_specs=[SMEM, whole(bg.shape), block, whole(inv.shape), whole((1, width))]
        + [HBM] * (1 + len(g_down.arrays) + len(g_up.arrays)),
        out_specs=[
            block,
            pl.BlockSpec((1, 1, units), lambda s: (s, 0, 0)),
            whole((length, width)),
            whole((length, width)),
            whole((3, width)),
        ],
        scratch_shapes=g_down.scratch(shards)
        + g_up.scratch(shards)
        + [pltpu.VMEM((length, width), f32)] * 2
        + [pltpu.SemaphoreType.DMA((1,))],
        compiler_params=params(),
        cost_estimate=cost(300),
        name="up_back",
    )(place, bg, slope, inv, gain, n1, *g_down.arrays, *g_up.arrays)


def attend_back_body(mg_ref, wo_ref, qkv, p_of, *refs):
    pg_ref, bias_ref, cg = refs[-3:]
    pair = pl.program_id(1)
    cols = cg.shape[1]

    @pl.when(pair == 0)
    def _():
        cg[...] = dot(mg_ref[...], wo_ref[0], ((1,), (1,))).astype(bf16)

    at = pl.multiple_of(pair * 2 * HD, 2 * HD)
    q = qkv[0, :, pl.ds(at, 2 * HD)]
    k = qkv[0, :, pl.ds(cols + at, 2 * HD)]
    v = qkv[0, :, pl.ds(2 * cols + at, 2 * HD)]
    g = cg[:, pl.ds(at, 2 * HD)]
    lane = lax.broadcasted_iota(jnp.int32, q.shape, 1)
    dq = dk = dv = None
    for hh in range(2):
        mine = (lane // HD) == hh
        zero = jnp.zeros_like(q)
        gh = jnp.where(mine, g, zero)
        kh = jnp.where(mine, k, zero)
        qh = jnp.where(mine, q, zero)
        p = p_of[0, hh]
        dpt = dot(v, gh, ((1,), (1,)))
        pf = p.astype(f32)
        row = row_sum(pf * dpt)
        ds = (pf * (dpt - row)).astype(bf16)
        a = dot(p, gh, ((1,), (0,)))
        b = dot(ds, qh, ((1,), (0,)))
        c = dot(ds, kh, ((0,), (0,)))
        dv = a if dv is None else dv + a
        dk = b if dk is None else dk + b
        dq = c if dq is None else dq + c
    for c, g in enumerate((dq * 0.125, dk * 0.125, dv)):
        low = g.astype(bf16)
        pg_ref[0, :, pl.ds(c * cols + at, 2 * HD)] = low
        bias_ref[0, :, pl.ds(c * cols + at, 2 * HD)] = row_sum(low.astype(f32))


def attend_back(covers, base, count, w_out, mg, qkv, p, pg):
    length, width = mg.shape
    shards, cols = w_out.shape[:2]
    pairs = cols // (2 * HD)
    old = [] if pg is None else [pg]
    return pl.pallas_call(
        attend_back_body,
        grid=(count, pairs),
        out_shape=[
            jax.ShapeDtypeStruct((shards, length, 3 * cols), bf16),
            jax.ShapeDtypeStruct((count, 1, 3 * cols), f32),
        ],
        in_specs=[
            whole(mg.shape),
            pl.BlockSpec((1, cols, width), lambda s, i: (s + base, 0, 0)),
            pl.BlockSpec((1, length, 3 * cols), lambda s, i: (s + base, 0, 0)),
            pl.BlockSpec((1, 2, length, length), lambda s, i: (s + base, i, 0, 0)),
        ]
        + [HBM] * len(old),
        out_specs=[
            pl.BlockSpec((1, length, 3 * cols), lambda s, i: (s + base, 0, 0)),
            pl.BlockSpec((1, 1, 3 * cols), lambda s, i: (s, 0, 0)),
        ],
        input_output_aliases={4: 0} if old else {},
        scratch_shapes=[pltpu.VMEM((length, cols), bf16)],
        compiler_params=params(),
        cost_estimate=cost(covers),
        name="attend_back",
    )(mg, w_out, qkv, p, *old)


def input_back_body(shards, gathered, place_ref, pg_ref, gf_hbm, *refs):
    n = len(gathered.arrays)
    w_refs, (gt_ref, tg_ref, w, sems, acc, gf_ref, late) = refs[:n], refs[n:]
    s = pl.program_id(0)
    place = place_ref[0]
    cols = w.shape[-1]
    length, width = acc.shape
    fetch = pltpu.make_async_copy(gf_hbm, gf_ref, late.at[0])

    @pl.when(s == 0)
    def _():
        gathered.start_all(w_refs, place, w, sems, shards)
        fetch.start()
        acc[...] = jnp.zeros_like(acc)

    gathered.wait(w_refs, place, w, sems, s)
    part = None
    for c in range(3):
        new = dot(pg_ref[0, :, c * cols : (c + 1) * cols], w[s, c].reshape(width, cols), ((1,), (1,)))
        part = new if part is None else part + new
    acc[...] += part

    @pl.when(s == shards - 1)
    def _():
        fetch.wait()

        def rows(at, total):
            grad = acc[at, :] + gf_ref[at, :]
            gt_ref[at, :] = grad.astype(bf16)
            return total + row_sum(grad)

        tg_ref[...] = over_rows(length, 64, rows, jnp.zeros((1, width), f32))


def input_back(gathered, place, pg, gf):
    shards, length, cols3 = pg.shape
    width = gf.shape[1]
    return pl.pallas_call(
        functools.partial(input_back_body, shards, gathered),
        grid=(shards,),
        out_shape=[
            jax.ShapeDtypeStruct((length, width), bf16),
            jax.ShapeDtypeStruct((1, width), f32),
        ],
        in_specs=[SMEM, pl.BlockSpec((1, length, cols3), lambda s: (s, 0, 0)), HBM]
        + [HBM] * len(gathered.arrays),
        out_specs=[whole((length, width)), whole((1, width))],
        scratch_shapes=gathered.scratch(shards)
        + [pltpu.VMEM((length, width), f32)] * 2
        + [pltpu.SemaphoreType.DMA((1,))],
        compiler_params=params(),
        cost_estimate=cost(1),
        name="input_back",
    )(place, pg, gf, *gathered.arrays)


def weight_grad_body(n_pairs, looped, place_ref, *refs):
    ins = refs[: 4 * n_pairs]
    keep_ref, send_ref = refs[4 * n_pairs : 4 * n_pairs + 2]
    turned = refs[4 * n_pairs + 2 :]
    place = place_ref[0]
    rows = keep_ref.shape[2]
    first, second = masks(place)

    @pl.when(pl.program_id(0) == 0)
    def _():
        for p in range(n_pairs):
            for core in range(2):
                feature_ref = ins[4 * p + core]
                length = feature_ref.shape[0]
                for j, mask in enumerate((0, second, first, 6)):
                    at = pl.multiple_of((place ^ mask) * rows, rows)
                    block = feature_ref[:, pl.ds(at, rows)]
                    turned[p][j * rows : (j + 1) * rows, core * length : (core + 1) * length] = block.T

    at = 0
    for p in range(n_pairs):
        b_ref, b2_ref = ins[4 * p + 2 : 4 * p + 4]
        length, cols = b_ref.shape[1:]

        def columns(n, _, p=p, b_ref=b_ref, b2_ref=b2_ref, length=length, at=at):
            start = n * 256 if isinstance(n, int) else pl.multiple_of(n * 256, 256)
            g = dot(turned[p][:, :length], b_ref[0, :, pl.ds(start, 256)], ((1,), (0,)))
            g += dot(turned[p][:, length:], b2_ref[0, :, pl.ds(start, 256)], ((1,), (0,)))
            g = g.astype(bf16)
            to = pl.ds(at + start if isinstance(n, int) else pl.multiple_of(at + start, 256), 256)
            for i in range(2):
                keep_ref[i, 0, :, to] = g[i * rows : (i + 1) * rows]
                send_ref[i, 0, :, to] = g[(i + 2) * rows : (i + 3) * rows]
            return 0

        if looped:
            lax.fori_loop(0, cols // 256, columns, 0)
        else:
            for n in range(cols // 256):
                columns(n, 0)
        at += cols


def weight_grad(covers, place, groups, looped=False):
    shards, length, _ = groups[0][2].shape
    rows = groups[0][0].shape[1] // 8
    cols = sum(g[2].shape[2] for g in groups)
    specs, args, scratch = [], [], []
    for feature, feature2, b, b2 in groups:
        block = pl.BlockSpec((1,) + b.shape[1:], lambda s: (s, 0, 0))
        specs += [whole(feature.shape)] * 2 + [block] * 2
        args += [feature, feature2, b, b2]
        scratch.append(pltpu.VMEM((4 * rows, 2 * length), bf16))
    out = jax.ShapeDtypeStruct((2, shards, rows, cols), bf16)
    return pl.pallas_call(
        functools.partial(weight_grad_body, len(groups), looped),
        grid=(shards,),
        out_shape=[out] * 2,
        in_specs=[SMEM] + specs,
        out_specs=[pl.BlockSpec((2, 1, rows, cols), lambda s: (0, s, 0, 0))] * 2,
        scratch_shapes=scratch,
        compiler_params=params(),
        cost_estimate=cost(covers),
        name="weight_grad",
    )(place, *args)


def pass_on_body(keep_ref, came_ref, out_ref):
    def rows(at, _):
        total = keep_ref[0, 0, at, :].astype(f32) + came_ref[0, 0, at, :].astype(f32)
        out_ref[0, at, :] = total.astype(bf16)
        return 0

    over_rows(out_ref.shape[1], 32, rows, 0)


def pass_on(keep, came):
    _, shards, rows, cols = keep.shape
    half = pl.BlockSpec((1, 1, rows, cols), lambda s: (1, s, 0, 0))
    return pl.pallas_call(
        pass_on_body,
        grid=(shards,),
        out_shape=jax.ShapeDtypeStruct((shards, rows, cols), bf16),
        in_specs=[half, half],
        out_specs=pl.BlockSpec((1, rows, cols), lambda s: (s, 0, 0)),
        compiler_params=params(),
        cost_estimate=cost(300),
        name="pass_on",
    )(keep, came)


def gather_up_body(keep_ref, came_ref, last_ref, own_ref, *out_refs):
    s = pl.program_id(0)

    def rows(at, _):
        part = keep_ref[0, 0, at, :].astype(f32) + came_ref[0, 0, at, :].astype(f32)
        part += last_ref[0, at, :].astype(f32)

        @pl.when(s == 0)
        def _():
            own_ref[at, :] = part

        low = part.astype(bf16)
        for i, ref in enumerate(out_refs):

            @pl.when(s == i + 1)
            def _():
                ref[at, :] = low

        return 0

    over_rows(own_ref.shape[0], 32, rows, 0)


def gather_up(covers, keep, came, last):
    _, shards, rows, cols = keep.shape
    half = pl.BlockSpec((1, 1, rows, cols), lambda s: (0, s, 0, 0))
    out = pl.BlockSpec((rows, cols), lambda s: (0, 0))
    return pl.pallas_call(
        gather_up_body,
        grid=(shards,),
        out_shape=[jax.ShapeDtypeStruct((rows, cols), f32)]
        + [jax.ShapeDtypeStruct((rows, cols), bf16)] * (shards - 1),
        in_specs=[half, half, pl.BlockSpec((1, rows, cols), lambda s: (s, 0, 0))],
        out_specs=[out] * shards,
        compiler_params=params(),
        cost_estimate=cost(covers),
        name="gather_up",
    )(keep, came, last)


def finish_body(pieces, scale_ref, *refs):
    n = len(refs) - len(pieces)
    total = refs[0][...]
    for ref in refs[1:n]:
        total += ref[...].astype(f32)
    total *= scale_ref[0]
    for ref, (kind, low, high) in zip(refs[n:], pieces):
        part = total[:, low:high]
        if kind == "turned":
            ref[...] = part.T
        elif kind == "plain":
            ref[...] = part
        else:
            cols = ref.shape[2]
            for c in range(ref.shape[0]):
                ref[c] = part[:, c * cols : (c + 1) * cols]


def finish_all(scale, parts, pieces):
    rows = parts[0].shape[0]
    shapes = []
    for kind, low, high in pieces:
        cols = high - low
        shapes.append({"turned": (cols, rows), "plain": (rows, cols), "three": (3, rows, cols // 3)}[kind])
    return pl.pallas_call(
        functools.partial(finish_body, pieces),
        out_shape=[jax.ShapeDtypeStruct(v, f32) for v in shapes],
        in_specs=[SMEM] + [pl.BlockSpec(memory_space=pltpu.VMEM)] * len(parts),
        compiler_params=params(),
        cost_estimate=cost(300),
        name="finish",
    )(scale, *parts)


def after(x, *deps):
    return lax.optimization_barrier((x, deps))[0]


def on_device(
    tokens,
    timesteps,
    buckets,
    counts,
    w_time,
    table,
    w_qkv,
    b_qv,
    w_out,
    b_out,
    gain1,
    shift1,
    w_up,
    b_up,
    w_down,
    b_down,
    gain2,
    shift2,
    cotangent,
):
    mpn = lax.axis_size("mp")
    dpn = lax.axis_size("dp")
    extra = dpn.bit_length() - 4
    me = lax.axis_index("dp")
    z = lax.axis_index("mp")
    q8 = me >> extra
    width = w_time.shape[0]
    positions, slots = tokens.shape[:2]
    length = positions * mpn
    head_cols = w_qkv.shape[2]
    units = w_up.shape[1]

    def exchange(x, partner):
        low = (1 << extra) - 1
        pairs = [(i, (partner(i >> extra) << extra) | (i & low)) for i in range(dpn)]
        return lax.ppermute(x, "dp", pairs)

    def cores(x):
        return exchange(x, lambda p: p ^ 1)

    def first_link(x):
        return exchange(x, lambda p: p ^ masks(p)[0])

    def second_link(x):
        return exchange(x, lambda p: p ^ masks(p)[1])

    def shift(x, s):
        return lax.ppermute(x, "mp", [(i, (i + s) % mpn) for i in range(mpn)])

    def to_items(x):
        x = lax.all_to_all(jnp.moveaxis(x, 1, 0), "mp", 0, 0, tiled=False)
        return x.reshape(length, width)

    def to_positions(x):
        return lax.all_to_all(x.reshape(mpn, positions, width), "mp", 0, 0, tiled=False)

    def split(shard, axis):
        dims = shard.shape
        return shard.reshape(dims[:axis] + (8, dims[axis] // 8) + dims[axis + 1 :])

    def eighth(shaped, axis):
        return lax.dynamic_index_in_dim(shaped, q8, axis, False)

    def along_z(part):
        return [shift(part, s) for s in range(1, mpn)]

    place = q8.astype(jnp.int32)[None]
    own_qkv, own_out, own_up, own_down = split(w_qkv, 1), split(w_out, 0), split(w_up, 0), split(w_down, 0)
    b_out, gain1, shift1, b_down, gain2, shift2 = [
        v[None] for v in (b_out, gain1, shift1, b_down, gain2, shift2)
    ]

    own_bias = jnp.stack([b_qv[0], jnp.zeros_like(b_qv[0]), b_qv[1]])[:, None]
    z_qkv = along_z(jnp.concatenate([eighth(own_qkv, 1), in_three(own_bias)], axis=1))
    part_up = jnp.concatenate([eighth(own_out, 0), eighth(own_up, 0), in_three(b_up[None])])
    part_down = eighth(own_down, 0)
    mine_qkv, far_bias = pack(300, after(z_qkv, part_up, part_down), own_qkv.shape[2])
    came_qkv = first_link(mine_qkv)
    z_up = along_z(after(part_up, mine_qkv))

    x = to_items(after(tokens, mine_qkv))
    held_qkv = pack(300, [mine_qkv, came_qkv])
    far_qkv = second_link(held_qkv)
    held2_qkv = cores(held_qkv)
    mine_up, far_up_bias = pack(300, after(z_up, held_qkv), own_out.shape[1] + own_up.shape[1])
    came_up = first_link(mine_up)

    timesteps, buckets, counts = after((timesteps, buckets, counts), mine_up)
    total_live = jnp.sum(counts).astype(f32)
    weighting = 1.0 / total_live
    live = (z < lax.dynamic_index_in_dim(counts, me, 0, True)).astype(f32)
    my_step = lax.dynamic_index_in_dim(timesteps, z, 0, True)
    my_bucket = lax.dynamic_index_in_dim(buckets, z, 0, False)
    time_embed = embed(
        300,
        sinusoid(my_step.astype(f32), width), w_time, lax.dynamic_index_in_dim(table, my_bucket, 0, True)
    )

    far2_qkv = cores(after(far_qkv, mine_up))
    g_qkv = Gathered(own_qkv, [held_qkv, far_qkv, held2_qkv, far2_qkv], 1, 0)
    held_up = pack(300, [mine_up, after(came_up, far2_qkv, held2_qkv, time_embed)])
    far_up = second_link(held_up)
    held2_up = cores(held_up)
    x = after(x, held_up)
    hidden = (x.astype(f32) + time_embed).astype(bf16)
    z_down = along_z(after(part_down, hidden))

    done = attend(300, 0, mpn, Gathered(own_qkv, [], 1, 0), place, hidden, own_bias[None], [])
    done = attend(300, 1, mpn, g_qkv, place, after(hidden, held2_up), far_bias, done)
    far2_up = cores(after(far_up, done))
    done = attend(300, 2, mpn, g_qkv, place, hidden, far_bias, done)
    mine_down = pack(300, after(z_down, done, far2_up))
    came_down = first_link(mine_down)
    qkv, probs, ctx = attend(300, 3, mpn, g_qkv, place, after(hidden, mine_down), far_bias, done)
    cot = to_items(after(cotangent, ctx))
    held_down = pack(300, [mine_down, after(came_down, ctx)])
    far_down = second_link(held_down)
    held2_down = cores(held_down)
    ctx2, hidden2 = cores(after(ctx, held_down)), cores(after(hidden, held_down))
    up_pieces = [held_up, far_up, held2_up, far2_up]
    g_out = Gathered(own_out, up_pieces, 0, 0)
    g_up = Gathered(own_up, up_pieces, 0, own_out.shape[1])
    n1, inv1, normed_low, active, slope, full_out = up_project(
        g_out,
        g_up,
        place,
        after(ctx, held_down),
        x,
        time_embed,
        b_out,
        gain1,
        shift1,
        jnp.concatenate([b_up[None, None], far_up_bias]),
    )
    full_out = full_out.reshape(mpn, head_cols, width)
    far2_down = cores(after(far_down, normed_low, held2_down, ctx2, hidden2))
    g_down = Gathered(own_down, [held_down, far_down, held2_down, far2_down], 0, 0)
    cot = after(cot, normed_low)
    active2 = cores(active)
    output, branch_grad, sums2 = down_project(
        g_down, place, live, active, n1, cot, b_down, gain1, shift1, gain2, shift2
    )
    def send_home(covers, keep, came, last):
        sums = gather_up(covers, keep, came, last)
        return [sums[0]] + [shift(v, -s - 1) for s, v in enumerate(sums[1:])], sums

    def finish(arrived, pieces):
        if extra == 0:
            return finish_all(weighting[None], arrived, pieces)
        total = sum(a.astype(f32) for a in arrived) * weighting
        for t in reversed(range(extra)):
            half = total.shape[0] // 2
            bit = (me >> t) & 1
            keep = lax.dynamic_slice_in_dim(total, bit * half, half, 0)
            sent = lax.dynamic_slice_in_dim(total, (1 - bit) * half, half, 0)
            total = keep + lax.ppermute(sent, "dp", [(i, i ^ (1 << t)) for i in range(dpn)])
        made = []
        for kind, low, high in pieces:
            part = total[:, low:high]
            if kind == "turned":
                part = part.T
            elif kind == "three":
                part = jnp.moveaxis(part.reshape(part.shape[0], 3, -1), 1, 0)
            made.append(part)
        return made

    devices = dpn * mpn
    both = ("dp", "mp")

    def in_order(parts):
        turned = jnp.stack([parts[-i % mpn] for i in range(mpn)] * 2)
        return lax.dynamic_slice_in_dim(turned, (mpn - z) % mpn, mpn, 0).reshape(-1)

    keep_d, send_d = weight_grad(300, place, [(branch_grad, cores(branch_grad), active, active2)])
    came_d = first_link(send_d)
    low2 = cores(after(normed_low, keep_d))
    up_grad, bias_up, grad_first, mixing_grad, sums1 = up_back(
        g_down, g_up, place, after(branch_grad, keep_d), slope, n1, inv1, gain1
    )
    up_grad2, mixing_grad2 = cores(up_grad), cores(mixing_grad)
    pass_d = pass_on(keep_d, after(came_d, mixing_grad, low2))
    last_d = second_link(pass_d)
    out_items = to_positions(after(output, mixing_grad))
    keep_u, send_u = weight_grad(
        300,
        place,
        after([(normed_low, low2, up_grad, up_grad2), (mixing_grad, mixing_grad2, ctx, ctx2)], pass_d),
    )
    came_u = first_link(send_u)
    pg, bias_near = attend_back(300, 0, mpn // 2, full_out, after(mixing_grad, keep_u), qkv, probs, None)
    home_d, sent_d = send_home(1, keep_d, came_d, after(last_d, pg))
    pg, bias_far = attend_back(
        1, mpn // 2, mpn - mpn // 2, full_out, after(mixing_grad, sent_d, out_items), qkv, probs, pg
    )
    pg2 = cores(pg)
    pass_u = pass_on(keep_u, after(came_u, pg))
    last_u = second_link(pass_u)
    grad_tokens, time_grad = input_back(g_qkv, place, after(pg, pass_u), grad_first)
    back_items = to_positions(grad_tokens)
    keep_q, send_q = weight_grad(300, place, [(hidden, hidden2, after(pg, grad_tokens), pg2)], looped=True)
    bias_proj = jnp.concatenate([bias_near, bias_far])
    vectors = [
        in_order(bias_proj[:, 0, :head_cols]),
        in_order(bias_proj[:, 0, 2 * head_cols :]),
        sums1[0],
        sums1[1],
        sums1[2],
        sums2[0],
        sums2[1],
        sums2[2],
        in_order(bias_up[:, 0]),
        after(time_grad, keep_q),
    ]
    facts = jnp.stack([my_step[0].astype(f32), my_bucket.astype(f32)])
    facts = jnp.broadcast_to(facts[None], (devices, 2))
    vectors = jnp.concatenate([facts] + [v.reshape(devices, -1) for v in vectors], axis=1)
    came_q = first_link(send_q)
    home_u, sent_u = send_home(300, keep_u, came_u, after(last_u, keep_q, home_d))
    pass_q = pass_on(keep_q, after(came_q, sent_u))
    last_q = second_link(pass_q)
    back_items = after(back_items, pass_q)
    gathered = lax.all_to_all(after(vectors, back_items), both, 0, 0, tiled=True)
    home_u = after(home_u, pass_q)
    (grad_w_down,) = finish(after(home_d, pass_q), [("turned", 0, units)])
    home_q, sent_q = send_home(300, keep_q, came_q, after(last_q, grad_w_down))
    grad_tokens = jnp.moveaxis(after(back_items, sent_q), 0, 1).astype(f32)
    output = jnp.moveaxis(after(out_items, sent_q), 0, 1)
    grad_w_up, grad_w_out = finish(
        after(home_u, sent_q), [("plain", 0, units), ("turned", units, units + head_cols)]
    )
    (grad_w_qkv,) = finish(home_q, [("three", 0, 3 * head_cols)])
    per = width // devices

    gathered = after(gathered, sent_q)
    grads = gathered[:, -per:]
    summed = jnp.sum(gathered[:, 2:-per], axis=0) * weighting
    steps, rows_of = gathered[:, 0], gathered[:, 1]
    small = [summed[i * per : (i + 1) * per] for i in range(8)]
    grad_b_up = summed[8 * per :]
    high = lax.Precision.HIGHEST
    grad_w_time = (
        jnp.einsum("nd,ne->de", sinusoid(steps, width).astype(f32), grads, precision=high)
        * weighting
    )
    onehot = (rows_of[:, None] == jnp.arange(table.shape[0], dtype=f32)[None, :]).astype(f32)
    grad_table = jnp.einsum("nb,nd->bd", onehot, grads, precision=high) * weighting
    return (
        output,
        grad_tokens,
        grad_w_time,
        grad_table,
        grad_w_qkv,
        jnp.stack(small[:2]),
        grad_w_out,
        small[2],
        small[3],
        small[4],
        grad_w_up,
        grad_b_up,
        grad_w_down,
        small[5],
        small[6],
        small[7],
    )


def solution(mesh):
    return jax.shard_map(
        on_device,
        mesh=mesh,
        in_specs=(
            P("mp", "dp", None),
            P("dp"),
            P("dp"),
            P(),
            P(),
            P(),
            P(None, None, "mp"),
            P(None, "mp"),
            P("mp", None),
            P(),
            P(),
            P(),
            P(None, "mp"),
            P("mp"),
            P("mp", None),
            P(),
            P(),
            P(),
            P("mp", "dp", None),
        ),
        out_specs=(
            P("mp", "dp", None),
            P("mp", "dp", None),
            P(None, ("dp", "mp")),
            P(None, ("dp", "mp")),
            P(None, "dp", "mp"),
            P(None, ("dp", "mp")),
            P("mp", "dp"),
            P(("dp", "mp")),
            P(("dp", "mp")),
            P(("dp", "mp")),
            P("dp", "mp"),
            P(("dp", "mp")),
            P("mp", "dp"),
            P(("dp", "mp")),
            P(("dp", "mp")),
            P(("dp", "mp")),
        ),
        check_vma=False,
    )
```
